128 devices in a mesh: dp: 16 (over x, y_hi, core), mp: 8 (over y_lo, z).
Axes of the slice: x: 4, y: 4 (y_hi: 2, y_lo: 2; y = y_hi * 2 + y_lo), z: 4, core: 2. Of those that a mesh axis runs over, the one named last changes fastest.
Arguments:
- hidden: bfloat16 [16384, 2048], P(('dp', 'mp')), may hold values from -4 to 4
- norm_gains: float32 [3, 2048], replicated, may hold values from 0.5 to 1.5
- head_gains: float32 [3, 128], replicated, may hold values from 0.25 to 1.75
- query_weight: bfloat16 [2048, 2048], P(('dp', 'mp')), may hold values from -0.125 to 0.125
- kv_weight: bfloat16 [2048, 512], P(('dp', 'mp')), may hold values from -0.125 to 0.125
- out_weight: bfloat16 [2048, 2048], P(('dp', 'mp')), may hold values from -0.5 to 0.5
- gate_up: bfloat16 [128, 2048, 1536], P(('dp', 'mp')), may hold values from -0.125 to 0.125
- down_weight: bfloat16 [128, 768, 2048], P(('dp', 'mp')), may hold values from -0.21875 to 0.21875
- next_weight: bfloat16 [2048, 512], P(('dp', 'mp')), may hold values from -0.125 to 0.125
- expert_ids: int32 [16384, 8], P(('dp', 'mp')), may hold values from 0 to 127, all different within a row; in each aligned block of 128 rows (0 to 127, 128 to 255, ...) at most 10 rows name the same one
- route_weights: float32 [16384, 8], P(('dp', 'mp')), may hold values from 0.05 to 0.5
- token_request: int32 [16384], P('dp'), may hold values from 0 to 31, as said below
- request_leaf: int32 [32], replicated, may hold values from 0 to 15
- leaf_parent: int32 [16], replicated, may hold values from 0 to 7
- mid_parent: int32 [8], replicated, may hold values from 0 to 7
- root_length: int32 [8], replicated, may hold values from 1 to 512, as said below
- mid_length: int32 [8], replicated, may hold values from 1 to 256, as said below
- leaf_length: int32 [16], replicated, may hold values from 1 to 128, as said below
- root_slot: int32 [8], replicated, may hold values from 0 to 7, each once
- mid_slot: int32 [8], replicated, may hold values from 0 to 7, each once
- leaf_slot: int32 [16], replicated, may hold values from 0 to 15, each once
- root_cache: bfloat16 [8, 512, 512], P('mp'), may hold values from -300 to 300
- mid_cache: bfloat16 [8, 256, 512], P('mp'), may hold values from -300 to 300
- leaf_cache: bfloat16 [16, 128, 512], P('mp'), may hold values from -300 to 300
Outputs:
- layer_out: bfloat16 [16384, 2048], P(('dp', 'mp'))
- next_rows: bfloat16 [16384, 512], P(('dp', 'mp'))
The draws below stay inside these ranges and needn't reach their ends.
Inputs may be any that keep to these rules, and one draw needn't show every extreme that they name: `expert_ids`: each row names 8 different experts; among the rows of one device no expert is named more than 10 times, a bound that some block reaches. `token_request`: Nondecreasing; tokens g * 1024 to (g + 1) * 1024 - 1 belong to requests g * 2 to (g + 1) * 2 - 1, and every request has at least one token. `root_length`: some root node has the full length. `mid_length`: some middle node has the full length. `leaf_length`: some leaf node has the full length. `root_slot`: each slot once; slot s is on index s // 1 of mp. `mid_slot`: each slot once; slot s is on index s // 1 of mp. `leaf_slot`: each slot once; slot s is on index s // 2 of mp.
All inputs are finite; a program needn't handle non-finite values.
Results may differ from the reference program's by a relative error of at most 0.024.
Values may be sent and summed in bfloat16 or wider, within the bound.
No kernel may reach another device: no remote copies, remote signals or barrier semaphores. Data moves between devices by JAX's collectives and lax.ppermute only.
A program may use at most 192 MiB of HBM per device.

```python
import math
import jax
import jax.numpy as jnp
import numpy as np
from jax import lax

D = 2048
HEADS = 16
KV_HEADS = 2
HEAD_DIM = 128
FF_E = 768
TOPK = 8
TOK_DEV = 128
REQ_GRP = 2
LEN0 = 512
LEN1 = 256
LEN2 = 128
GROUP_TOK = 1024
TOKENS = 16384
REQUESTS = 32
EXPERTS = 128
CAP = 10
NODES0 = 8
NODES1 = 8
NODES2 = 16
N_DP = 16
N_MP = 8


def draw_token_request(key, part):
    jitter = GROUP_TOK // (4 * REQ_GRP)
    group_total = TOKENS // GROUP_TOK
    base_cuts = (jnp.arange(1, REQ_GRP, dtype=jnp.int32) * (GROUP_TOK // REQ_GRP))[None, :]
    cut_points = base_cuts + jax.random.randint(jax.random.fold_in(key, 3), (group_total, REQ_GRP - 1), -jitter, jitter + 1, dtype=jnp.int32)
    local_place = jnp.arange(GROUP_TOK, dtype=jnp.int32)[None, :, None]
    inside = jnp.sum((local_place >= cut_points[:, None, :]).astype(jnp.int32), axis=2)
    owners = jnp.arange(group_total, dtype=jnp.int32)[:, None] * REQ_GRP
    return (owners + inside).reshape(-1).astype(jnp.int32)


def full_once(key, node_count, level_span):
    drawn = jax.random.randint(key, (node_count,), 1, level_span + 1, dtype=jnp.int32)
    chosen = jax.random.randint(jax.random.fold_in(key, 11), (), 0, node_count, dtype=jnp.int32)
    return jnp.where(jnp.arange(node_count, dtype=jnp.int32) == chosen, level_span, drawn).astype(jnp.int32)


def draw_root_length(key, part):
    return full_once(jax.random.fold_in(key, 21), NODES0, LEN0)


def draw_mid_length(key, part):
    return full_once(jax.random.fold_in(key, 22), NODES1, LEN1)


def draw_leaf_length(key, part):
    return full_once(jax.random.fold_in(key, 23), NODES2, LEN2)


def cache_block(key, node_count, level_span):
    row_width = 2 * KV_HEADS * HEAD_DIM
    values = jax.random.normal(key, (node_count, level_span, row_width), jnp.float32)
    return jnp.clip(values, -300.0, 300.0).astype(jnp.bfloat16)


def draw_root_cache(key, part):
    return cache_block(jax.random.fold_in(key, 31), NODES0, LEN0)


def draw_mid_cache(key, part):
    return cache_block(jax.random.fold_in(key, 32), NODES1, LEN1)


def draw_leaf_cache(key, part):
    return cache_block(jax.random.fold_in(key, 33), NODES2, LEN2)


def plant(values, key, low, largest):
    shape = values.shape
    spot = [jax.random.randint(jax.random.fold_in(key, axis), (), 0, shape[axis]) for axis in range(len(shape))]
    values = values.at[tuple(spot)].set(low)
    longest = shape.index(max(shape))
    spot[longest] = (spot[longest] + 1) % shape[longest]
    return values.at[tuple(spot)].set(largest)


def levels(stream_key, extent, shards, low, largest):
    gain = 1.0
    for dim, parts in shards:
        steps = jax.random.uniform(jax.random.fold_in(jax.random.fold_in(stream_key, 6), dim), (parts,), jnp.float32, low / len(shards), largest / len(shards))
        gain = gain * jnp.repeat(jnp.exp(steps), extent[dim] // parts).reshape((-1,) + (1,) * (len(extent) - 1 - dim))
    return gain


def routed_block(rng, own, number, rows, number_of, top, limit, slope):
    sequence = jax.random.permutation(rng, number_of)
    heavy_load, ordinary = load_shares(number_of, rows * top, limit, slope, True), load_shares(number_of, rows * top, limit, slope, False)
    places = jnp.arange(number_of)

    def named(sizes, rotation):
        used = int((sizes > 0).sum())
        fixed = max(1, used // 4)
        moved = fixed + (places - fixed + rotation * (used - fixed)) % max(1, number_of - fixed)
        return jnp.zeros((number_of,), jnp.int32).at[sequence[jnp.where(places < fixed, places, moved)]].set(jnp.asarray(sizes, jnp.int32))

    sizes = jnp.where(number % 4 == 0, named(heavy_load, number // 4), named(ordinary, number - number // 4 - 1))
    mixed = jax.random.permutation(jax.random.fold_in(own, 3), number_of)
    giver, receiver = mixed[0:number_of // 2 * 2:2], mixed[1:number_of // 2 * 2:2]
    slack = jnp.minimum(sizes[giver] - 1, limit - sizes[receiver]) // 2
    slack = jnp.where((giver == sequence[0]) | (receiver == sequence[0]) | (sizes[receiver] == 0), 0, jnp.maximum(slack, 0))
    moved = jax.random.randint(jax.random.fold_in(own, 4), (number_of // 2,), 0, 1 << 20) % (slack + 1)
    sizes = sizes.at[giver].add(-moved).at[receiver].add(moved)
    members = jnp.searchsorted(jnp.cumsum(sizes), jnp.arange(rows * top), side="right").astype(jnp.int32)
    listing = members.reshape(top, rows).T
    listing = listing[jax.random.permutation(jax.random.fold_in(own, 1), rows)]
    rotation = jax.random.randint(jax.random.fold_in(own, 2), (rows, 1), 0, top)
    return jnp.take_along_axis(listing, (jnp.arange(top)[None, :] + rotation) % top, axis=1)


def load_shares(number_of, total, limit, slope, full):
    loads = [(1 << 20) // math.isqrt(standing ** slope) + 1 for standing in range(1, number_of + 1)]
    largest = limit if full else min(limit, max(-(-total // number_of), total * loads[0] // sum(loads)))
    least = 1 if total - largest >= number_of - 1 else 0
    holding, surplus = [largest] + [least] * (number_of - 1), total - largest - least * (number_of - 1)
    while surplus > 0:
        candidates = [i for i in range(1, number_of) if holding[i] < largest] or [i for i in range(1, number_of) if holding[i] < limit]
        mass, budget = sum([loads[i] for i in candidates]), surplus
        for i in candidates:
            addition = min(limit - holding[i], max(1, budget * loads[i] // mass), surplus)
            holding[i] = holding[i] + addition
            surplus = surplus - addition
    return np.array(holding)


def noise(rng, dims, spread, reach, pieces=(), held_as=jnp.bfloat16):
    values = spread * jax.random.normal(rng, dims, jnp.float32)
    if pieces:
        values = values * levels(rng, dims, pieces, -0.22, 0.18)
    return jnp.clip(values, -reach, reach).astype(held_as)


def setup_inputs(seed: int = 0) -> dict:
    streams_of = jax.random.split(jax.random.key(seed), 25)
    hidden = noise(streams_of[0], (TOKENS, D), 0.5, 4.0, ((0, 128),))
    norm_gains = jnp.clip(1.0 + 0.1 * jax.random.normal(streams_of[1], (3, D), jnp.float32), 0.5, 1.5)
    head_gains = jnp.clip(1.0 + 0.15 * jax.random.normal(streams_of[2], (3, HEAD_DIM), jnp.float32), 0.25, 1.75)
    query_weight = noise(streams_of[3], (D, HEADS * HEAD_DIM), D ** -0.5, 0.125, ((0, 128),))
    kv_weight = noise(streams_of[4], (D, 2 * KV_HEADS * HEAD_DIM), D ** -0.5, 0.125, ((0, 128),))
    out_weight = noise(streams_of[5], (HEADS * HEAD_DIM, D), (HEADS * HEAD_DIM // 16) ** -0.5, 0.5, ((0, 128),))
    gate_up = noise(streams_of[6], (EXPERTS, D, 2 * FF_E), D ** -0.5, 0.125, ((0, 128),))
    down_weight = noise(streams_of[7], (EXPERTS, FF_E, D), FF_E ** -0.5, 0.21875, ((0, 128),))
    next_weight = noise(streams_of[8], (D, 2 * KV_HEADS * HEAD_DIM), D ** -0.5, 0.125, ((0, 128),))
    expert_ids_keys = jax.random.split(jax.random.fold_in(streams_of[9], 1), TOKENS // TOK_DEV)
    expert_ids_turns = jax.random.permutation(jax.random.fold_in(streams_of[9], 3), TOKENS // TOK_DEV)
    expert_ids = jax.vmap(lambda own, number: routed_block(jax.random.fold_in(streams_of[9], 2), own, number, TOK_DEV, EXPERTS, TOPK, CAP, 2))(expert_ids_keys, expert_ids_turns).reshape((TOKENS, TOPK))
    route_weights = jnp.clip(jnp.exp(math.log(0.5) - 2.3025851 * jax.random.uniform(streams_of[10], (TOKENS, TOPK), jnp.float32) ** levels(streams_of[10], (TOKENS, TOPK), ((0, 128),), -0.2, 0.2)), 0.05, 0.5)
    token_request = draw_token_request(jax.random.fold_in(streams_of[24], 71), 0)
    request_leaf = plant(jax.random.randint(streams_of[12], (REQUESTS,), 0, NODES2), jax.random.fold_in(streams_of[12], 1), 0, NODES2 - 1).astype(jnp.int32)
    leaf_parent = plant(jax.random.randint(streams_of[13], (NODES2,), 0, NODES1), jax.random.fold_in(streams_of[13], 1), 0, NODES1 - 1).astype(jnp.int32)
    mid_parent = plant(jax.random.randint(streams_of[14], (NODES1,), 0, NODES0), jax.random.fold_in(streams_of[14], 1), 0, NODES0 - 1).astype(jnp.int32)
    root_length = draw_root_length(jax.random.fold_in(streams_of[24], 71), 0)
    mid_length = draw_mid_length(jax.random.fold_in(streams_of[24], 71), 0)
    leaf_length = draw_leaf_length(jax.random.fold_in(streams_of[24], 71), 0)
    root_slot = jax.random.permutation(streams_of[18], NODES0).astype(jnp.int32)
    mid_slot = jax.random.permutation(streams_of[19], NODES1).astype(jnp.int32)
    leaf_slot = jax.random.permutation(streams_of[20], NODES2).astype(jnp.int32)
    root_cache = draw_root_cache(jax.random.fold_in(streams_of[24], 71), 0)
    mid_cache = draw_mid_cache(jax.random.fold_in(streams_of[24], 71), 0)
    leaf_cache = draw_leaf_cache(jax.random.fold_in(streams_of[24], 71), 0)
    return dict(hidden=hidden, norm_gains=norm_gains, head_gains=head_gains, query_weight=query_weight, kv_weight=kv_weight, out_weight=out_weight, gate_up=gate_up, down_weight=down_weight, next_weight=next_weight, expert_ids=expert_ids, route_weights=route_weights, token_request=token_request, request_leaf=request_leaf, leaf_parent=leaf_parent, mid_parent=mid_parent, root_length=root_length, mid_length=mid_length, leaf_length=leaf_length, root_slot=root_slot, mid_slot=mid_slot, leaf_slot=leaf_slot, root_cache=root_cache, mid_cache=mid_cache, leaf_cache=leaf_cache)


EPS = 1e-06
THETA = 1000000.0
MASKED = -1e+30

def rms_norm(values, weight_row):
    values = values.astype(jnp.float32)
    return values * lax.rsqrt(lax.optimization_barrier(jnp.mean(values * values, axis=-1, keepdims=True)) + EPS) * weight_row

def rotate(values, positions):
    half_dim = values.shape[-1] // 2
    frequency = THETA ** (-2.0 * jnp.arange(half_dim, dtype=jnp.float32) / values.shape[-1])
    angles = positions.astype(jnp.float32)[:, None] * frequency[None, :]
    cosine = jnp.cos(angles)[:, None, :]
    sine_part = jnp.sin(angles)[:, None, :]
    front_part = values[..., :half_dim]
    back_part = values[..., half_dim:]
    return jnp.concatenate([front_part * cosine - back_part * sine_part, back_part * cosine + front_part * sine_part], axis=-1)

def part_sums(scores, allowed):
    row_peak = lax.optimization_barrier(jnp.max(scores, axis=3))
    weights = jnp.where(allowed, jnp.exp(scores - row_peak[..., None]), 0.0)
    rounded = lax.optimization_barrier(weights.astype(jnp.bfloat16)).astype(jnp.float32)
    return (row_peak, lax.optimization_barrier(jnp.sum(weights, axis=3)), rounded)

def join_parts(pre_peak, pre_num, pre_total, self_peak, self_num, self_total):
    row_top = jnp.maximum(pre_peak, self_peak)
    pre_factor = jnp.exp(pre_peak - row_top)
    self_factor = jnp.exp(self_peak - row_top)
    combined = pre_num * pre_factor[..., None] + self_num * self_factor[..., None]
    divisor = pre_total * pre_factor + self_total * self_factor
    return combined / divisor[..., None]

def reference(hidden, norm_gains, head_gains, query_weight, kv_weight, out_weight, gate_up, down_weight, next_weight, expert_ids, route_weights, token_request, request_leaf, leaf_parent, mid_parent, root_length, mid_length, leaf_length, root_slot, mid_slot, leaf_slot, root_cache, mid_cache, leaf_cache):
    kv_width = KV_HEADS * HEAD_DIM
    head_ratio = HEADS // KV_HEADS
    score_scale = HEAD_DIM ** (-0.5)
    normed = rms_norm(hidden, norm_gains[0]).astype(jnp.bfloat16)
    query_raw = jnp.dot(normed, query_weight, preferred_element_type=jnp.float32)
    kv_raw = jnp.dot(normed, kv_weight, preferred_element_type=jnp.float32)
    leaf_node = request_leaf[token_request]
    mid_node = leaf_parent[leaf_node]
    root_node = mid_parent[mid_node]
    path_slots = (root_slot[root_node].astype(jnp.int32), mid_slot[mid_node].astype(jnp.int32), leaf_slot[leaf_node].astype(jnp.int32))
    path_lengths = (root_length[root_node].astype(jnp.int32), mid_length[mid_node].astype(jnp.int32), leaf_length[leaf_node].astype(jnp.int32))
    request_first = jnp.searchsorted(token_request, token_request, side='left').astype(jnp.int32)
    positions = path_lengths[0] + path_lengths[1] + path_lengths[2] + jnp.arange(TOKENS, dtype=jnp.int32) - request_first
    queries = rotate(rms_norm(query_raw.reshape(TOKENS, HEADS, HEAD_DIM), head_gains[0]), positions).astype(jnp.bfloat16)
    new_keys = rotate(rms_norm(kv_raw[:, :kv_width].reshape(TOKENS, KV_HEADS, HEAD_DIM), head_gains[1]), positions).astype(jnp.bfloat16)
    new_rows = jnp.concatenate([new_keys.reshape(TOKENS, kv_width), kv_raw[:, kv_width:].astype(jnp.bfloat16)], axis=1)
    caches = (root_cache, mid_cache, leaf_cache)
    level_spans = (LEN0, LEN1, LEN2)

    def one_block(block_no):
        first_row = block_no * TOK_DEV
        group_first = block_no // N_MP * GROUP_TOK
        block_q = lax.dynamic_slice_in_dim(queries, first_row, TOK_DEV).astype(jnp.float32).reshape(TOK_DEV, KV_HEADS, head_ratio, HEAD_DIM)
        block_ids = lax.dynamic_slice_in_dim(token_request, first_row, TOK_DEV)
        group_ids = lax.dynamic_slice_in_dim(token_request, group_first, GROUP_TOK)
        group_rows = lax.dynamic_slice_in_dim(new_rows, group_first, GROUP_TOK).astype(jnp.float32)
        self_keys = group_rows[:, :kv_width].reshape(GROUP_TOK, KV_HEADS, HEAD_DIM)
        self_values = group_rows[:, kv_width:].reshape(GROUP_TOK, KV_HEADS, HEAD_DIM)
        row_place = first_row + jnp.arange(TOK_DEV, dtype=jnp.int32)
        key_place = group_first + jnp.arange(GROUP_TOK, dtype=jnp.int32)
        self_allowed = ((block_ids[:, None] == group_ids[None, :]) & (key_place[None, :] <= row_place[:, None]))[:, None, None, :]
        level_rows = []
        level_masks = []
        for level_no in range(3):
            slot_pick = lax.dynamic_slice_in_dim(path_slots[level_no], first_row, TOK_DEV)
            length_pick = lax.dynamic_slice_in_dim(path_lengths[level_no], first_row, TOK_DEV)
            level_rows.append(caches[level_no][slot_pick])
            level_masks.append(jnp.arange(level_spans[level_no], dtype=jnp.int32)[None, :] < length_pick[:, None])
        prefix_rows = jnp.concatenate(level_rows, axis=1).astype(jnp.float32)
        prefix_count = prefix_rows.shape[1]
        prefix_keys = prefix_rows[..., :kv_width].reshape(TOK_DEV, prefix_count, KV_HEADS, HEAD_DIM)
        prefix_values = prefix_rows[..., kv_width:].reshape(TOK_DEV, prefix_count, KV_HEADS, HEAD_DIM)
        prefix_allowed = jnp.concatenate(level_masks, axis=1)[:, None, None, :]
        pre_scores = jnp.where(prefix_allowed, jnp.einsum('tkgd,tpkd->tkgp', block_q, prefix_keys) * score_scale, MASKED)
        pre_peak, pre_total, pre_weights = part_sums(pre_scores, prefix_allowed)
        pre_num = jnp.einsum('tkgp,tpkd->tkgd', pre_weights, prefix_values)
        self_scores = jnp.where(self_allowed, jnp.einsum('tkgd,pkd->tkgp', block_q, self_keys) * score_scale, MASKED)
        self_peak, self_total, self_weights = part_sums(self_scores, self_allowed)
        self_num = jnp.einsum('tkgp,pkd->tkgd', self_weights, self_values)
        joined = join_parts(pre_peak, pre_num, pre_total, self_peak, self_num, self_total)
        return joined.reshape(TOK_DEV, HEADS * HEAD_DIM).astype(jnp.bfloat16)
    attended = lax.map(one_block, jnp.arange(TOKENS // TOK_DEV, dtype=jnp.int32)).reshape(TOKENS, HEADS * HEAD_DIM)
    projected = jnp.dot(attended, out_weight, preferred_element_type=jnp.float32)
    after_attention = (hidden.astype(jnp.float32) + projected).astype(jnp.bfloat16)
    moe_in = rms_norm(after_attention, norm_gains[1]).astype(jnp.bfloat16)
    flat_ids = expert_ids.reshape(-1)
    flat_weights = route_weights.reshape(-1)
    row_cap = N_DP * N_MP * CAP

    def one_expert(carry, expert_no):
        matches = flat_ids == expert_no
        picked = jnp.nonzero(matches, size=row_cap, fill_value=0)[0]
        valid = jnp.arange(row_cap, dtype=jnp.int32) < jnp.sum(matches.astype(jnp.int32))
        token_no = picked // TOPK
        chosen_rows = moe_in[token_no]
        gate_up_out = jnp.dot(chosen_rows, gate_up[expert_no], preferred_element_type=jnp.float32)
        active = (jax.nn.silu(gate_up_out[:, :FF_E]) * gate_up_out[:, FF_E:]).astype(jnp.bfloat16)
        result = jnp.dot(active, down_weight[expert_no], preferred_element_type=jnp.float32).astype(jnp.bfloat16)
        result = lax.optimization_barrier(result).astype(jnp.float32)
        factor = jnp.where(valid, flat_weights[picked], 0.0)
        return (carry.at[token_no].add(result * factor[:, None]), None)
    mixture, unused = lax.scan(one_expert, jnp.zeros((TOKENS, D), jnp.float32), jnp.arange(EXPERTS, dtype=jnp.int32))
    layer_out = (after_attention.astype(jnp.float32) + mixture).astype(jnp.bfloat16)
    next_in = rms_norm(layer_out, norm_gains[2]).astype(jnp.bfloat16)
    next_raw = jnp.dot(next_in, next_weight, preferred_element_type=jnp.float32)
    next_keys = rotate(rms_norm(next_raw[:, :kv_width].reshape(TOKENS, KV_HEADS, HEAD_DIM), head_gains[2]), positions).astype(jnp.bfloat16)
    next_rows = jnp.concatenate([next_keys.reshape(TOKENS, kv_width), next_raw[:, kv_width:].astype(jnp.bfloat16)], axis=1)
    return (layer_out, next_rows)
```

```python
import jax
import jax.numpy as jnp
from jax import lax
from jax.experimental import pallas as pl
from jax.experimental.pallas import tpu as pltpu
from jax.sharding import PartitionSpec as P

EPS = 1e-06
THETA = 1000000.0
MASKED = -1e30
LOG2E = 1.4426950408889634
BOTH = ("dp", "mp")
MAIN = 8


def rms_norm(values, weight_row):
    values = values.astype(jnp.float32)
    return values * lax.rsqrt(jnp.mean(values * values, axis=-1, keepdims=True) + EPS) * weight_row


def look_up(lookup_table, indices):
    places = jnp.arange(lookup_table.shape[0], dtype=jnp.int32)
    return jnp.sum(jnp.where(indices[:, None] == places[None, :], lookup_table[None, :], 0), axis=1)


def pack_weights_kernel(query, kv, out_rows, next_rows, packed):
    count = packed.shape[0]
    dim = out_rows.shape[1]
    extra = next_rows.shape[1]
    wide = query.shape[1] // count
    hd = wide // 2
    heads = kv.shape[1] // 2 // hd
    base = dim + extra
    for dest in range(count):
        head = dest * heads // count
        packed[dest, :, 0:dim] = out_rows[...]
        packed[dest, :, dim:base] = next_rows[...]
        packed[dest, :, base : base + wide] = query[:, dest * wide : (dest + 1) * wide]
        for half in range(2):
            source = (half * heads + head) * hd
            target = base + wide + half * hd
            packed[dest, :, target : target + hd] = kv[:, source : source + hd]


def pack_weights(query, kv, out_rows, next_rows, count):
    rows = query.shape[0]
    width = out_rows.shape[1] + next_rows.shape[1] + 2 * (query.shape[1] // count)
    in_vmem = pl.BlockSpec(memory_space=pltpu.VMEM)
    return pl.pallas_call(
        pack_weights_kernel,
        out_shape=jax.ShapeDtypeStruct((count, rows, width), jnp.bfloat16),
        in_specs=[in_vmem] * 4,
        out_specs=in_vmem,
        name="pack_weights",
    )(query, kv, out_rows, next_rows)


def pack_paths_kernel(meta, root, mid, leaf, packed):
    me = meta[0]
    heads = packed.shape[0] // 4
    hd = packed.shape[2] // 2
    part = packed.shape[1]
    for req in range(2):
        own = [meta[8 + 3 * req + level] for level in range(3)]
        levels = []
        for level, cache in enumerate((root, mid, leaf)):
            here = cache.shape[0]
            rows = jnp.zeros(cache.shape[1:], cache.dtype)
            for local in range(here):
                rows = jnp.where(own[level] == me * here + local, cache[local], rows)
            levels.append(rows)
        top = levels[0].shape[0] - part
        middle = levels[1].shape[0]
        for head in range(heads):
            for half in range(2):
                source = slice((half * heads + head) * hd, (half * heads + head + 1) * hd)
                target = slice(half * hd, (half + 1) * hd)
                place = 4 * head + 2 * req
                packed[place, :, target] = levels[0][:part, source]
                packed[place + 1, 0:top, target] = levels[0][part:, source]
                packed[place + 1, top : top + middle, target] = levels[1][:, source]
                packed[place + 1, top + middle :, target] = levels[2][:, source]


def pack_paths(meta, root, mid, leaf, count):
    hd = root.shape[2] // 4
    part = (root.shape[1] + mid.shape[1] + leaf.shape[1]) // 2
    in_vmem = pl.BlockSpec(memory_space=pltpu.VMEM)
    return pl.pallas_call(
        pack_paths_kernel,
        out_shape=jax.ShapeDtypeStruct((count, part, 2 * hd), jnp.bfloat16),
        in_specs=[pl.BlockSpec(memory_space=pltpu.SMEM)] + [in_vmem] * 3,
        out_specs=in_vmem,
        compiler_params=pltpu.CompilerParams(vmem_limit_bytes=24 * 1024 * 1024),
        name="pack_paths",
    )(meta, root, mid, leaf)


def attention_kernel(
    meta,
    rows_all,
    weight,
    piece_0,
    piece_1,
    piece_2,
    piece_3,
    gains,
    cosine,
    sine,
    out,
    q_all,
    k_all,
    v_all,
    pk_all,
    pv_all,
):
    pieces = (piece_0, piece_1, piece_2, piece_3)
    me = meta[0]
    cut = meta[1]
    tok = 128
    count = rows_all.shape[0] // tok
    hd = gains.shape[1]
    span = pk_all.shape[0] // 2
    part = piece_0.shape[0]

    def turn(raw, gain, cos_now, sin_now):
        scaled = raw * lax.rsqrt(jnp.mean(raw * raw, axis=-1, keepdims=True) + EPS) * gain
        return (scaled * cos_now + pltpu.roll(scaled, hd // 2, 1) * sin_now).astype(jnp.bfloat16)

    for step in range(count):
        rows = slice(step * tok, (step + 1) * tok)
        raw = jnp.dot(rows_all[rows, :], weight[...], preferred_element_type=jnp.float32)
        cos_now = cosine[rows, :]
        sin_now = sine[rows, :]
        q_at = 2 * step * tok
        q_all[q_at : q_at + tok, :] = turn(raw[:, :hd], gains[0:1, :], cos_now, sin_now)
        q_all[q_at + tok : q_at + 2 * tok, :] = turn(
            raw[:, hd : 2 * hd], gains[0:1, :], cos_now, sin_now
        )
        k_all[rows, :] = turn(raw[:, 2 * hd : 3 * hd], gains[1:2, :], cos_now, sin_now)
        v_all[rows, :] = raw[:, 3 * hd :].astype(jnp.bfloat16)
    quarter = lax.rem(me, 4)
    for step, piece in enumerate(pieces):
        place = pl.multiple_of((quarter ^ step) * part, part)
        pk_all[pl.ds(place, part), :] = piece[:, :hd]
        pv_all[pl.ds(place, part), :] = piece[:, hd:]

    scale = hd ** (-0.5) * LOG2E
    col = lax.broadcasted_iota(jnp.int32, (1, span), 1)
    row = lax.broadcasted_iota(jnp.int32, (2 * tok, 1), 0)
    row = jnp.where(row >= tok, row - tok, row)

    def join(state, scores, values):
        peak, total, acc = state
        top = jnp.maximum(peak, jnp.max(scores, axis=1, keepdims=True))
        keep = jnp.exp2(peak - top)
        weights = jnp.exp2(scores - top)
        total = total * keep + jnp.sum(weights, axis=1, keepdims=True)
        acc = acc * keep + jnp.dot(
            weights.astype(jnp.bfloat16), values, preferred_element_type=jnp.float32
        )
        return top, total, acc

    for step in range(count):
        first = step * tok
        q_now = q_all[2 * first : 2 * first + 2 * tok, :]
        token = row + first
        late = token >= cut

        def prefix(req, state, q_now=q_now, late=late):
            start = pl.multiple_of(req * span, span)
            scores = scale * lax.dot_general(
                q_now,
                pk_all[pl.ds(start, span), :],
                (((1,), (1,)), ((), ())),
                preferred_element_type=jnp.float32,
            )
            base = 2 + 3 * req
            inside = jnp.where(
                col < 512,
                (col < meta[base]).astype(jnp.int32),
                jnp.where(
                    col < 768,
                    (col - 512 < meta[base + 1]).astype(jnp.int32),
                    (col - 768 < meta[base + 2]).astype(jnp.int32),
                ),
            )
            mine = (late.astype(jnp.int32) == req).astype(jnp.int32)
            scores = jnp.where(inside * mine > 0, scores, MASKED)
            return join(state, scores, pv_all[pl.ds(start, span), :])

        state = (
            jnp.full((2 * tok, 1), MASKED, jnp.float32),
            jnp.zeros((2 * tok, 1), jnp.float32),
            jnp.zeros((2 * tok, hd), jnp.float32),
        )
        low = (first >= cut).astype(jnp.int32)
        high = (first + tok > cut).astype(jnp.int32)
        state = lax.fori_loop(low, high + 1, prefix, state)
        keys = first + tok
        scores = scale * lax.dot_general(
            q_now,
            k_all[0:keys, :],
            (((1,), (1,)), ((), ())),
            preferred_element_type=jnp.float32,
        )
        other = lax.broadcasted_iota(jnp.int32, (1, keys), 1)
        bottom = jnp.where(late, cut, 0)
        scores = jnp.where(
            jnp.logical_and(other <= token, other >= bottom), scores, MASKED
        )
        peak, total, acc = join(state, scores, v_all[0:keys, :])
        done = (acc / total).astype(jnp.bfloat16)
        out[first : first + tok, 0:hd] = done[:tok]
        out[first : first + tok, hd : 2 * hd] = done[tok:]


def attend(meta, rows_all, weight, pieces, gains, cosine, sine):
    group = cosine.shape[0]
    hd = gains.shape[1]
    rows = 4 * pieces[0].shape[0]
    in_vmem = pl.BlockSpec(memory_space=pltpu.VMEM)
    return pl.pallas_call(
        attention_kernel,
        out_shape=jax.ShapeDtypeStruct((group, 2 * hd), jnp.bfloat16),
        in_specs=[pl.BlockSpec(memory_space=pltpu.SMEM)] + [in_vmem] * 9,
        out_specs=in_vmem,
        scratch_shapes=[
            pltpu.VMEM((2 * group, hd), jnp.bfloat16),
            pltpu.VMEM((group, hd), jnp.bfloat16),
            pltpu.VMEM((group, hd), jnp.bfloat16),
            pltpu.VMEM((rows, hd), jnp.bfloat16),
            pltpu.VMEM((rows, hd), jnp.bfloat16),
        ],
        compiler_params=pltpu.CompilerParams(vmem_limit_bytes=40 * 1024 * 1024),
        name="tree_attention",
    )(meta, rows_all, weight, *pieces, gains, cosine, sine)


def exchange(values):
    return lax.all_to_all(values, BOTH, split_axis=0, concat_axis=0, tiled=True)


def expert(rows, gate_up, down_weight):
    ff_width = down_weight.shape[0]
    both = jnp.dot(rows, gate_up, preferred_element_type=jnp.float32)
    active = (jax.nn.silu(both[:, :ff_width]) * both[:, ff_width:]).astype(jnp.bfloat16)
    return jnp.dot(active, down_weight, preferred_element_type=jnp.float32).astype(jnp.bfloat16)


def per_device(
    hidden,
    norm_gains,
    head_gains,
    query_weight,
    kv_weight,
    out_weight,
    gate_up,
    down_weight,
    next_weight,
    expert_ids,
    route_weights,
    token_request,
    request_leaf,
    leaf_parent,
    mid_parent,
    root_length,
    mid_length,
    leaf_length,
    root_slot,
    mid_slot,
    leaf_slot,
    root_cache,
    mid_cache,
    leaf_cache,
):
    tok, dim = hidden.shape
    hd = head_gains.shape[1]
    kv_width = kv_weight.shape[1] // 2
    kv_heads = kv_width // hd
    group = token_request.shape[0]
    mp_size = lax.axis_size("mp")
    dp_size = lax.axis_size("dp")
    devices = dp_size * mp_size
    me = lax.axis_index("mp")
    own_rows = query_weight.shape[0]

    pair = token_request[0] + jnp.arange(2, dtype=jnp.int32)
    cut = jnp.sum((token_request == pair[0]).astype(jnp.int32))
    leaf_node = look_up(request_leaf, pair)
    mid_node = look_up(leaf_parent, leaf_node)
    root_node = look_up(mid_parent, mid_node)
    slots = (
        look_up(root_slot, root_node),
        look_up(mid_slot, mid_node),
        look_up(leaf_slot, leaf_node),
    )
    lengths = (
        look_up(root_length, root_node),
        look_up(mid_length, mid_node),
        look_up(leaf_length, leaf_node),
    )
    prefix_length = lengths[0] + lengths[1] + lengths[2]
    token = jnp.arange(group, dtype=jnp.int32)
    positions = token + jnp.where(token >= cut, prefix_length[1] - cut, prefix_length[0])
    frequency = THETA ** (-2.0 * jnp.arange(hd // 2, dtype=jnp.float32) / hd)
    angles = positions.astype(jnp.float32)[:, None] * frequency[None, :]
    cos_half = jnp.cos(angles)
    sin_half = jnp.sin(angles)
    cosine = jnp.concatenate([cos_half, cos_half], axis=1)
    sine = jnp.concatenate([-sin_half, sin_half], axis=1)

    normed = rms_norm(hidden, norm_gains[0]).astype(jnp.bfloat16)
    rows_all = lax.all_gather(normed, "mp", axis=0, tiled=True)
    packed = pack_weights(query_weight, kv_weight, out_weight, next_weight, mp_size)
    packed = lax.all_to_all(packed, "mp", split_axis=0, concat_axis=0, tiled=True)
    packed = packed.reshape(mp_size * own_rows, -1)
    late_width = dim + next_weight.shape[1]
    late = lax.all_gather(packed[:, :late_width], "dp", axis=0, tiled=True)
    early = packed[:, late_width:]
    early = jnp.broadcast_to(early[None], (dp_size,) + early.shape)
    weight = lax.all_to_all(early, "dp", split_axis=0, concat_axis=0, tiled=True)
    weight = weight.reshape(dim, -1)

    meta = jnp.concatenate(
        [
            jnp.stack([me, cut]),
            jnp.stack(lengths, axis=1).reshape(-1),
            jnp.stack(slots, axis=1).reshape(-1),
        ]
    ).astype(jnp.int32)
    path = pack_paths(meta, root_cache, mid_cache, leaf_cache, mp_size)
    path = lax.all_to_all(path, "mp", split_axis=0, concat_axis=0, tiled=True)
    own_piece = jnp.sum(path.astype(jnp.float32), axis=0).astype(jnp.bfloat16)
    pieces = [own_piece] + [
        lax.ppermute(own_piece, "mp", [(j, j ^ s) for j in range(mp_size)]) for s in range(1, 4)
    ]
    attended = attend(meta, rows_all, weight, pieces, head_gains, cosine, sine)
    attended = lax.all_to_all(
        attended.reshape(mp_size, tok, 2 * hd), "mp", split_axis=0, concat_axis=0, tiled=True
    )
    out_full = late[:, :dim]
    next_full = late[:, dim:]
    projected = jnp.einsum(
        "mtk,mkd->td",
        attended,
        out_full.reshape(mp_size, 2 * hd, dim),
        preferred_element_type=jnp.float32,
    )
    after_attention = (hidden.astype(jnp.float32) + projected).astype(jnp.bfloat16)
    moe_in = rms_norm(after_attention, norm_gains[1]).astype(jnp.bfloat16)

    top_k = expert_ids.shape[1]
    capacity = max(2, 5 * tok * top_k // (4 * devices))
    names = expert_ids[:, :, None] == jnp.arange(devices, dtype=jnp.int32)[None, None, :]
    named = jnp.any(names, axis=1)
    route = jnp.sum(jnp.where(names, route_weights[:, :, None], 0.0), axis=1)
    before = jnp.tril(jnp.ones((tok, tok), jnp.bfloat16), -1)
    slot_no = jnp.dot(before, named.astype(jnp.bfloat16), preferred_element_type=jnp.float32)
    slot_no = jnp.where(named, slot_no.astype(jnp.int32), -1)

    def spread(first, last):
        count = jnp.arange(first, last, dtype=jnp.int32)
        taken = slot_no.T[:, None, :] == count[None, :, None]
        return taken.astype(jnp.bfloat16).reshape(devices * (last - first), tok)

    def gather_back(first, last):
        count = jnp.arange(first, last, dtype=jnp.int32)
        taken = slot_no[:, :, None] == count[None, None, :]
        share = jnp.where(taken, route[:, :, None], 0.0).reshape(tok, devices * (last - first))
        upper = lax.reduce_precision(share, 8, 7)
        return jnp.concatenate([upper, share - upper], axis=0).astype(jnp.bfloat16)

    def outbound(first, last, source):
        picked = jnp.dot(spread(first, last), source, preferred_element_type=jnp.float32)
        return picked.astype(jnp.bfloat16).reshape(devices, last - first, dim)

    def mixed(first, last, returned):
        returned = returned.reshape(-1, dim)
        halves = jnp.dot(gather_back(first, last), returned, preferred_element_type=jnp.float32)
        return halves[:tok] + halves[tok:]

    main_in = exchange(outbound(0, MAIN, moe_in))
    main_in, moe_again = lax.optimization_barrier((main_in, moe_in))
    rest_in = exchange(outbound(MAIN, capacity, moe_again))
    main_out = expert(main_in.reshape(-1, dim), gate_up[0], down_weight[0])
    main_out = exchange(main_out.reshape(devices, MAIN, dim))
    rest_out = expert(rest_in.reshape(-1, dim), gate_up[0], down_weight[0])
    main_out, rest_out = lax.optimization_barrier((main_out, rest_out))
    rest_out = exchange(rest_out.reshape(devices, capacity - MAIN, dim))
    mixture = mixed(0, MAIN, main_out) + mixed(MAIN, capacity, rest_out)
    layer_out = (after_attention.astype(jnp.float32) + mixture).astype(jnp.bfloat16)
    next_in = rms_norm(layer_out, norm_gains[2]).astype(jnp.bfloat16)
    next_raw = jnp.dot(next_in, next_full, preferred_element_type=jnp.float32)
    my_cos = lax.dynamic_slice_in_dim(cosine, me * tok, tok)[:, None, :]
    my_sin = lax.dynamic_slice_in_dim(sine, me * tok, tok)[:, None, :]
    next_keys = rms_norm(next_raw[:, :kv_width].reshape(tok, kv_heads, hd), head_gains[2])
    swapped = jnp.concatenate([next_keys[..., hd // 2 :], next_keys[..., : hd // 2]], axis=-1)
    next_keys = (next_keys * my_cos + swapped * my_sin).astype(jnp.bfloat16)
    next_rows = jnp.concatenate(
        [next_keys.reshape(tok, kv_width), next_raw[:, kv_width:].astype(jnp.bfloat16)], axis=1
    )
    return (layer_out, next_rows)


def solution(mesh):
    both = P(BOTH, None)
    placed = (
        both,
        P(),
        P(),
        both,
        both,
        both,
        P(BOTH, None, None),
        P(BOTH, None, None),
        both,
        both,
        both,
        P("dp"),
        P(),
        P(),
        P(),
        P(),
        P(),
        P(),
        P(),
        P(),
        P(),
        P("mp", None, None),
        P("mp", None, None),
        P("mp", None, None),
    )
    return jax.shard_map(
        per_device,
        mesh=mesh,
        in_specs=placed,
        out_specs=(both, both),
        check_vma=False,
    )
```

```python
import jax
import jax.numpy as jnp
from jax import lax
from jax.experimental import pallas as pl
from jax.experimental.pallas import tpu as pltpu
from jax.sharding import PartitionSpec as P

EPS = 1e-06
THETA = 1000000.0
MASKED = -1e30
LOG2E = 1.4426950408889634
BOTH = ("dp", "mp")
MAIN = 8


def rms_norm(values, weight_row):
    values = values.astype(jnp.float32)
    return values * lax.rsqrt(jnp.mean(values * values, axis=-1, keepdims=True) + EPS) * weight_row


def look_up(lookup_table, indices):
    places = jnp.arange(lookup_table.shape[0], dtype=jnp.int32)
    return jnp.sum(jnp.where(indices[:, None] == places[None, :], lookup_table[None, :], 0), axis=1)


def pack_kernel(meta, query, kv, out_rows, next_rows, root, mid, leaf, packed):
    count, _, wide = packed.shape
    own_rows = query.shape[0]
    hd = wide // 2
    heads = kv.shape[1] // wide
    columns = [out_rows[:, at : at + wide] for at in range(0, out_rows.shape[1], wide)]
    columns += [next_rows[:, at : at + wide] for at in range(0, next_rows.shape[1], wide)]
    shared = len(columns)
    for dest in range(count):
        head = dest * heads // count
        for place, column in enumerate(columns):
            packed[dest, place * own_rows : (place + 1) * own_rows, :] = column
        at = shared * own_rows
        packed[dest, at : at + own_rows, :] = query[:, dest * wide : (dest + 1) * wide]
        at += own_rows
        for half in range(2):
            source = (half * heads + head) * hd
            packed[dest, at : at + own_rows, half * hd : (half + 1) * hd] = kv[
                :, source : source + hd
            ]
    begin = (shared + 2) * own_rows
    part = packed.shape[1] - begin
    me = meta[0]
    for req in range(2):
        levels = []
        for level, cache in enumerate((root, mid, leaf)):
            here = cache.shape[0]
            rows = jnp.zeros(cache.shape[1:], cache.dtype)
            for local in range(here):
                wanted = meta[8 + 3 * req + level] == me * here + local
                rows = jnp.where(wanted, cache[local], rows)
            levels.append(rows)
        top = levels[0].shape[0] - part
        middle = levels[1].shape[0]
        for head in range(heads):
            for half in range(2):
                source = slice((half * heads + head) * hd, (half * heads + head + 1) * hd)
                target = slice(half * hd, (half + 1) * hd)
                place = 4 * head + 2 * req
                packed[place, begin:, target] = levels[0][:part, source]
                packed[place + 1, begin : begin + top, target] = levels[0][part:, source]
                packed[place + 1, begin + top : begin + top + middle, target] = levels[1][:, source]
                packed[place + 1, begin + top + middle :, target] = levels[2][:, source]


def pack(meta, query, kv, out_rows, next_rows, root, mid, leaf, count):
    wide = query.shape[1] // count
    pieces = (out_rows.shape[1] + next_rows.shape[1]) // wide + 2
    part = (root.shape[1] + mid.shape[1] + leaf.shape[1]) // 2
    in_vmem = pl.BlockSpec(memory_space=pltpu.VMEM)
    return pl.pallas_call(
        pack_kernel,
        out_shape=jax.ShapeDtypeStruct(
            (count, pieces * query.shape[0] + part, wide), jnp.bfloat16
        ),
        in_specs=[pl.BlockSpec(memory_space=pltpu.SMEM)] + [in_vmem] * 7,
        out_specs=in_vmem,
        compiler_params=pltpu.CompilerParams(vmem_limit_bytes=24 * 1024 * 1024),
        name="pack",
    )(meta, query, kv, out_rows, next_rows, root, mid, leaf)


def attention_kernel(
    meta,
    own,
    across,
    own_left,
    own_right,
    across_left,
    across_right,
    own_far_top,
    own_far_bottom,
    across_far_top,
    across_far_bottom,
    weight,
    piece_0,
    piece_1,
    piece_2,
    piece_3,
    gains,
    cosine,
    sine,
    out,
    rows_all,
    q_all,
    k_all,
    v_all,
    pk_all,
    pv_all,
):
    pieces = (piece_0, piece_1, piece_2, piece_3)
    me = meta[0]
    cut = meta[1]
    tok, dim = own.shape
    count = rows_all.shape[0] // tok
    hd = gains.shape[1]
    span = pk_all.shape[0] // 2
    part = piece_0.shape[0]
    ring = lax.rem(me, 4)
    base = me - ring
    far_base = 4 - base

    def put(first, step, block, offset=0):
        at = (first + lax.rem(ring + step, 4)) * tok + offset
        at = pl.multiple_of(at, block.shape[0])
        rows_all[pl.ds(at, block.shape[0]), :] = block[...]

    put(base, 0, own)
    put(far_base, 0, across)
    put(base, 3, own_left)
    put(base, 1, own_right)
    put(far_base, 3, across_left)
    put(far_base, 1, across_right)
    put(base, 2, own_far_top)
    put(base, 2, own_far_bottom, tok // 2)
    put(far_base, 2, across_far_top)
    put(far_base, 2, across_far_bottom, tok // 2)
    for step, piece in enumerate(pieces):
        place = pl.multiple_of((ring ^ step) * part, part)
        pk_all[pl.ds(place, part), :] = piece[:, :hd]
        pv_all[pl.ds(place, part), :] = piece[:, hd:]
    weight_q = weight[:, 0].reshape(dim, 2 * hd)
    weight_kv = weight[:, 1].reshape(dim, 2 * hd)

    def turn(raw, gain, cos_now, sin_now):
        scaled = raw * lax.rsqrt(jnp.mean(raw * raw, axis=-1, keepdims=True) + EPS) * gain
        return (scaled * cos_now + pltpu.roll(scaled, hd // 2, 1) * sin_now).astype(jnp.bfloat16)

    @pl.loop(0, count)
    def _(step):
        at = pl.multiple_of(step * tok, tok)
        rows = rows_all[pl.ds(at, tok), :]
        cos_now = cosine[pl.ds(at, tok), :]
        sin_now = sine[pl.ds(at, tok), :]
        raw = jnp.dot(rows, weight_q, preferred_element_type=jnp.float32)
        q_at = pl.multiple_of(2 * step * tok, 2 * tok)
        q_all[pl.ds(q_at, tok), :] = turn(raw[:, :hd], gains[0:1, :], cos_now, sin_now)
        q_all[pl.ds(q_at + tok, tok), :] = turn(raw[:, hd:], gains[0:1, :], cos_now, sin_now)
        raw = jnp.dot(rows, weight_kv, preferred_element_type=jnp.float32)
        k_all[pl.ds(at, tok), :] = turn(raw[:, :hd], gains[1:2, :], cos_now, sin_now)
        v_all[pl.ds(at, tok), :] = raw[:, hd:].astype(jnp.bfloat16)

    scale = hd ** (-0.5) * LOG2E
    col = lax.broadcasted_iota(jnp.int32, (1, span), 1)
    row = lax.broadcasted_iota(jnp.int32, (2 * tok, 1), 0)
    row = jnp.where(row >= tok, row - tok, row)
    chunk = 2 * tok
    key_col = lax.broadcasted_iota(jnp.int32, (1, chunk), 1)

    def join(state, q_now, keys, values, allowed):
        peak, total, acc = state
        scores = scale * lax.dot_general(
            q_now, keys, (((1,), (1,)), ((), ())), preferred_element_type=jnp.float32
        )
        scores = jnp.where(allowed, scores, MASKED)
        top = jnp.maximum(peak, jnp.max(scores, axis=1, keepdims=True))
        keep = jnp.exp2(peak - top)
        weights = jnp.exp2(scores - top)
        total = total * keep + jnp.sum(weights, axis=1, keepdims=True)
        acc = acc * keep + jnp.dot(
            weights.astype(jnp.bfloat16), values, preferred_element_type=jnp.float32
        )
        return top, total, acc

    @pl.loop(0, count)
    def _(step):
        first = pl.multiple_of(step * tok, tok)
        q_now = q_all[pl.ds(pl.multiple_of(2 * step * tok, 2 * tok), 2 * tok), :]
        token = row + first
        late = token >= cut

        def prefix(req, state):
            start = pl.multiple_of(req * span, span)
            at = 2 + 3 * req
            inside = jnp.where(
                col < 512,
                (col < meta[at]).astype(jnp.int32),
                jnp.where(
                    col < 768,
                    (col - 512 < meta[at + 1]).astype(jnp.int32),
                    (col - 768 < meta[at + 2]).astype(jnp.int32),
                ),
            )
            mine = (late.astype(jnp.int32) == req).astype(jnp.int32)
            return join(
                state,
                q_now,
                pk_all[pl.ds(start, span), :],
                pv_all[pl.ds(start, span), :],
                inside * mine > 0,
            )

        state = (
            jnp.full((2 * tok, 1), MASKED, jnp.float32),
            jnp.zeros((2 * tok, 1), jnp.float32),
            jnp.zeros((2 * tok, hd), jnp.float32),
        )
        low = (first >= cut).astype(jnp.int32)
        high = (first + tok > cut).astype(jnp.int32)
        state = lax.fori_loop(low, high + 1, prefix, state)
        bottom = jnp.where(late, cut, 0)

        def new(number, state):
            start = pl.multiple_of(number * chunk, chunk)
            other = key_col + start
            return join(
                state,
                q_now,
                k_all[pl.ds(start, chunk), :],
                v_all[pl.ds(start, chunk), :],
                jnp.logical_and(other <= token, other >= bottom),
            )

        peak, total, acc = lax.fori_loop(0, step // 2 + 1, new, state)
        done = (acc / total).astype(jnp.bfloat16)
        out[pl.ds(first, tok), 0:hd] = done[:tok]
        out[pl.ds(first, tok), hd : 2 * hd] = done[tok:]


def attend(meta, rows, weight, pieces, gains, cosine, sine):
    group = cosine.shape[0]
    hd = gains.shape[1]
    path_rows = 4 * pieces[0].shape[0]
    in_vmem = pl.BlockSpec(memory_space=pltpu.VMEM)
    return pl.pallas_call(
        attention_kernel,
        out_shape=jax.ShapeDtypeStruct((group, 2 * hd), jnp.bfloat16),
        in_specs=[pl.BlockSpec(memory_space=pltpu.SMEM)] + [in_vmem] * 18,
        out_specs=in_vmem,
        scratch_shapes=[
            pltpu.VMEM((group, rows[0].shape[1]), jnp.bfloat16),
            pltpu.VMEM((2 * group, hd), jnp.bfloat16),
            pltpu.VMEM((group, hd), jnp.bfloat16),
            pltpu.VMEM((group, hd), jnp.bfloat16),
            pltpu.VMEM((path_rows, hd), jnp.bfloat16),
            pltpu.VMEM((path_rows, hd), jnp.bfloat16),
        ],
        compiler_params=pltpu.CompilerParams(vmem_limit_bytes=40 * 1024 * 1024),
        name="tree_attention",
    )(meta, *rows, weight, *pieces, gains, cosine, sine)


def exchange(values):
    return lax.all_to_all(values, BOTH, split_axis=0, concat_axis=0, tiled=True)


def expert(rows, gate_up, down_weight):
    ff_width = down_weight.shape[0]
    both = jnp.dot(rows, gate_up, preferred_element_type=jnp.float32)
    active = (jax.nn.silu(both[:, :ff_width]) * both[:, ff_width:]).astype(jnp.bfloat16)
    return jnp.dot(active, down_weight, preferred_element_type=jnp.float32).astype(jnp.bfloat16)


def per_device(
    hidden,
    norm_gains,
    head_gains,
    query_weight,
    kv_weight,
    out_weight,
    gate_up,
    down_weight,
    next_weight,
    expert_ids,
    route_weights,
    token_request,
    request_leaf,
    leaf_parent,
    mid_parent,
    root_length,
    mid_length,
    leaf_length,
    root_slot,
    mid_slot,
    leaf_slot,
    root_cache,
    mid_cache,
    leaf_cache,
):
    tok, dim = hidden.shape
    hd = head_gains.shape[1]
    kv_width = kv_weight.shape[1] // 2
    kv_heads = kv_width // hd
    group = token_request.shape[0]
    mp_size = lax.axis_size("mp")
    dp_size = lax.axis_size("dp")
    devices = dp_size * mp_size
    me = lax.axis_index("mp")
    own_rows = query_weight.shape[0]

    pair = token_request[0] + jnp.arange(2, dtype=jnp.int32)
    cut = jnp.sum((token_request == pair[0]).astype(jnp.int32))
    leaf_node = look_up(request_leaf, pair)
    mid_node = look_up(leaf_parent, leaf_node)
    root_node = look_up(mid_parent, mid_node)
    slots = (
        look_up(root_slot, root_node),
        look_up(mid_slot, mid_node),
        look_up(leaf_slot, leaf_node),
    )
    lengths = (
        look_up(root_length, root_node),
        look_up(mid_length, mid_node),
        look_up(leaf_length, leaf_node),
    )
    prefix_length = lengths[0] + lengths[1] + lengths[2]
    token = jnp.arange(group, dtype=jnp.int32)
    positions = token + jnp.where(token >= cut, prefix_length[1] - cut, prefix_length[0])
    frequency = THETA ** (-2.0 * jnp.arange(hd // 2, dtype=jnp.float32) / hd)
    angles = positions.astype(jnp.float32)[:, None] * frequency[None, :]
    cos_half = jnp.cos(angles)
    sin_half = jnp.sin(angles)
    cosine = jnp.concatenate([cos_half, cos_half], axis=1)
    sine = jnp.concatenate([-sin_half, sin_half], axis=1)

    normed = rms_norm(hidden, norm_gains[0]).astype(jnp.bfloat16)
    def shift(values, step):
        moves = [(j, j - j % 4 + (j % 4 + step) % 4) for j in range(mp_size)]
        return lax.ppermute(values, "mp", moves)

    across = lax.ppermute(normed, "mp", [(j, (j + 4) % mp_size) for j in range(mp_size)])
    sides = []
    far = []
    for block in (normed, across):
        left = shift(block, 1)
        right = shift(block, -1)
        sides += [left, right]
        far += [shift(left[: tok // 2], 1), shift(right[tok // 2 :], -1)]
    rows = [normed, across] + sides + far

    meta = jnp.concatenate(
        [
            jnp.stack([me, cut]),
            jnp.stack(lengths, axis=1).reshape(-1),
            jnp.stack(slots, axis=1).reshape(-1),
        ]
    ).astype(jnp.int32)
    packed = pack(
        meta,
        query_weight,
        kv_weight,
        out_weight,
        next_weight,
        root_cache,
        mid_cache,
        leaf_cache,
        mp_size,
    )
    packed = lax.all_to_all(packed, "mp", split_axis=0, concat_axis=0, tiled=True)
    wide = packed.shape[2]
    out_end = dim // wide * own_rows
    next_end = out_end + next_weight.shape[1] // wide * own_rows
    early_end = next_end + 2 * own_rows

    def whole_rows(values):
        values = values.reshape(mp_size, -1, own_rows, wide).transpose(0, 2, 1, 3)
        return lax.all_gather(
            values.reshape(mp_size * own_rows, -1), "dp", axis=0, tiled=True
        )

    out_full = whole_rows(packed[:, :out_end])
    next_full = whole_rows(packed[:, out_end:next_end])
    early = packed[:, next_end:early_end].reshape(1, mp_size, 2, own_rows, wide)
    early = jnp.broadcast_to(early, (dp_size, mp_size, 2, own_rows, wide))
    weight = lax.all_to_all(early, "dp", split_axis=0, concat_axis=0, tiled=True)
    weight = weight.reshape(devices, 2, own_rows, wide)
    own_piece = jnp.sum(packed[:, early_end:].astype(jnp.float32), axis=0).astype(jnp.bfloat16)
    pieces = [own_piece] + [
        lax.ppermute(own_piece, "mp", [(j, j ^ s) for j in range(mp_size)]) for s in range(1, 4)
    ]
    attended = attend(meta, rows, weight, pieces, head_gains, cosine, sine)
    attended = lax.all_to_all(
        attended.reshape(mp_size, tok, 2 * hd), "mp", split_axis=0, concat_axis=0, tiled=True
    )
    projected = jnp.einsum(
        "mtk,mkd->td",
        attended,
        out_full.reshape(mp_size, 2 * hd, dim),
        preferred_element_type=jnp.float32,
    )
    after_attention = (hidden.astype(jnp.float32) + projected).astype(jnp.bfloat16)
    moe_in = rms_norm(after_attention, norm_gains[1]).astype(jnp.bfloat16)

    top_k = expert_ids.shape[1]
    capacity = max(2, 5 * tok * top_k // (4 * devices))
    names = expert_ids[:, :, None] == jnp.arange(devices, dtype=jnp.int32)[None, None, :]
    named = jnp.any(names, axis=1)
    route = jnp.sum(jnp.where(names, route_weights[:, :, None], 0.0), axis=1)
    before = jnp.tril(jnp.ones((tok, tok), jnp.bfloat16), -1)
    slot_no = jnp.dot(before, named.astype(jnp.bfloat16), preferred_element_type=jnp.float32)
    slot_no = jnp.where(named, slot_no.astype(jnp.int32), -1)

    def spread(first, last):
        count = jnp.arange(first, last, dtype=jnp.int32)
        taken = slot_no.T[:, None, :] == count[None, :, None]
        return taken.astype(jnp.bfloat16).reshape(devices * (last - first), tok)

    def gather_back(first, last):
        count = jnp.arange(first, last, dtype=jnp.int32)
        taken = slot_no[:, :, None] == count[None, None, :]
        share = jnp.where(taken, route[:, :, None], 0.0).reshape(tok, devices * (last - first))
        upper = lax.reduce_precision(share, 8, 7)
        return jnp.concatenate([upper, share - upper], axis=0).astype(jnp.bfloat16)

    def outbound(first, last, source):
        picked = jnp.dot(spread(first, last), source, preferred_element_type=jnp.float32)
        return picked.astype(jnp.bfloat16).reshape(devices, last - first, dim)

    def mixed(first, last, returned):
        returned = returned.reshape(-1, dim)
        halves = jnp.dot(gather_back(first, last), returned, preferred_element_type=jnp.float32)
        return halves[:tok] + halves[tok:]

    main_in = exchange(outbound(0, MAIN, moe_in))
    main_in, rest_in = lax.optimization_barrier((main_in, outbound(MAIN, capacity, moe_in)))
    rest_in = exchange(rest_in)
    main_out = expert(main_in.reshape(-1, dim), gate_up[0], down_weight[0])
    main_out = exchange(main_out.reshape(devices, MAIN, dim))
    rest_out = expert(rest_in.reshape(-1, dim), gate_up[0], down_weight[0])
    rest_out = rest_out.reshape(devices, capacity - MAIN, dim)
    main_out, rest_out = lax.optimization_barrier((main_out, rest_out))
    rest_out = exchange(rest_out)
    mixture = mixed(0, MAIN, main_out) + mixed(MAIN, capacity, rest_out)
    layer_out = (after_attention.astype(jnp.float32) + mixture).astype(jnp.bfloat16)
    next_in = rms_norm(layer_out, norm_gains[2]).astype(jnp.bfloat16)
    next_raw = jnp.dot(next_in, next_full, preferred_element_type=jnp.float32)
    my_cos = lax.dynamic_slice_in_dim(cosine, me * tok, tok)[:, None, :]
    my_sin = lax.dynamic_slice_in_dim(sine, me * tok, tok)[:, None, :]
    next_keys = rms_norm(next_raw[:, :kv_width].reshape(tok, kv_heads, hd), head_gains[2])
    swapped = jnp.concatenate([next_keys[..., hd // 2 :], next_keys[..., : hd // 2]], axis=-1)
    next_keys = (next_keys * my_cos + swapped * my_sin).astype(jnp.bfloat16)
    next_rows = jnp.concatenate(
        [next_keys.reshape(tok, kv_width), next_raw[:, kv_width:].astype(jnp.bfloat16)], axis=1
    )
    return (layer_out, next_rows)


def solution(mesh):
    both = P(BOTH, None)
    placed = (
        both,
        P(),
        P(),
        both,
        both,
        both,
        P(BOTH, None, None),
        P(BOTH, None, None),
        both,
        both,
        both,
        P("dp"),
        P(),
        P(),
        P(),
        P(),
        P(),
        P(),
        P(),
        P(),
        P(),
        P("mp", None, None),
        P("mp", None, None),
        P("mp", None, None),
    )
    return jax.shard_map(
        per_device,
        mesh=mesh,
        in_specs=placed,
        out_specs=(both, both),
        check_vma=False,
    )
```

```python
import jax
import jax.numpy as jnp
from jax import lax
from jax.experimental import pallas as pl
from jax.experimental.pallas import tpu as pltpu
from jax.sharding import PartitionSpec as P

EPS = 1e-06
THETA = 1000000.0
MASKED = -1e30
LOG2E = 1.4426950408889634
BOTH = ("dp", "mp")
MAIN = 8


def rms_norm(values, weight_row):
    values = values.astype(jnp.float32)
    return values * lax.rsqrt(jnp.mean(values * values, axis=-1, keepdims=True) + EPS) * weight_row


def look_up(lookup_table, indices):
    places = jnp.arange(lookup_table.shape[0], dtype=jnp.int32)
    return jnp.sum(jnp.where(indices[:, None] == places[None, :], lookup_table[None, :], 0), axis=1)


def pack_kernel(
    token_request,
    request_leaf,
    leaf_parent,
    mid_parent,
    root_slot,
    mid_slot,
    leaf_slot,
    query,
    kv,
    root,
    mid,
    leaf,
    packed,
):
    count, _, wide = packed.shape
    own_rows = query.shape[0]
    hd = wide // 2
    heads = kv.shape[1] // wide
    for dest in range(count):
        head = dest * heads // count
        packed[dest, 0:own_rows, :] = query[:, dest * wide : (dest + 1) * wide]
        for half in range(2):
            source = (half * heads + head) * hd
            packed[dest, own_rows : 2 * own_rows, half * hd : (half + 1) * hd] = kv[
                :, source : source + hd
            ]
    begin = 2 * own_rows
    part = packed.shape[1] - begin
    me = lax.axis_index("mp")
    for req in range(2):
        leaf_node = request_leaf[token_request[0] + req]
        mid_node = leaf_parent[leaf_node]
        slots = (root_slot[mid_parent[mid_node]], mid_slot[mid_node], leaf_slot[leaf_node])
        levels = []
        for slot, cache in zip(slots, (root, mid, leaf)):
            here = cache.shape[0]
            rows = jnp.zeros(cache.shape[1:], cache.dtype)
            for local in range(here):
                rows = jnp.where(slot == me * here + local, cache[local], rows)
            levels.append(rows)
        top = levels[0].shape[0] - part
        middle = levels[1].shape[0]
        for head in range(heads):
            for half in range(2):
                source = slice((half * heads + head) * hd, (half * heads + head + 1) * hd)
                target = slice(half * hd, (half + 1) * hd)
                place = 4 * head + 2 * req
                packed[place, begin:, target] = levels[0][:part, source]
                packed[place + 1, begin : begin + top, target] = levels[0][part:, source]
                packed[place + 1, begin + top : begin + top + middle, target] = levels[1][:, source]
                packed[place + 1, begin + top + middle :, target] = levels[2][:, source]


def pack(tables, query, kv, root, mid, leaf, count):
    wide = query.shape[1] // count
    part = (root.shape[1] + mid.shape[1] + leaf.shape[1]) // 2
    in_vmem = pl.BlockSpec(memory_space=pltpu.VMEM)
    in_smem = pl.BlockSpec(memory_space=pltpu.SMEM)
    return pl.pallas_call(
        pack_kernel,
        out_shape=jax.ShapeDtypeStruct((count, 2 * query.shape[0] + part, wide), jnp.bfloat16),
        in_specs=[in_smem] * len(tables) + [in_vmem] * 5,
        out_specs=in_vmem,
        compiler_params=pltpu.CompilerParams(vmem_limit_bytes=24 * 1024 * 1024),
        name="pack",
    )(*tables, query, kv, root, mid, leaf)


def attention_kernel(
    meta,
    own,
    across,
    own_left,
    own_right,
    across_left,
    across_right,
    own_far_top,
    own_far_bottom,
    across_far_top,
    across_far_bottom,
    weight_own,
    weight_other,
    piece_0,
    piece_1,
    piece_2,
    piece_3,
    gains,
    cosine,
    sine,
    out,
    rows_all,
    weights,
    q_all,
    k_all,
    v_all,
    pk_all,
    pv_all,
    peak_all,
    total_all,
    acc_all,
):
    pieces = (piece_0, piece_1, piece_2, piece_3)
    me = meta[0]
    cut = meta[1]
    tok, dim = own.shape
    count = rows_all.shape[0] // tok
    hd = gains.shape[1]
    span = pk_all.shape[0] // 2
    part = piece_0.shape[0]
    ring = lax.rem(me, 4)
    base = me - ring
    far_base = 4 - base

    def put(first, step, block, offset=0):
        at = (first + lax.rem(ring + step, 4)) * tok + offset
        at = pl.multiple_of(at, block.shape[0])
        rows_all[pl.ds(at, block.shape[0]), :] = block[...]

    put(base, 0, own)
    put(far_base, 0, across)
    put(base, 3, own_left)
    put(base, 1, own_right)
    put(far_base, 3, across_left)
    put(far_base, 1, across_right)
    put(base, 2, own_far_top)
    put(base, 2, own_far_bottom, tok // 2)
    put(far_base, 2, across_far_top)
    put(far_base, 2, across_far_bottom, tok // 2)
    for step, piece in enumerate(pieces):
        place = pl.multiple_of((ring ^ step) * part, part)
        pk_all[pl.ds(place, part), :] = piece[:, :hd]
        pv_all[pl.ds(place, part), :] = piece[:, hd:]
    core = meta[8]
    weights[core] = weight_own[...].reshape(dim, 2 * hd)
    weights[1 - core] = weight_other[...].reshape(dim, 2 * hd)
    weight_q = weights[0]
    weight_kv = weights[1]

    def turn(raw, gain, cos_now, sin_now):
        scaled = raw * lax.rsqrt(jnp.mean(raw * raw, axis=-1, keepdims=True) + EPS) * gain
        return (scaled * cos_now + pltpu.roll(scaled, hd // 2, 1) * sin_now).astype(jnp.bfloat16)

    large = 4 * tok

    @pl.loop(0, count // 4)
    def _(step):
        at = pl.multiple_of(step * large, large)
        rows = rows_all[pl.ds(at, large), :]
        cos_now = cosine[pl.ds(at, large), :]
        sin_now = sine[pl.ds(at, large), :]
        raw = jnp.dot(rows, weight_q, preferred_element_type=jnp.float32)
        heads = [
            turn(raw[:, half * hd : (half + 1) * hd], gains[0:1, :], cos_now, sin_now)
            for half in range(2)
        ]
        for block in range(4):
            for half in range(2):
                q_at = pl.multiple_of(2 * at + (2 * block + half) * tok, tok)
                q_all[pl.ds(q_at, tok), :] = heads[half][block * tok : (block + 1) * tok]
        raw = jnp.dot(rows, weight_kv, preferred_element_type=jnp.float32)
        k_all[pl.ds(at, large), :] = turn(raw[:, :hd], gains[1:2, :], cos_now, sin_now)
        v_all[pl.ds(at, large), :] = raw[:, hd:].astype(jnp.bfloat16)

    scale = hd ** (-0.5) * LOG2E
    col = lax.broadcasted_iota(jnp.int32, (1, span), 1)
    row = lax.broadcasted_iota(jnp.int32, (2 * tok, 1), 0)
    row = jnp.where(row >= tok, row - tok, row)

    def join(state, q_now, keys, values, allowed):
        peak, total, acc = state
        scores = scale * lax.dot_general(
            q_now, keys, (((1,), (1,)), ((), ())), preferred_element_type=jnp.float32
        )
        scores = jnp.where(allowed, scores, MASKED)
        top = jnp.maximum(peak, jnp.max(scores, axis=1, keepdims=True))
        keep = jnp.exp2(peak - top)
        weights = jnp.exp2(scores - top)
        total = total * keep + jnp.sum(weights, axis=1, keepdims=True)
        acc = acc * keep + jnp.dot(
            weights.astype(jnp.bfloat16), values, preferred_element_type=jnp.float32
        )
        return top, total, acc

    @pl.loop(0, count)
    def _(step):
        first = pl.multiple_of(step * tok, tok)
        q_now = q_all[pl.ds(pl.multiple_of(2 * step * tok, 2 * tok), 2 * tok), :]
        token = row + first
        late = token >= cut

        def prefix(req, state):
            start = pl.multiple_of(req * span, span)
            at = 2 + 3 * req
            inside = jnp.where(
                col < 512,
                (col < meta[at]).astype(jnp.int32),
                jnp.where(
                    col < 768,
                    (col - 512 < meta[at + 1]).astype(jnp.int32),
                    (col - 768 < meta[at + 2]).astype(jnp.int32),
                ),
            )
            mine = (late.astype(jnp.int32) == req).astype(jnp.int32)
            return join(
                state,
                q_now,
                pk_all[pl.ds(start, span), :],
                pv_all[pl.ds(start, span), :],
                inside * mine > 0,
            )

        peak_all[...] = jnp.full((2 * tok, 1), MASKED, jnp.float32)
        total_all[...] = jnp.zeros((2 * tok, 1), jnp.float32)
        acc_all[...] = jnp.zeros((2 * tok, hd), jnp.float32)
        low = (first >= cut).astype(jnp.int32)
        high = (first + tok > cut).astype(jnp.int32)

        @pl.loop(low, high + 1)
        def _(req):
            peak, total, acc = prefix(req, (peak_all[...], total_all[...], acc_all[...]))
            peak_all[...] = peak
            total_all[...] = total
            acc_all[...] = acc

        bottom = jnp.where(late, cut, 0)

        for quarter in range(count // 2):

            @pl.when(step // 2 == quarter)
            def _(quarter=quarter):
                keys = 2 * tok * (quarter + 1)
                other = lax.broadcasted_iota(jnp.int32, (1, keys), 1)
                allowed = jnp.logical_and(other <= token, other >= bottom)
                peak, total, acc = join(
                    (peak_all[...], total_all[...], acc_all[...]),
                    q_now,
                    k_all[0:keys, :],
                    v_all[0:keys, :],
                    allowed,
                )
                done = (acc / total).astype(jnp.bfloat16)
                out[pl.ds(first, tok), 0:hd] = done[:tok]
                out[pl.ds(first, tok), hd : 2 * hd] = done[tok:]


def attend(meta, rows, weights, pieces, gains, cosine, sine):
    group = cosine.shape[0]
    hd = gains.shape[1]
    path_rows = 4 * pieces[0].shape[0]
    in_vmem = pl.BlockSpec(memory_space=pltpu.VMEM)
    return pl.pallas_call(
        attention_kernel,
        out_shape=jax.ShapeDtypeStruct((group, 2 * hd), jnp.bfloat16),
        in_specs=[pl.BlockSpec(memory_space=pltpu.SMEM)] + [in_vmem] * 19,
        out_specs=in_vmem,
        scratch_shapes=[
            pltpu.VMEM((group, rows[0].shape[1]), jnp.bfloat16),
            pltpu.VMEM((2, rows[0].shape[1], 2 * hd), jnp.bfloat16),
            pltpu.VMEM((2 * group, hd), jnp.bfloat16),
            pltpu.VMEM((group, hd), jnp.bfloat16),
            pltpu.VMEM((group, hd), jnp.bfloat16),
            pltpu.VMEM((path_rows, hd), jnp.bfloat16),
            pltpu.VMEM((path_rows, hd), jnp.bfloat16),
            pltpu.VMEM((256, 1), jnp.float32),
            pltpu.VMEM((256, 1), jnp.float32),
            pltpu.VMEM((256, hd), jnp.float32),
        ],
        compiler_params=pltpu.CompilerParams(vmem_limit_bytes=40 * 1024 * 1024),
        name="tree_attention",
    )(meta, *rows, *weights, *pieces, gains, cosine, sine)


def exchange(values):
    return lax.all_to_all(values, BOTH, split_axis=0, concat_axis=0, tiled=True)


def expert(rows, gate_up, down_weight):
    ff_width = down_weight.shape[0]
    both = jnp.dot(rows, gate_up, preferred_element_type=jnp.float32)
    active = (jax.nn.silu(both[:, :ff_width]) * both[:, ff_width:]).astype(jnp.bfloat16)
    return jnp.dot(active, down_weight, preferred_element_type=jnp.float32).astype(jnp.bfloat16)


def per_device(
    hidden,
    norm_gains,
    head_gains,
    query_weight,
    kv_weight,
    out_weight,
    gate_up,
    down_weight,
    next_weight,
    expert_ids,
    route_weights,
    token_request,
    request_leaf,
    leaf_parent,
    mid_parent,
    root_length,
    mid_length,
    leaf_length,
    root_slot,
    mid_slot,
    leaf_slot,
    root_cache,
    mid_cache,
    leaf_cache,
):
    tok, dim = hidden.shape
    hd = head_gains.shape[1]
    kv_width = kv_weight.shape[1] // 2
    kv_heads = kv_width // hd
    group = token_request.shape[0]
    mp_size = lax.axis_size("mp")
    dp_size = lax.axis_size("dp")
    devices = dp_size * mp_size
    me = lax.axis_index("mp")
    own_rows = query_weight.shape[0]

    pair = token_request[0] + jnp.arange(2, dtype=jnp.int32)
    cut = jnp.sum((token_request == pair[0]).astype(jnp.int32))
    leaf_node = look_up(request_leaf, pair)
    mid_node = look_up(leaf_parent, leaf_node)
    root_node = look_up(mid_parent, mid_node)
    lengths = (
        look_up(root_length, root_node),
        look_up(mid_length, mid_node),
        look_up(leaf_length, leaf_node),
    )
    prefix_length = lengths[0] + lengths[1] + lengths[2]
    token = jnp.arange(group, dtype=jnp.int32)
    positions = token + jnp.where(token >= cut, prefix_length[1] - cut, prefix_length[0])
    frequency = THETA ** (-2.0 * jnp.arange(hd // 2, dtype=jnp.float32) / hd)
    angles = positions.astype(jnp.float32)[:, None] * frequency[None, :]
    cos_half = jnp.cos(angles)
    sin_half = jnp.sin(angles)
    cosine = jnp.concatenate([cos_half, cos_half], axis=1)
    sine = jnp.concatenate([-sin_half, sin_half], axis=1)

    normed = rms_norm(hidden, norm_gains[0]).astype(jnp.bfloat16)
    def shift(values, step):
        moves = [(j, j - j % 4 + (j % 4 + step) % 4) for j in range(mp_size)]
        return lax.ppermute(values, "mp", moves)

    across = lax.ppermute(normed, "mp", [(j, (j + 4) % mp_size) for j in range(mp_size)])
    left = shift(normed, 1)
    right = shift(normed, -1)
    late = jnp.concatenate([out_weight, next_weight], axis=1)
    late = jnp.broadcast_to(late[None], (mp_size,) + late.shape)
    late = lax.all_to_all(late, "mp", split_axis=0, concat_axis=0, tiled=True)
    late = late.reshape(mp_size * own_rows, -1)
    out_full = lax.all_gather(late[:, :dim], "dp", axis=0, tiled=True)
    next_full = lax.all_gather(late[:, dim:], "dp", axis=0, tiled=True)

    tables = (
        token_request,
        request_leaf,
        leaf_parent,
        mid_parent,
        root_slot,
        mid_slot,
        leaf_slot,
    )
    packed = pack(
        tables, query_weight, kv_weight, root_cache, mid_cache, leaf_cache, mp_size
    )
    packed, across, left, right, late = lax.optimization_barrier(
        (packed, across, left, right, late)
    )
    packed = lax.all_to_all(packed, "mp", split_axis=0, concat_axis=0, tiled=True)
    wide = packed.shape[2]
    early_end = 2 * own_rows
    early = packed[:, :early_end].reshape(mp_size, 2, own_rows, wide).transpose(1, 0, 2, 3)
    early = jnp.broadcast_to(early[None], (dp_size // 2, 2, mp_size, own_rows, wide))
    early = early.reshape(dp_size, mp_size, own_rows, wide)
    sides = [left, right, shift(across, 1), shift(across, -1)]
    early, *sides = lax.optimization_barrier((early, *sides))
    early = lax.all_to_all(early, "dp", split_axis=0, concat_axis=0, tiled=True)
    far = []
    for near in range(0, 4, 2):
        far += [shift(sides[near][: tok // 2], 1), shift(sides[near + 1][tok // 2 :], -1)]
    own_piece = jnp.sum(packed[:, early_end:].astype(jnp.float32), axis=0).astype(jnp.bfloat16)
    pieces = [own_piece] + [
        lax.ppermute(own_piece, "mp", [(j, j ^ s) for j in range(mp_size)]) for s in range(1, 4)
    ]
    early, far, pieces = lax.optimization_barrier((early, far, pieces))
    early = early.reshape(devices, own_rows, wide)
    weights = (early, lax.ppermute(early, "dp", [(j, j ^ 1) for j in range(dp_size)]))
    rows = [normed, across] + sides + far
    meta = jnp.concatenate(
        [
            jnp.stack([me, cut]),
            jnp.stack(lengths, axis=1).reshape(-1),
            jnp.stack([lax.rem(lax.axis_index("dp"), 2)]),
        ]
    ).astype(jnp.int32)
    attended = attend(meta, rows, weights, pieces, head_gains, cosine, sine)
    attended = lax.all_to_all(
        attended.reshape(mp_size, tok, 2 * hd), "mp", split_axis=0, concat_axis=0, tiled=True
    )
    projected = jnp.einsum(
        "mtk,mkd->td",
        attended,
        out_full.reshape(mp_size, 2 * hd, dim),
        preferred_element_type=jnp.float32,
    )
    after_attention = (hidden.astype(jnp.float32) + projected).astype(jnp.bfloat16)
    moe_in = rms_norm(after_attention, norm_gains[1]).astype(jnp.bfloat16)

    top_k = expert_ids.shape[1]
    capacity = max(2, 5 * tok * top_k // (4 * devices))
    names = expert_ids[:, :, None] == jnp.arange(devices, dtype=jnp.int32)[None, None, :]
    named = jnp.any(names, axis=1)
    route = jnp.sum(jnp.where(names, route_weights[:, :, None], 0.0), axis=1)
    before = jnp.tril(jnp.ones((tok, tok), jnp.bfloat16), -1)
    slot_no = jnp.dot(before, named.astype(jnp.bfloat16), preferred_element_type=jnp.float32)
    slot_no = jnp.where(named, slot_no.astype(jnp.int32), -1)

    def spread(first, last):
        count = jnp.arange(first, last, dtype=jnp.int32)
        taken = slot_no.T[:, None, :] == count[None, :, None]
        return taken.astype(jnp.bfloat16).reshape(devices * (last - first), tok)

    def gather_back(first, last):
        count = jnp.arange(first, last, dtype=jnp.int32)
        taken = slot_no[:, :, None] == count[None, None, :]
        share = jnp.where(taken, route[:, :, None], 0.0).reshape(tok, devices * (last - first))
        upper = lax.reduce_precision(share, 8, 7)
        return jnp.concatenate([upper, share - upper], axis=0).astype(jnp.bfloat16)

    def outbound(first, last, source):
        picked = jnp.dot(spread(first, last), source, preferred_element_type=jnp.float32)
        return picked.astype(jnp.bfloat16).reshape(devices, last - first, dim)

    def mixed(first, last, returned):
        returned = returned.reshape(-1, dim)
        halves = jnp.dot(gather_back(first, last), returned, preferred_element_type=jnp.float32)
        return halves[:tok] + halves[tok:]

    main_in = exchange(outbound(0, MAIN, moe_in))
    main_in, rest_in = lax.optimization_barrier((main_in, outbound(MAIN, capacity, moe_in)))
    rest_in = exchange(rest_in)
    main_out = expert(main_in.reshape(-1, dim), gate_up[0], down_weight[0])
    main_out = exchange(main_out.reshape(devices, MAIN, dim))
    rest_out = expert(rest_in.reshape(-1, dim), gate_up[0], down_weight[0])
    rest_out = rest_out.reshape(devices, capacity - MAIN, dim)
    main_out, rest_out = lax.optimization_barrier((main_out, rest_out))
    rest_out = exchange(rest_out)
    mixture = mixed(0, MAIN, main_out) + mixed(MAIN, capacity, rest_out)
    layer_out = (after_attention.astype(jnp.float32) + mixture).astype(jnp.bfloat16)
    next_in = rms_norm(layer_out, norm_gains[2]).astype(jnp.bfloat16)
    next_raw = jnp.dot(next_in, next_full, preferred_element_type=jnp.float32)
    my_cos = lax.dynamic_slice_in_dim(cosine, me * tok, tok)[:, None, :]
    my_sin = lax.dynamic_slice_in_dim(sine, me * tok, tok)[:, None, :]
    next_keys = rms_norm(next_raw[:, :kv_width].reshape(tok, kv_heads, hd), head_gains[2])
    swapped = jnp.concatenate([next_keys[..., hd // 2 :], next_keys[..., : hd // 2]], axis=-1)
    next_keys = (next_keys * my_cos + swapped * my_sin).astype(jnp.bfloat16)
    next_rows = jnp.concatenate(
        [next_keys.reshape(tok, kv_width), next_raw[:, kv_width:].astype(jnp.bfloat16)], axis=1
    )
    return (layer_out, next_rows)


def solution(mesh):
    both = P(BOTH, None)
    placed = (
        both,
        P(),
        P(),
        both,
        both,
        both,
        P(BOTH, None, None),
        P(BOTH, None, None),
        both,
        both,
        both,
        P("dp"),
        P(),
        P(),
        P(),
        P(),
        P(),
        P(),
        P(),
        P(),
        P(),
        P("mp", None, None),
        P("mp", None, None),
        P("mp", None, None),
    )
    return jax.shard_map(
        per_device,
        mesh=mesh,
        in_specs=placed,
        out_specs=(both, both),
        check_vma=False,
    )
```

```python
import jax
import jax.numpy as jnp
from jax import lax
from jax.experimental import pallas as pl
from jax.experimental.pallas import tpu as pltpu
from jax.sharding import PartitionSpec as P

EPS = 1e-06
THETA = 1000000.0
MASKED = -1e30
LOG2E = 1.4426950408889634
BOTH = ("dp", "mp")
MAIN = 8


def rms_norm(values, weight_row):
    values = values.astype(jnp.float32)
    return values * lax.rsqrt(jnp.mean(values * values, axis=-1, keepdims=True) + EPS) * weight_row


def look_up(lookup_table, indices):
    places = jnp.arange(lookup_table.shape[0], dtype=jnp.int32)
    return jnp.sum(jnp.where(indices[:, None] == places[None, :], lookup_table[None, :], 0), axis=1)


def pack_weights_kernel(query, kv, out_rows, next_rows, packed):
    count = packed.shape[0]
    dim = out_rows.shape[1]
    extra = next_rows.shape[1]
    wide = query.shape[1] // count
    hd = wide // 2
    heads = kv.shape[1] // 2 // hd
    base = dim + extra
    for dest in range(count):
        head = dest * heads // count
        packed[dest, :, 0:dim] = out_rows[...]
        packed[dest, :, dim:base] = next_rows[...]
        packed[dest, :, base : base + wide] = query[:, dest * wide : (dest + 1) * wide]
        for half in range(2):
            source = (half * heads + head) * hd
            target = base + wide + half * hd
            packed[dest, :, target : target + hd] = kv[:, source : source + hd]


def pack_weights(query, kv, out_rows, next_rows, count):
    rows = query.shape[0]
    width = out_rows.shape[1] + next_rows.shape[1] + 2 * (query.shape[1] // count)
    in_vmem = pl.BlockSpec(memory_space=pltpu.VMEM)
    return pl.pallas_call(
        pack_weights_kernel,
        out_shape=jax.ShapeDtypeStruct((count, rows, width), jnp.bfloat16),
        in_specs=[in_vmem] * 4,
        out_specs=in_vmem,
        name="pack_weights",
    )(query, kv, out_rows, next_rows)


def pack_paths_kernel(
    token_request,
    request_leaf,
    leaf_parent,
    mid_parent,
    root_slot,
    mid_slot,
    leaf_slot,
    root,
    mid,
    leaf,
    packed,
):
    count, part, wide = packed.shape
    hd = wide // 2
    heads = count // 4
    me = lax.axis_index("mp")
    for req in range(2):
        leaf_node = request_leaf[token_request[0] + req]
        mid_node = leaf_parent[leaf_node]
        slots = (root_slot[mid_parent[mid_node]], mid_slot[mid_node], leaf_slot[leaf_node])
        levels = []
        for slot, cache in zip(slots, (root, mid, leaf)):
            here = cache.shape[0]
            rows = jnp.zeros(cache.shape[1:], cache.dtype)
            for local in range(here):
                rows = jnp.where(slot == me * here + local, cache[local], rows)
            levels.append(rows)
        top = levels[0].shape[0] - part
        middle = levels[1].shape[0]
        for head in range(heads):
            for half in range(2):
                source = slice((half * heads + head) * hd, (half * heads + head + 1) * hd)
                target = slice(half * hd, (half + 1) * hd)
                place = 4 * head + 2 * req
                packed[place, :, target] = levels[0][:part, source]
                packed[place + 1, 0:top, target] = levels[0][part:, source]
                packed[place + 1, top : top + middle, target] = levels[1][:, source]
                packed[place + 1, top + middle :, target] = levels[2][:, source]


def pack_paths(tables, root, mid, leaf, count):
    wide = root.shape[2] // 2
    part = (root.shape[1] + mid.shape[1] + leaf.shape[1]) // 2
    in_vmem = pl.BlockSpec(memory_space=pltpu.VMEM)
    in_smem = pl.BlockSpec(memory_space=pltpu.SMEM)
    return pl.pallas_call(
        pack_paths_kernel,
        out_shape=jax.ShapeDtypeStruct((count, part, wide), jnp.bfloat16),
        in_specs=[in_smem] * len(tables) + [in_vmem] * 3,
        out_specs=in_vmem,
        compiler_params=pltpu.CompilerParams(vmem_limit_bytes=24 * 1024 * 1024),
        name="pack_paths",
    )(*tables, root, mid, leaf)


def attention_kernel(
    meta,
    own,
    across,
    own_left,
    own_right,
    across_left,
    across_right,
    own_far,
    across_far,
    weight_own,
    weight_other,
    piece_0,
    piece_1,
    piece_2,
    piece_3,
    gains,
    cosine,
    sine,
    out,
    rows_all,
    weights,
    q_all,
    k_all,
    v_all,
    pk_all,
    pv_all,
    peak_all,
    total_all,
    acc_all,
):
    pieces = (piece_0, piece_1, piece_2, piece_3)
    me = meta[0]
    cut = meta[1]
    tok, dim = own.shape
    count = rows_all.shape[0] // tok
    hd = gains.shape[1]
    span = pk_all.shape[0] // 2
    part = piece_0.shape[0]
    ring = lax.rem(me, 4)
    base = me - ring
    far_base = 4 - base

    def put(first, step, block):
        at = pl.multiple_of((first + lax.rem(ring + step, 4)) * tok, tok)
        rows_all[pl.ds(at, tok), :] = block[...]

    put(base, 0, own)
    put(far_base, 0, across)
    put(base, 3, own_left)
    put(base, 1, own_right)
    put(far_base, 3, across_left)
    put(far_base, 1, across_right)
    put(base, 2, own_far)
    put(far_base, 2, across_far)
    for step, piece in enumerate(pieces):
        place = pl.multiple_of((ring ^ step) * part, part)
        pk_all[pl.ds(place, part), :] = piece[:, :hd]
        pv_all[pl.ds(place, part), :] = piece[:, hd:]
    core = meta[8]
    weights[core] = weight_own[...]
    weights[1 - core] = weight_other[...]
    weight_q = weights[0]
    weight_kv = weights[1]

    def turn(raw, gain, cos_now, sin_now):
        scaled = raw * lax.rsqrt(jnp.mean(raw * raw, axis=-1, keepdims=True) + EPS) * gain
        return (scaled * cos_now + pltpu.roll(scaled, hd // 2, 1) * sin_now).astype(jnp.bfloat16)

    large = 4 * tok

    @pl.loop(0, count // 4)
    def _(step):
        at = pl.multiple_of(step * large, large)
        rows = rows_all[pl.ds(at, large), :]
        cos_now = cosine[pl.ds(at, large), :]
        sin_now = sine[pl.ds(at, large), :]
        raw = jnp.dot(rows, weight_q, preferred_element_type=jnp.float32)
        heads = [
            turn(raw[:, half * hd : (half + 1) * hd], gains[0:1, :], cos_now, sin_now)
            for half in range(2)
        ]
        for block in range(4):
            for half in range(2):
                q_at = pl.multiple_of(2 * at + (2 * block + half) * tok, tok)
                q_all[pl.ds(q_at, tok), :] = heads[half][block * tok : (block + 1) * tok]
        raw = jnp.dot(rows, weight_kv, preferred_element_type=jnp.float32)
        k_all[pl.ds(at, large), :] = turn(raw[:, :hd], gains[1:2, :], cos_now, sin_now)
        v_all[pl.ds(at, large), :] = raw[:, hd:].astype(jnp.bfloat16)

    scale = hd ** (-0.5) * LOG2E
    col = lax.broadcasted_iota(jnp.int32, (1, span), 1)
    row = lax.broadcasted_iota(jnp.int32, (2 * tok, 1), 0)
    row = jnp.where(row >= tok, row - tok, row)

    def join(state, q_now, keys, values, allowed):
        peak, total, acc = state
        scores = scale * lax.dot_general(
            q_now, keys, (((1,), (1,)), ((), ())), preferred_element_type=jnp.float32
        )
        scores = jnp.where(allowed, scores, MASKED)
        top = jnp.maximum(peak, jnp.max(scores, axis=1, keepdims=True))
        keep = jnp.exp2(peak - top)
        weights = jnp.exp2(scores - top)
        total = total * keep + jnp.sum(weights, axis=1, keepdims=True)
        acc = acc * keep + jnp.dot(
            weights.astype(jnp.bfloat16), values, preferred_element_type=jnp.float32
        )
        return top, total, acc

    @pl.loop(0, count)
    def _(step):
        first = pl.multiple_of(step * tok, tok)
        q_now = q_all[pl.ds(pl.multiple_of(2 * step * tok, 2 * tok), 2 * tok), :]
        token = row + first
        late = token >= cut

        def prefix(req, state):
            start = pl.multiple_of(req * span, span)
            at = 2 + 3 * req
            inside = jnp.where(
                col < 512,
                (col < meta[at]).astype(jnp.int32),
                jnp.where(
                    col < 768,
                    (col - 512 < meta[at + 1]).astype(jnp.int32),
                    (col - 768 < meta[at + 2]).astype(jnp.int32),
                ),
            )
            mine = (late.astype(jnp.int32) == req).astype(jnp.int32)
            return join(
                state,
                q_now,
                pk_all[pl.ds(start, span), :],
                pv_all[pl.ds(start, span), :],
                inside * mine > 0,
            )

        peak_all[...] = jnp.full((2 * tok, 1), MASKED, jnp.float32)
        total_all[...] = jnp.zeros((2 * tok, 1), jnp.float32)
        acc_all[...] = jnp.zeros((2 * tok, hd), jnp.float32)
        low = (first >= cut).astype(jnp.int32)
        high = (first + tok > cut).astype(jnp.int32)

        @pl.loop(low, high + 1)
        def _(req):
            peak, total, acc = prefix(req, (peak_all[...], total_all[...], acc_all[...]))
            peak_all[...] = peak
            total_all[...] = total
            acc_all[...] = acc

        bottom = jnp.where(late, cut, 0)

        for quarter in range(count // 2):

            @pl.when(step // 2 == quarter)
            def _(quarter=quarter):
                keys = 2 * tok * (quarter + 1)
                other = lax.broadcasted_iota(jnp.int32, (1, keys), 1)
                allowed = jnp.logical_and(other <= token, other >= bottom)
                peak, total, acc = join(
                    (peak_all[...], total_all[...], acc_all[...]),
                    q_now,
                    k_all[0:keys, :],
                    v_all[0:keys, :],
                    allowed,
                )
                done = (acc / total).astype(jnp.bfloat16)
                out[pl.ds(first, tok), 0:hd] = done[:tok]
                out[pl.ds(first, tok), hd : 2 * hd] = done[tok:]


def attend(meta, rows, weights, pieces, gains, cosine, sine):
    group = cosine.shape[0]
    hd = gains.shape[1]
    path_rows = 4 * pieces[0].shape[0]
    in_vmem = pl.BlockSpec(memory_space=pltpu.VMEM)
    return pl.pallas_call(
        attention_kernel,
        out_shape=jax.ShapeDtypeStruct((group, 2 * hd), jnp.bfloat16),
        in_specs=[pl.BlockSpec(memory_space=pltpu.SMEM)] + [in_vmem] * 17,
        out_specs=in_vmem,
        scratch_shapes=[
            pltpu.VMEM((group, rows[0].shape[1]), jnp.bfloat16),
            pltpu.VMEM((2, rows[0].shape[1], 2 * hd), jnp.bfloat16),
            pltpu.VMEM((2 * group, hd), jnp.bfloat16),
            pltpu.VMEM((group, hd), jnp.bfloat16),
            pltpu.VMEM((group, hd), jnp.bfloat16),
            pltpu.VMEM((path_rows, hd), jnp.bfloat16),
            pltpu.VMEM((path_rows, hd), jnp.bfloat16),
            pltpu.VMEM((256, 1), jnp.float32),
            pltpu.VMEM((256, 1), jnp.float32),
            pltpu.VMEM((256, hd), jnp.float32),
        ],
        compiler_params=pltpu.CompilerParams(vmem_limit_bytes=40 * 1024 * 1024),
        name="tree_attention",
    )(meta, *rows, *weights, *pieces, gains, cosine, sine)


def project_kernel(attended, weight, hidden, gain, out, normed, joined, layer):
    count, _, wide = attended.shape
    step = pl.program_id(0)

    @pl.when(step == 0)
    def _():
        for source in range(count):
            joined[:, source * wide : (source + 1) * wide] = attended[source]

    added = jnp.dot(joined[...], weight[...], preferred_element_type=jnp.float32)
    done = (hidden[...].astype(jnp.float32) + added).astype(jnp.bfloat16)
    out[...] = done
    layer[step] = done

    @pl.when(step == layer.shape[0] - 1)
    def _():
        columns = layer.shape[2]
        parts = [layer[at].astype(jnp.float32) for at in range(layer.shape[0])]
        square = sum(jnp.sum(part * part, axis=1, keepdims=True) for part in parts)
        inverse = lax.rsqrt(square / (columns * len(parts)) + EPS)
        for at, part in enumerate(parts):
            place = slice(at * columns, (at + 1) * columns)
            normed[:, place] = (part * inverse * gain[:, place]).astype(jnp.bfloat16)


def project(attended, weight, hidden, gain):
    tok, dim = hidden.shape
    columns = dim // 4
    return pl.pallas_call(
        project_kernel,
        grid=(4,),
        out_shape=(
            jax.ShapeDtypeStruct(hidden.shape, hidden.dtype),
            jax.ShapeDtypeStruct(hidden.shape, hidden.dtype),
        ),
        in_specs=[
            pl.BlockSpec(attended.shape, lambda j: (0, 0, 0)),
            pl.BlockSpec((dim, columns), lambda j: (0, j)),
            pl.BlockSpec((tok, columns), lambda j: (0, j)),
            pl.BlockSpec((1, dim), lambda j: (0, 0)),
        ],
        out_specs=(
            pl.BlockSpec((tok, columns), lambda j: (0, j)),
            pl.BlockSpec((tok, dim), lambda j: (0, 0)),
        ),
        scratch_shapes=[
            pltpu.VMEM((tok, dim), jnp.bfloat16),
            pltpu.VMEM((4, tok, columns), jnp.bfloat16),
        ],
        compiler_params=pltpu.CompilerParams(vmem_limit_bytes=24 * 1024 * 1024),
        name="project",
    )(attended, weight, hidden, gain)


def exchange(values):
    return lax.all_to_all(values, BOTH, split_axis=0, concat_axis=0, tiled=True)


def expert(rows, gate_up, down_weight):
    ff_width = down_weight.shape[0]
    both = jnp.dot(rows, gate_up, preferred_element_type=jnp.float32)
    active = (jax.nn.silu(both[:, :ff_width]) * both[:, ff_width:]).astype(jnp.bfloat16)
    return jnp.dot(active, down_weight, preferred_element_type=jnp.float32).astype(jnp.bfloat16)


def rest_kernel(rows, gate_up, down_weight, main_block, out):
    del main_block
    ff_width = down_weight.shape[0]
    spans = out.shape[0]
    wide = out.shape[2]
    chunks = down_weight.shape[1] // wide
    per = rows.shape[0] // spans
    both = jnp.dot(rows[...], gate_up[...], preferred_element_type=jnp.float32)
    gate = both[:, :ff_width]
    active = (gate / (1.0 + jnp.exp(-gate)) * both[:, ff_width:]).astype(jnp.bfloat16)
    served = jnp.dot(active, down_weight[...], preferred_element_type=jnp.float32)
    served = served.astype(jnp.bfloat16)
    batch = 16
    size = batch * per * chunks
    to = lax.broadcasted_iota(jnp.int32, (size, size), 0)
    source = lax.broadcasted_iota(jnp.int32, (size, size), 1)
    device = to // (per * chunks)
    chunk = to // per % chunks
    wanted = chunk * (batch * per) + device * per + to % per
    order = (source == wanted).astype(jnp.bfloat16)
    for first in range(0, spans, batch):
        stacked = jnp.concatenate(
            [
                served[first * per : (first + batch) * per, at * wide : (at + 1) * wide]
                for at in range(chunks)
            ],
            axis=0,
        )
        sorted_rows = jnp.dot(order, stacked, preferred_element_type=jnp.float32)
        out[first : first + batch] = sorted_rows.reshape(batch, per * chunks, wide).astype(
            jnp.bfloat16
        )


def expert_rest(rows, gate_up, down_weight, main_block):
    spans, height, wide = main_block.shape
    extra = rows.shape[0] // spans * down_weight.shape[1] // wide
    in_vmem = pl.BlockSpec(memory_space=pltpu.VMEM)
    return pl.pallas_call(
        rest_kernel,
        grid=(1,),
        out_shape=jax.ShapeDtypeStruct(main_block.shape, main_block.dtype),
        in_specs=[in_vmem, in_vmem, in_vmem, pl.BlockSpec(memory_space=pl.ANY)],
        out_specs=pl.BlockSpec((spans, extra, wide), lambda i: (0, height // extra - 1, 0)),
        input_output_aliases={3: 0},
        compiler_params=pltpu.CompilerParams(vmem_limit_bytes=48 * 1024 * 1024),
        name="expert_rest",
    )(rows, gate_up, down_weight, main_block)


def finish_kernel(
    main_share,
    rest_share,
    main_rows,
    rest_rows,
    stream,
    next_weight,
    norm_gain,
    head_gain,
    cosine,
    sine,
    out,
    next_rows,
    layer,
):
    tok = stream.shape[0]
    count = main_share.shape[1]
    wide = main_rows.shape[2]
    hd = head_gain.shape[1]
    step = pl.program_id(0)

    def flat(values):
        values = values[...].astype(jnp.float32).reshape(count, wide)
        return values.astype(jnp.bfloat16)

    total = jnp.dot(main_share[...], flat(main_rows), preferred_element_type=jnp.float32)
    total += jnp.dot(rest_share[0], flat(rest_rows), preferred_element_type=jnp.float32)
    done = (stream[...].astype(jnp.float32) + total[:tok] + total[tok:]).astype(jnp.bfloat16)
    out[...] = done
    layer[step] = done

    @pl.when(step == layer.shape[0] - 1)
    def _():
        parts = [layer[at].astype(jnp.float32) for at in range(layer.shape[0])]
        square = sum(jnp.sum(part * part, axis=1, keepdims=True) for part in parts)
        inverse = lax.rsqrt(square / (wide * len(parts)) + EPS)
        raw = jnp.zeros((tok, next_weight.shape[1]), jnp.float32)
        for at, part in enumerate(parts):
            columns = slice(at * wide, (at + 1) * wide)
            normed = (part * inverse * norm_gain[:, columns]).astype(jnp.bfloat16)
            raw += jnp.dot(normed, next_weight[columns, :], preferred_element_type=jnp.float32)
        half = raw.shape[1] // 2
        for head in range(half // hd):
            columns = slice(head * hd, (head + 1) * hd)
            values = raw[:, columns]
            values = values * lax.rsqrt(jnp.mean(values * values, axis=-1, keepdims=True) + EPS)
            values = values * head_gain[...]
            values = values * cosine[...] + pltpu.roll(values, hd // 2, 1) * sine[...]
            next_rows[:, columns] = values.astype(jnp.bfloat16)
        next_rows[:, half:] = raw[:, half:].astype(jnp.bfloat16)


def finish(main_share, rest_share, returned, stream, late, norm_gain, head_gain, cos, sin):
    devices, height, wide = returned.shape
    tok, dim = stream.shape
    extra = late.shape[1] - dim
    chunks = dim // wide
    rows = height // (chunks + 1)
    shape = main_share.shape

    def fixed(values):
        return pl.BlockSpec(values.shape, lambda j: (0, 0))

    return pl.pallas_call(
        finish_kernel,
        grid=(chunks,),
        out_shape=(
            jax.ShapeDtypeStruct(stream.shape, stream.dtype),
            jax.ShapeDtypeStruct((tok, extra), stream.dtype),
        ),
        in_specs=[
            fixed(main_share),
            pl.BlockSpec((1,) + shape, lambda j: (j, 0, 0)),
            pl.BlockSpec((devices, rows, wide), lambda j: (0, j, 0)),
            pl.BlockSpec((devices, rows, wide), lambda j: (0, chunks, 0)),
            pl.BlockSpec((tok, wide), lambda j: (0, j)),
            pl.BlockSpec((dim, extra), lambda j: (0, dim // extra)),
            fixed(norm_gain),
            fixed(head_gain),
            fixed(cos),
            fixed(sin),
        ],
        out_specs=(
            pl.BlockSpec((tok, wide), lambda j: (0, j)),
            pl.BlockSpec((tok, extra), lambda j: (0, 0)),
        ),
        scratch_shapes=[pltpu.VMEM((chunks, tok, wide), jnp.bfloat16)],
        compiler_params=pltpu.CompilerParams(vmem_limit_bytes=32 * 1024 * 1024),
        name="finish",
    )(main_share, rest_share, returned, returned, stream, late, norm_gain, head_gain, cos, sin)


def per_device(
    hidden,
    norm_gains,
    head_gains,
    query_weight,
    kv_weight,
    out_weight,
    gate_up,
    down_weight,
    next_weight,
    expert_ids,
    route_weights,
    token_request,
    request_leaf,
    leaf_parent,
    mid_parent,
    root_length,
    mid_length,
    leaf_length,
    root_slot,
    mid_slot,
    leaf_slot,
    root_cache,
    mid_cache,
    leaf_cache,
):
    tok, dim = hidden.shape
    hd = head_gains.shape[1]
    group = token_request.shape[0]
    mp_size = lax.axis_size("mp")
    dp_size = lax.axis_size("dp")
    devices = dp_size * mp_size
    me = lax.axis_index("mp")
    own_rows = query_weight.shape[0]

    pair = token_request[0] + jnp.arange(2, dtype=jnp.int32)
    cut = jnp.sum((token_request == pair[0]).astype(jnp.int32))
    leaf_node = look_up(request_leaf, pair)
    mid_node = look_up(leaf_parent, leaf_node)
    root_node = look_up(mid_parent, mid_node)
    lengths = (
        look_up(root_length, root_node),
        look_up(mid_length, mid_node),
        look_up(leaf_length, leaf_node),
    )
    prefix_length = lengths[0] + lengths[1] + lengths[2]
    token = jnp.arange(group, dtype=jnp.int32)
    positions = token + jnp.where(token >= cut, prefix_length[1] - cut, prefix_length[0])
    frequency = THETA ** (-2.0 * jnp.arange(hd // 2, dtype=jnp.float32) / hd)
    angles = positions.astype(jnp.float32)[:, None] * frequency[None, :]
    cos_half = jnp.cos(angles)
    sin_half = jnp.sin(angles)
    cosine = jnp.concatenate([cos_half, cos_half], axis=1)
    sine = jnp.concatenate([-sin_half, sin_half], axis=1)

    normed = rms_norm(hidden, norm_gains[0]).astype(jnp.bfloat16)
    def shift(values, step):
        moves = [(j, j - j % 4 + (j % 4 + step) % 4) for j in range(mp_size)]
        return lax.ppermute(values, "mp", moves)

    across = lax.ppermute(normed, "mp", [(j, (j + 4) % mp_size) for j in range(mp_size)])
    left = shift(normed, 1)
    right = shift(normed, -1)
    packed = pack_weights(query_weight, kv_weight, out_weight, next_weight, mp_size)
    packed = lax.all_to_all(packed, "mp", split_axis=0, concat_axis=0, tiled=True)
    packed = packed.reshape(mp_size * own_rows, -1)
    late_width = dim + next_weight.shape[1]
    late = lax.all_gather(packed[:, :late_width], "dp", axis=0, tiled=True)
    early = packed[:, late_width:].reshape(packed.shape[0], 2, 2 * hd).transpose(1, 0, 2)
    early = jnp.broadcast_to(early[None], (dp_size // 2,) + early.shape)
    early = early.reshape(dp_size, packed.shape[0], 2 * hd)
    early = lax.all_to_all(early, "dp", split_axis=0, concat_axis=0, tiled=True)
    early = early.reshape(dim, 2 * hd)
    weights = (early, lax.ppermute(early, "dp", [(j, j ^ 1) for j in range(dp_size)]))
    sides = [left, right, shift(across, 1), shift(across, -1)]
    far = [shift(left, 1), shift(sides[3], -1)]
    tables = (
        token_request,
        request_leaf,
        leaf_parent,
        mid_parent,
        root_slot,
        mid_slot,
        leaf_slot,
    )
    path = pack_paths(tables, root_cache, mid_cache, leaf_cache, mp_size)
    path, sides = lax.optimization_barrier((path, sides))
    path = lax.all_to_all(path, "mp", split_axis=0, concat_axis=0, tiled=True)
    own_piece = jnp.sum(path.astype(jnp.float32), axis=0).astype(jnp.bfloat16)
    own_piece, far = lax.optimization_barrier((own_piece, far))
    pieces = [own_piece] + [
        lax.ppermute(own_piece, "mp", [(j, j ^ s) for j in range(mp_size)]) for s in range(1, 4)
    ]
    rows = [normed, across] + sides + far
    meta = jnp.concatenate(
        [
            jnp.stack([me, cut]),
            jnp.stack(lengths, axis=1).reshape(-1),
            jnp.stack([lax.rem(lax.axis_index("dp"), 2)]),
        ]
    ).astype(jnp.int32)
    attended = attend(meta, rows, weights, pieces, head_gains, cosine, sine)
    attended = lax.all_to_all(
        attended.reshape(mp_size, tok, 2 * hd), "mp", split_axis=0, concat_axis=0, tiled=True
    )
    after_attention, moe_in = project(attended, late, hidden, norm_gains[1:2])

    top_k = expert_ids.shape[1]
    capacity = max(2, 5 * tok * top_k // (4 * devices))
    names = expert_ids[:, :, None] == jnp.arange(devices, dtype=jnp.int32)[None, None, :]
    named = jnp.any(names, axis=1)
    route = jnp.sum(jnp.where(names, route_weights[:, :, None], 0.0), axis=1)
    before = jnp.tril(jnp.ones((tok, tok), jnp.bfloat16), -1)
    slot_no = jnp.dot(before, named.astype(jnp.bfloat16), preferred_element_type=jnp.float32)
    slot_no = jnp.where(named, slot_no.astype(jnp.int32), -1)

    def spread(first, last):
        count = jnp.arange(first, last, dtype=jnp.int32)
        taken = slot_no.T[:, None, :] == count[None, :, None]
        return taken.astype(jnp.bfloat16).reshape(devices * (last - first), tok)

    def gather_back(first, last):
        count = jnp.arange(first, last, dtype=jnp.int32)
        taken = slot_no[:, :, None] == count[None, None, :]
        share = jnp.where(taken, route[:, :, None], 0.0).reshape(tok, devices * (last - first))
        upper = lax.reduce_precision(share, 8, 7)
        return jnp.concatenate([upper, share - upper], axis=0).astype(jnp.bfloat16)

    def outbound(first, last, source):
        picked = jnp.dot(spread(first, last), source, preferred_element_type=jnp.float32)
        return picked.astype(jnp.bfloat16).reshape(devices, last - first, dim)

    main_in = exchange(outbound(0, MAIN, moe_in))
    main_in, rest_in = lax.optimization_barrier((main_in, outbound(MAIN, capacity, moe_in)))
    rest_in = exchange(rest_in)
    chunks = MAIN // (capacity - MAIN)
    wide = dim // chunks
    main_out = expert(main_in.reshape(-1, dim), gate_up[0], down_weight[0])
    main_out = main_out.reshape(devices, MAIN, chunks, wide).transpose(0, 2, 1, 3)
    main_out = main_out.reshape(devices, MAIN * chunks, wide)
    main_out = jnp.pad(main_out, ((0, 0), (0, MAIN), (0, 0)))
    main_out, rest_in = lax.optimization_barrier((main_out, rest_in))
    returned = exchange(expert_rest(rest_in.reshape(-1, dim), gate_up[0], down_weight[0], main_out))
    main_share = gather_back(0, MAIN)
    rest_share = gather_back(MAIN, capacity).reshape(1, 2 * tok, devices, 1, capacity - MAIN)
    which = jnp.eye(chunks, dtype=jnp.bfloat16).reshape(chunks, 1, 1, chunks, 1)
    rest_share = (rest_share * which).reshape(chunks, 2 * tok, devices * MAIN)
    my_cos = lax.dynamic_slice_in_dim(cosine, me * tok, tok)
    my_sin = lax.dynamic_slice_in_dim(sine, me * tok, tok)
    layer_out, next_rows = finish(
        main_share,
        rest_share,
        returned,
        after_attention,
        late,
        norm_gains[2:3],
        head_gains[2:3],
        my_cos,
        my_sin,
    )
    return (layer_out, next_rows)


def solution(mesh):
    both = P(BOTH, None)
    placed = (
        both,
        P(),
        P(),
        both,
        both,
        both,
        P(BOTH, None, None),
        P(BOTH, None, None),
        both,
        both,
        both,
        P("dp"),
        P(),
        P(),
        P(),
        P(),
        P(),
        P(),
        P(),
        P(),
        P(),
        P("mp", None, None),
        P("mp", None, None),
        P("mp", None, None),
    )
    return jax.shard_map(
        per_device,
        mesh=mesh,
        in_specs=placed,
        out_specs=(both, both),
        check_vma=False,
    )
```

```python
import jax
import jax.numpy as jnp
from jax import lax
from jax.experimental import pallas as pl
from jax.experimental.pallas import tpu as pltpu
from jax.sharding import PartitionSpec as P

EPS = 1e-06
THETA = 1000000.0
MASKED = -1e30
LOG2E = 1.4426950408889634
BOTH = ("dp", "mp")
MAIN = 8


def rms_norm(values, weight_row):
    values = values.astype(jnp.float32)
    return values * lax.rsqrt(jnp.mean(values * values, axis=-1, keepdims=True) + EPS) * weight_row


def look_up(lookup_table, indices):
    places = jnp.arange(lookup_table.shape[0], dtype=jnp.int32)
    return jnp.sum(jnp.where(indices[:, None] == places[None, :], lookup_table[None, :], 0), axis=1)


def pack_weights_kernel(query, kv, out_rows, next_rows, packed):
    count = packed.shape[0]
    dim = out_rows.shape[1]
    extra = next_rows.shape[1]
    wide = query.shape[1] // count
    hd = wide // 2
    heads = kv.shape[1] // 2 // hd
    base = dim + extra
    for dest in range(count):
        head = dest * heads // count
        for half in range(2):
            at = half * base // 2
            packed[dest, :, at : at + dim // 2] = out_rows[
                :, half * dim // 2 : (half + 1) * dim // 2
            ]
            packed[dest, :, at + dim // 2 : at + base // 2] = next_rows[
                :, half * extra // 2 : (half + 1) * extra // 2
            ]
        packed[dest, :, base : base + wide] = query[:, dest * wide : (dest + 1) * wide]
        for half in range(2):
            source = (half * heads + head) * hd
            target = base + wide + half * hd
            packed[dest, :, target : target + hd] = kv[:, source : source + hd]


def pack_weights(query, kv, out_rows, next_rows, count):
    rows = query.shape[0]
    width = out_rows.shape[1] + next_rows.shape[1] + 2 * (query.shape[1] // count)
    in_vmem = pl.BlockSpec(memory_space=pltpu.VMEM)
    return pl.pallas_call(
        pack_weights_kernel,
        out_shape=jax.ShapeDtypeStruct((count, rows, width), jnp.bfloat16),
        in_specs=[in_vmem] * 4,
        out_specs=in_vmem,
        name="pack_weights",
    )(query, kv, out_rows, next_rows)


def pack_paths_kernel(
    token_request,
    request_leaf,
    leaf_parent,
    mid_parent,
    root_slot,
    mid_slot,
    leaf_slot,
    root,
    mid,
    leaf,
    packed,
):
    count, part, wide = packed.shape
    hd = wide // 2
    heads = count // 4
    me = lax.axis_index("mp")
    for req in range(2):
        leaf_node = request_leaf[token_request[0] + req]
        mid_node = leaf_parent[leaf_node]
        slots = (root_slot[mid_parent[mid_node]], mid_slot[mid_node], leaf_slot[leaf_node])
        levels = []
        for slot, cache in zip(slots, (root, mid, leaf)):
            here = cache.shape[0]
            rows = jnp.zeros(cache.shape[1:], cache.dtype)
            for local in range(here):
                rows = jnp.where(slot == me * here + local, cache[local], rows)
            levels.append(rows)
        top = levels[0].shape[0] - part
        middle = levels[1].shape[0]
        for head in range(heads):
            for half in range(2):
                source = slice((half * heads + head) * hd, (half * heads + head + 1) * hd)
                target = slice(half * hd, (half + 1) * hd)
                place = 4 * head + 2 * req
                packed[place, :, target] = levels[0][:part, source]
                packed[place + 1, 0:top, target] = levels[0][part:, source]
                packed[place + 1, top : top + middle, target] = levels[1][:, source]
                packed[place + 1, top + middle :, target] = levels[2][:, source]


def pack_paths(tables, root, mid, leaf, count):
    wide = root.shape[2] // 2
    part = (root.shape[1] + mid.shape[1] + leaf.shape[1]) // 2
    in_vmem = pl.BlockSpec(memory_space=pltpu.VMEM)
    in_smem = pl.BlockSpec(memory_space=pltpu.SMEM)
    return pl.pallas_call(
        pack_paths_kernel,
        out_shape=jax.ShapeDtypeStruct((count, part, wide), jnp.bfloat16),
        in_specs=[in_smem] * len(tables) + [in_vmem] * 3,
        out_specs=in_vmem,
        compiler_params=pltpu.CompilerParams(vmem_limit_bytes=24 * 1024 * 1024),
        name="pack_paths",
    )(*tables, root, mid, leaf)


def attention_kernel(
    meta,
    own,
    across,
    own_left,
    own_right,
    across_left,
    across_right,
    own_far,
    across_far,
    weight_own,
    weight_other,
    piece_0,
    piece_1,
    piece_2,
    piece_3,
    gains,
    cosine,
    sine,
    out,
    rows_all,
    weights,
    q_all,
    k_all,
    v_all,
    pk_all,
    pv_all,
    peak_all,
    total_all,
    acc_all,
):
    pieces = (piece_0, piece_1, piece_2, piece_3)
    me = meta[0]
    cut = meta[1]
    tok, dim = own.shape
    count = rows_all.shape[0] // tok
    hd = gains.shape[1]
    span = pk_all.shape[0] // 2
    part = piece_0.shape[0]
    ring = lax.rem(me, 4)
    base = me - ring
    far_base = 4 - base

    def put(first, step, block):
        at = pl.multiple_of((first + lax.rem(ring + step, 4)) * tok, tok)
        rows_all[pl.ds(at, tok), :] = block[...]

    put(base, 0, own)
    put(far_base, 0, across)
    put(base, 3, own_left)
    put(base, 1, own_right)
    put(far_base, 3, across_left)
    put(far_base, 1, across_right)
    put(base, 2, own_far)
    put(far_base, 2, across_far)
    for step, piece in enumerate(pieces):
        place = pl.multiple_of((ring ^ step) * part, part)
        pk_all[pl.ds(place, part), :] = piece[:, :hd]
        pv_all[pl.ds(place, part), :] = piece[:, hd:]
    core = meta[8]
    weights[core] = weight_own[...]
    weights[1 - core] = weight_other[...]
    weight_q = weights[0]
    weight_kv = weights[1]

    def turn(raw, gain, cos_now, sin_now):
        scaled = raw * lax.rsqrt(jnp.mean(raw * raw, axis=-1, keepdims=True) + EPS) * gain
        return (scaled * cos_now + pltpu.roll(scaled, hd // 2, 1) * sin_now).astype(jnp.bfloat16)

    large = 4 * tok

    @pl.loop(0, count // 4)
    def _(step):
        at = pl.multiple_of(step * large, large)
        rows = rows_all[pl.ds(at, large), :]
        cos_now = cosine[pl.ds(at, large), :]
        sin_now = sine[pl.ds(at, large), :]
        raw = jnp.dot(rows, weight_q, preferred_element_type=jnp.float32)
        heads = [
            turn(raw[:, half * hd : (half + 1) * hd], gains[0:1, :], cos_now, sin_now)
            for half in range(2)
        ]
        for block in range(4):
            for half in range(2):
                q_at = pl.multiple_of(2 * at + (2 * block + half) * tok, tok)
                q_all[pl.ds(q_at, tok), :] = heads[half][block * tok : (block + 1) * tok]
        raw = jnp.dot(rows, weight_kv, preferred_element_type=jnp.float32)
        k_all[pl.ds(at, large), :] = turn(raw[:, :hd], gains[1:2, :], cos_now, sin_now)
        v_all[pl.ds(at, large), :] = raw[:, hd:].astype(jnp.bfloat16)

    scale = hd ** (-0.5) * LOG2E
    col = lax.broadcasted_iota(jnp.int32, (1, span), 1)
    row = lax.broadcasted_iota(jnp.int32, (2 * tok, 1), 0)
    row = jnp.where(row >= tok, row - tok, row)

    def join(state, q_now, keys, values, allowed):
        peak, total, acc = state
        scores = scale * lax.dot_general(
            q_now, keys, (((1,), (1,)), ((), ())), preferred_element_type=jnp.float32
        )
        scores = jnp.where(allowed, scores, MASKED)
        top = jnp.maximum(peak, jnp.max(scores, axis=1, keepdims=True))
        keep = jnp.exp2(peak - top)
        weights = jnp.exp2(scores - top)
        total = total * keep + jnp.sum(weights, axis=1, keepdims=True)
        acc = acc * keep + jnp.dot(
            weights.astype(jnp.bfloat16), values, preferred_element_type=jnp.float32
        )
        return top, total, acc

    @pl.loop(0, count)
    def _(step):
        first = pl.multiple_of(step * tok, tok)
        q_now = q_all[pl.ds(pl.multiple_of(2 * step * tok, 2 * tok), 2 * tok), :]
        token = row + first
        late = token >= cut

        def prefix(req, state):
            start = pl.multiple_of(req * span, span)
            at = 2 + 3 * req
            inside = jnp.where(
                col < 512,
                (col < meta[at]).astype(jnp.int32),
                jnp.where(
                    col < 768,
                    (col - 512 < meta[at + 1]).astype(jnp.int32),
                    (col - 768 < meta[at + 2]).astype(jnp.int32),
                ),
            )
            mine = (late.astype(jnp.int32) == req).astype(jnp.int32)
            return join(
                state,
                q_now,
                pk_all[pl.ds(start, span), :],
                pv_all[pl.ds(start, span), :],
                inside * mine > 0,
            )

        peak_all[...] = jnp.full((2 * tok, 1), MASKED, jnp.float32)
        total_all[...] = jnp.zeros((2 * tok, 1), jnp.float32)
        acc_all[...] = jnp.zeros((2 * tok, hd), jnp.float32)
        low = (first >= cut).astype(jnp.int32)
        high = (first + tok > cut).astype(jnp.int32)

        @pl.loop(low, high + 1)
        def _(req):
            peak, total, acc = prefix(req, (peak_all[...], total_all[...], acc_all[...]))
            peak_all[...] = peak
            total_all[...] = total
            acc_all[...] = acc

        bottom = jnp.where(late, cut, 0)

        for quarter in range(count // 2):

            @pl.when(step // 2 == quarter)
            def _(quarter=quarter):
                keys = 2 * tok * (quarter + 1)
                other = lax.broadcasted_iota(jnp.int32, (1, keys), 1)
                allowed = jnp.logical_and(other <= token, other >= bottom)
                peak, total, acc = join(
                    (peak_all[...], total_all[...], acc_all[...]),
                    q_now,
                    k_all[0:keys, :],
                    v_all[0:keys, :],
                    allowed,
                )
                done = (acc / total).astype(jnp.bfloat16)
                out[pl.ds(first, tok), 0:hd] = done[:tok]
                out[pl.ds(first, tok), hd : 2 * hd] = done[tok:]


def attend(meta, rows, weights, pieces, gains, cosine, sine):
    group = cosine.shape[0]
    hd = gains.shape[1]
    path_rows = 4 * pieces[0].shape[0]
    in_vmem = pl.BlockSpec(memory_space=pltpu.VMEM)
    return pl.pallas_call(
        attention_kernel,
        out_shape=jax.ShapeDtypeStruct((group, 2 * hd), jnp.bfloat16),
        in_specs=[pl.BlockSpec(memory_space=pltpu.SMEM)] + [in_vmem] * 17,
        out_specs=in_vmem,
        scratch_shapes=[
            pltpu.VMEM((group, rows[0].shape[1]), jnp.bfloat16),
            pltpu.VMEM((2, rows[0].shape[1], 2 * hd), jnp.bfloat16),
            pltpu.VMEM((2 * group, hd), jnp.bfloat16),
            pltpu.VMEM((group, hd), jnp.bfloat16),
            pltpu.VMEM((group, hd), jnp.bfloat16),
            pltpu.VMEM((path_rows, hd), jnp.bfloat16),
            pltpu.VMEM((path_rows, hd), jnp.bfloat16),
            pltpu.VMEM((256, 1), jnp.float32),
            pltpu.VMEM((256, 1), jnp.float32),
            pltpu.VMEM((256, hd), jnp.float32),
        ],
        compiler_params=pltpu.CompilerParams(vmem_limit_bytes=60 * 1024 * 1024),
        cost_estimate=pl.CostEstimate(
            flops=16 * group * group * hd, bytes_accessed=16 * group * 512, transcendentals=3 * group * group
        ),
        name="tree_attention",
    )(meta, *rows, *weights, *pieces, gains, cosine, sine)


def column_block(step, core):
    half = jnp.where(step < 2, core, 1 - core)
    return 2 * half + lax.rem(step, 2)


def project_kernel(
    place, attended, own, other, hidden, gain, out, normed, joined_own, joined_other, layer
):
    wide = attended.shape[2]
    step = pl.program_id(0)
    x, y, core = place[0], place[1], place[2]

    @pl.when(step == 0)
    def _():
        for at, shift in enumerate((0, 3, 1, 2)):
            for turn in range(2):
                block = attended[lax.rem(x + shift, 4) * 2 + lax.rem(y + turn, 2)]
                swapped = jnp.concatenate([block[:, wide // 2 :], block[:, : wide // 2]], axis=1)
                columns = slice((2 * at + turn) * wide, (2 * at + turn + 1) * wide)
                joined_own[:, columns] = jnp.where(core == 0, block, swapped)
                joined_other[:, columns] = jnp.where(core == 0, swapped, block)

    def add(joined, weight):
        added = jnp.dot(joined[...], weight[...], preferred_element_type=jnp.float32)
        done = (hidden[...].astype(jnp.float32) + added).astype(jnp.bfloat16)
        out[...] = done
        layer[column_block(step, core)] = done

    @pl.when(step < 2)
    def _():
        add(joined_own, own)

    @pl.when(step >= 2)
    def _():
        add(joined_other, other)

    @pl.when(step == layer.shape[0] - 1)
    def _():
        columns = layer.shape[2]
        parts = [layer[at].astype(jnp.float32) for at in range(layer.shape[0])]
        square = sum(jnp.sum(part * part, axis=1, keepdims=True) for part in parts)
        inverse = lax.rsqrt(square / (columns * len(parts)) + EPS)
        for at, part in enumerate(parts):
            where = slice(at * columns, (at + 1) * columns)
            normed[:, where] = (part * inverse * gain[:, where]).astype(jnp.bfloat16)


def project(place, attended, halves, hidden, gain):
    tok, dim = hidden.shape
    columns = dim // 4
    return pl.pallas_call(
        project_kernel,
        grid_spec=pltpu.PrefetchScalarGridSpec(
            num_scalar_prefetch=1,
            grid=(4,),
            in_specs=[
                pl.BlockSpec(attended.shape, lambda j, at: (0, 0, 0)),
                pl.BlockSpec((dim, columns), lambda j, at: (0, jnp.minimum(j, 1))),
                pl.BlockSpec((dim, columns), lambda j, at: (0, jnp.maximum(j - 2, 0))),
                pl.BlockSpec((tok, columns), lambda j, at: (0, column_block(j, at[2]))),
                pl.BlockSpec((1, dim), lambda j, at: (0, 0)),
            ],
            out_specs=(
                pl.BlockSpec((tok, columns), lambda j, at: (0, column_block(j, at[2]))),
                pl.BlockSpec((tok, dim), lambda j, at: (0, 0)),
            ),
            scratch_shapes=[
                pltpu.VMEM((tok, dim), jnp.bfloat16),
                pltpu.VMEM((tok, dim), jnp.bfloat16),
                pltpu.VMEM((4, tok, columns), jnp.bfloat16),
            ],
        ),
        out_shape=(
            jax.ShapeDtypeStruct(hidden.shape, hidden.dtype),
            jax.ShapeDtypeStruct(hidden.shape, hidden.dtype),
        ),
        compiler_params=pltpu.CompilerParams(vmem_limit_bytes=60 * 1024 * 1024),
        name="project",
    )(place, attended, *halves, hidden, gain)


def exchange(values):
    return lax.all_to_all(values, BOTH, split_axis=0, concat_axis=0, tiled=True)


def expert(rows, gate_up, down_weight):
    ff_width = down_weight.shape[0]
    both = jnp.dot(rows, gate_up, preferred_element_type=jnp.float32)
    active = (jax.nn.silu(both[:, :ff_width]) * both[:, ff_width:]).astype(jnp.bfloat16)
    return jnp.dot(active, down_weight, preferred_element_type=jnp.float32).astype(jnp.bfloat16)


def rest_kernel(rows, gate_up, down_weight, main_block, out):
    del main_block
    ff_width = down_weight.shape[0]
    spans = out.shape[0]
    wide = out.shape[2]
    chunks = down_weight.shape[1] // wide
    per = rows.shape[0] // spans
    both = jnp.dot(rows[...], gate_up[...], preferred_element_type=jnp.float32)
    gate = both[:, :ff_width]
    active = (gate / (1.0 + jnp.exp(-gate)) * both[:, ff_width:]).astype(jnp.bfloat16)
    served = jnp.dot(active, down_weight[...], preferred_element_type=jnp.float32)
    served = served.astype(jnp.bfloat16)
    batch = 16
    size = batch * per * chunks
    to = lax.broadcasted_iota(jnp.int32, (size, size), 0)
    source = lax.broadcasted_iota(jnp.int32, (size, size), 1)
    device = to // (per * chunks)
    chunk = to // per % chunks
    wanted = chunk * (batch * per) + device * per + to % per
    order = (source == wanted).astype(jnp.bfloat16)
    for first in range(0, spans, batch):
        stacked = jnp.concatenate(
            [
                served[first * per : (first + batch) * per, at * wide : (at + 1) * wide]
                for at in range(chunks)
            ],
            axis=0,
        )
        sorted_rows = jnp.dot(order, stacked, preferred_element_type=jnp.float32)
        out[first : first + batch] = sorted_rows.reshape(batch, per * chunks, wide).astype(
            jnp.bfloat16
        )


def expert_rest(rows, gate_up, down_weight, main_block):
    spans, height, wide = main_block.shape
    extra = rows.shape[0] // spans * down_weight.shape[1] // wide
    in_vmem = pl.BlockSpec(memory_space=pltpu.VMEM)
    return pl.pallas_call(
        rest_kernel,
        grid=(1,),
        out_shape=jax.ShapeDtypeStruct(main_block.shape, main_block.dtype),
        in_specs=[in_vmem, in_vmem, in_vmem, pl.BlockSpec(memory_space=pl.ANY)],
        out_specs=pl.BlockSpec((spans, extra, wide), lambda i: (0, height // extra - 1, 0)),
        input_output_aliases={3: 0},
        compiler_params=pltpu.CompilerParams(vmem_limit_bytes=60 * 1024 * 1024),
        name="expert_rest",
    )(rows, gate_up, down_weight, main_block)


def reorder(place, joined):
    x, y, core = place[0], place[1], place[2]
    wide = joined.shape[1] // 8
    mine, theirs = [], []
    for shift in (0, 3, 1, 2):
        for turn in range(2):
            block_no = lax.rem(x + shift, 4) * 2 + lax.rem(y + turn, 2)
            block = joined[:, pl.ds(pl.multiple_of(block_no * wide, wide), wide)]
            swapped = jnp.concatenate([block[:, wide // 2 :], block[:, : wide // 2]], axis=1)
            mine.append(jnp.where(core == 0, block, swapped))
            theirs.append(jnp.where(core == 0, swapped, block))
    return jnp.concatenate(mine, axis=1), jnp.concatenate(theirs, axis=1)


def finish_kernel(
    place,
    main_share,
    rest_share,
    main_rows,
    rest_rows,
    stream,
    next_own,
    next_other,
    norm_gain,
    head_gain,
    cosine,
    sine,
    out,
    next_rows,
    layer,
    joined,
):
    tok = stream.shape[0]
    count = main_share.shape[1]
    wide = main_rows.shape[2]
    hd = head_gain.shape[1]
    step = pl.program_id(0)

    def flat(values):
        values = values[...].astype(jnp.float32).reshape(count, wide)
        return values.astype(jnp.bfloat16)

    total = jnp.dot(main_share[...], flat(main_rows), preferred_element_type=jnp.float32)
    total += jnp.dot(rest_share[0], flat(rest_rows), preferred_element_type=jnp.float32)
    done = (stream[...].astype(jnp.float32) + total[:tok] + total[tok:]).astype(jnp.bfloat16)
    out[...] = done
    layer[step] = done

    @pl.when(step == layer.shape[0] - 1)
    def _():
        parts = [layer[at].astype(jnp.float32) for at in range(layer.shape[0])]
        square = sum(jnp.sum(part * part, axis=1, keepdims=True) for part in parts)
        inverse = lax.rsqrt(square / (wide * len(parts)) + EPS)
        for at, part in enumerate(parts):
            columns = slice(at * wide, (at + 1) * wide)
            normed = (part * inverse * norm_gain[:, columns]).astype(jnp.bfloat16)
            joined[:, columns] = normed
        mine, theirs = reorder(place, joined)
        raw_own = jnp.dot(mine, next_own[...], preferred_element_type=jnp.float32)
        raw_other = jnp.dot(theirs, next_other[...], preferred_element_type=jnp.float32)
        keys = jnp.where(place[2] == 0, raw_own, raw_other)
        values = jnp.where(place[2] == 0, raw_other, raw_own)
        half = keys.shape[1]
        for head in range(half // hd):
            columns = slice(head * hd, (head + 1) * hd)
            key = keys[:, columns]
            key = key * lax.rsqrt(jnp.mean(key * key, axis=-1, keepdims=True) + EPS)
            key = key * head_gain[...]
            key = key * cosine[...] + pltpu.roll(key, hd // 2, 1) * sine[...]
            next_rows[:, columns] = key.astype(jnp.bfloat16)
        next_rows[:, half:] = values.astype(jnp.bfloat16)


def finish(place, main_share, rest_share, returned, stream, halves, norm_gain, head_gain, turns):
    devices, height, wide = returned.shape
    tok, dim = stream.shape
    extra = halves[0].shape[1] - dim // 2
    chunks = dim // wide
    rows = height // (chunks + 1)
    shape = main_share.shape

    def fixed(values):
        return pl.BlockSpec(values.shape, lambda j, at: (0, 0))

    next_spec = pl.BlockSpec((dim, extra), lambda j, at: (0, dim // 2 // extra))
    return pl.pallas_call(
        finish_kernel,
        grid_spec=pltpu.PrefetchScalarGridSpec(
            num_scalar_prefetch=1,
            grid=(chunks,),
            in_specs=[
                fixed(main_share),
                pl.BlockSpec((1,) + shape, lambda j, at: (j, 0, 0)),
                pl.BlockSpec((devices, rows, wide), lambda j, at: (0, j, 0)),
                pl.BlockSpec((devices, rows, wide), lambda j, at: (0, chunks, 0)),
                pl.BlockSpec((tok, wide), lambda j, at: (0, j)),
                next_spec,
                next_spec,
                fixed(norm_gain),
                fixed(head_gain),
                fixed(turns[0]),
                fixed(turns[1]),
            ],
            out_specs=(
                pl.BlockSpec((tok, wide), lambda j, at: (0, j)),
                pl.BlockSpec((tok, 2 * extra), lambda j, at: (0, 0)),
            ),
            scratch_shapes=[
                pltpu.VMEM((chunks, tok, wide), jnp.bfloat16),
                pltpu.VMEM((tok, dim), jnp.bfloat16),
            ],
        ),
        out_shape=(
            jax.ShapeDtypeStruct(stream.shape, stream.dtype),
            jax.ShapeDtypeStruct((tok, 2 * extra), stream.dtype),
        ),
        compiler_params=pltpu.CompilerParams(vmem_limit_bytes=60 * 1024 * 1024),
        name="finish",
    )(
        place,
        main_share,
        rest_share,
        returned,
        returned,
        stream,
        *halves,
        norm_gain,
        head_gain,
        *turns,
    )


def per_device(
    hidden,
    norm_gains,
    head_gains,
    query_weight,
    kv_weight,
    out_weight,
    gate_up,
    down_weight,
    next_weight,
    expert_ids,
    route_weights,
    token_request,
    request_leaf,
    leaf_parent,
    mid_parent,
    root_length,
    mid_length,
    leaf_length,
    root_slot,
    mid_slot,
    leaf_slot,
    root_cache,
    mid_cache,
    leaf_cache,
):
    tok, dim = hidden.shape
    hd = head_gains.shape[1]
    group = token_request.shape[0]
    mp_size = lax.axis_size("mp")
    dp_size = lax.axis_size("dp")
    devices = dp_size * mp_size
    me = lax.axis_index("mp")
    own_rows = query_weight.shape[0]

    pair = token_request[0] + jnp.arange(2, dtype=jnp.int32)
    cut = jnp.sum((token_request == pair[0]).astype(jnp.int32))
    leaf_node = look_up(request_leaf, pair)
    mid_node = look_up(leaf_parent, leaf_node)
    root_node = look_up(mid_parent, mid_node)
    lengths = (
        look_up(root_length, root_node),
        look_up(mid_length, mid_node),
        look_up(leaf_length, leaf_node),
    )
    prefix_length = lengths[0] + lengths[1] + lengths[2]
    token = jnp.arange(group, dtype=jnp.int32)
    positions = token + jnp.where(token >= cut, prefix_length[1] - cut, prefix_length[0])
    frequency = THETA ** (-2.0 * jnp.arange(hd // 2, dtype=jnp.float32) / hd)
    angles = positions.astype(jnp.float32)[:, None] * frequency[None, :]
    cos_half = jnp.cos(angles)
    sin_half = jnp.sin(angles)
    cosine = jnp.concatenate([cos_half, cos_half], axis=1)
    sine = jnp.concatenate([-sin_half, sin_half], axis=1)

    normed = rms_norm(hidden, norm_gains[0]).astype(jnp.bfloat16)
    def shift(values, step):
        moves = [(j, j - j % 4 + (j % 4 + step) % 4) for j in range(mp_size)]
        return lax.ppermute(values, "mp", moves)

    across = lax.ppermute(normed, "mp", [(j, (j + 4) % mp_size) for j in range(mp_size)])
    left = shift(normed, 1)
    right = shift(normed, -1)
    packed = pack_weights(query_weight, kv_weight, out_weight, next_weight, mp_size)
    packed = lax.all_to_all(packed, "mp", split_axis=0, concat_axis=0, tiled=True)
    packed = packed.reshape(mp_size * own_rows, -1)
    late_width = dim + next_weight.shape[1]
    dp_at = lax.axis_index("dp")
    core = lax.rem(dp_at, 2)
    place = jnp.stack([dp_at // 4, lax.rem(dp_at // 2, 2), core]).astype(jnp.int32)

    def swap(values, bit):
        return lax.ppermute(values, "dp", [(j, j ^ bit) for j in range(dp_size)])

    def shift_x(values, step):
        moves = [(j, (j + 4 * step) % dp_size) for j in range(dp_size)]
        return lax.ppermute(values, "dp", moves)

    low, high = packed[:, : late_width // 2], packed[:, late_width // 2 : late_width]
    kept = jnp.where(core == 0, low, high)
    late = jnp.concatenate([kept, swap(jnp.where(core == 0, high, low), 1)], axis=0)
    late = jnp.concatenate([late, swap(late, 2)], axis=0)
    early = packed[:, late_width:].reshape(packed.shape[0], 2, 2 * hd).transpose(1, 0, 2)
    early = jnp.broadcast_to(early[None], (dp_size // 2,) + early.shape)
    early = early.reshape(dp_size, packed.shape[0], 2 * hd)
    early = lax.all_to_all(early, "dp", split_axis=0, concat_axis=0, tiled=True)
    early = early.reshape(dim, 2 * hd)
    sides = [left, right, shift(across, 1), shift(across, -1)]
    far = [shift(left, 1), shift(sides[3], -1)]
    tables = (
        token_request,
        request_leaf,
        leaf_parent,
        mid_parent,
        root_slot,
        mid_slot,
        leaf_slot,
    )
    path = pack_paths(tables, root_cache, mid_cache, leaf_cache, mp_size)
    path, sides, late, early = lax.optimization_barrier((path, sides, late, early))
    weights = (early, swap(early, 1))
    x_left = shift_x(late, 1)
    x_right = shift_x(late, -1)
    path = lax.all_to_all(path, "mp", split_axis=0, concat_axis=0, tiled=True)
    own_piece = jnp.sum(path.astype(jnp.float32), axis=0).astype(jnp.bfloat16)
    own_piece, far, x_left, x_right = lax.optimization_barrier((own_piece, far, x_left, x_right))
    middle = x_left.shape[0] // 2
    x_far = [shift_x(x_left[:middle], 1), shift_x(x_right[middle:], -1)]
    pieces = [own_piece] + [
        lax.ppermute(own_piece, "mp", [(j, j ^ s) for j in range(mp_size)]) for s in range(1, 4)
    ]
    rows = [normed, across] + sides + far
    meta = jnp.concatenate(
        [
            jnp.stack([me, cut]),
            jnp.stack(lengths, axis=1).reshape(-1),
            jnp.stack([lax.rem(lax.axis_index("dp"), 2)]),
        ]
    ).astype(jnp.int32)
    attended = attend(meta, rows, weights, pieces, head_gains, cosine, sine)
    attended, x_far = lax.optimization_barrier((attended, x_far))
    own_half = jnp.concatenate([late, x_left, x_right] + x_far, axis=0)
    halves = (own_half, swap(own_half, 1))
    attended = lax.all_to_all(
        attended.reshape(mp_size, tok, 2 * hd), "mp", split_axis=0, concat_axis=0, tiled=True
    )
    after_attention, moe_in = project(place, attended, halves, hidden, norm_gains[1:2])

    top_k = expert_ids.shape[1]
    capacity = max(2, 5 * tok * top_k // (4 * devices))
    names = expert_ids[:, :, None] == jnp.arange(devices, dtype=jnp.int32)[None, None, :]
    named = jnp.any(names, axis=1)
    route = jnp.sum(jnp.where(names, route_weights[:, :, None], 0.0), axis=1)
    before = jnp.tril(jnp.ones((tok, tok), jnp.bfloat16), -1)
    slot_no = jnp.dot(before, named.astype(jnp.bfloat16), preferred_element_type=jnp.float32)
    slot_no = jnp.where(named, slot_no.astype(jnp.int32), -1)

    def spread(first, last):
        count = jnp.arange(first, last, dtype=jnp.int32)
        taken = slot_no.T[:, None, :] == count[None, :, None]
        return taken.astype(jnp.bfloat16).reshape(devices * (last - first), tok)

    def gather_back(first, last):
        count = jnp.arange(first, last, dtype=jnp.int32)
        taken = slot_no[:, :, None] == count[None, None, :]
        share = jnp.where(taken, route[:, :, None], 0.0).reshape(tok, devices * (last - first))
        upper = lax.reduce_precision(share, 8, 7)
        return jnp.concatenate([upper, share - upper], axis=0).astype(jnp.bfloat16)

    def outbound(first, last, source):
        picked = jnp.dot(spread(first, last), source, preferred_element_type=jnp.float32)
        return picked.astype(jnp.bfloat16).reshape(devices, last - first, dim)

    main_in = exchange(outbound(0, MAIN, moe_in))
    main_in, rest_in = lax.optimization_barrier((main_in, outbound(MAIN, capacity, moe_in)))
    rest_in = exchange(rest_in)
    chunks = MAIN // (capacity - MAIN)
    wide = dim // chunks
    main_out = expert(main_in.reshape(-1, dim), gate_up[0], down_weight[0])
    main_out = main_out.reshape(devices, MAIN, chunks, wide).transpose(0, 2, 1, 3)
    main_out = main_out.reshape(devices, MAIN * chunks, wide)
    main_out = jnp.pad(main_out, ((0, 0), (0, MAIN), (0, 0)))
    main_out, rest_in = lax.optimization_barrier((main_out, rest_in))
    returned = exchange(expert_rest(rest_in.reshape(-1, dim), gate_up[0], down_weight[0], main_out))
    main_share = gather_back(0, MAIN)
    rest_share = gather_back(MAIN, capacity).reshape(1, 2 * tok, devices, 1, capacity - MAIN)
    which = jnp.eye(chunks, dtype=jnp.bfloat16).reshape(chunks, 1, 1, chunks, 1)
    rest_share = (rest_share * which).reshape(chunks, 2 * tok, devices * MAIN)
    my_cos = lax.dynamic_slice_in_dim(cosine, me * tok, tok)
    my_sin = lax.dynamic_slice_in_dim(sine, me * tok, tok)
    layer_out, next_rows = finish(
        place,
        main_share,
        rest_share,
        returned,
        after_attention,
        halves,
        norm_gains[2:3],
        head_gains[2:3],
        (my_cos, my_sin),
    )
    return (layer_out, next_rows)


def solution(mesh):
    both = P(BOTH, None)
    placed = (
        both,
        P(),
        P(),
        both,
        both,
        both,
        P(BOTH, None, None),
        P(BOTH, None, None),
        both,
        both,
        both,
        P("dp"),
        P(),
        P(),
        P(),
        P(),
        P(),
        P(),
        P(),
        P(),
        P(),
        P("mp", None, None),
        P("mp", None, None),
        P("mp", None, None),
    )
    return jax.shard_map(
        per_device,
        mesh=mesh,
        in_specs=placed,
        out_specs=(both, both),
        check_vma=False,
    )
```

```python
import jax
import jax.numpy as jnp
from jax import lax
from jax.experimental import pallas as pl
from jax.experimental.pallas import tpu as pltpu
from jax.sharding import PartitionSpec as P

EPS = 1e-06
THETA = 1000000.0
MASKED = -1e30
LOG2E = 1.4426950408889634
BOTH = ("dp", "mp")
MAIN = 8


def rms_norm(values, weight_row):
    values = values.astype(jnp.float32)
    return values * lax.rsqrt(jnp.mean(values * values, axis=-1, keepdims=True) + EPS) * weight_row


def look_up(lookup_table, indices):
    places = jnp.arange(lookup_table.shape[0], dtype=jnp.int32)
    return jnp.sum(jnp.where(indices[:, None] == places[None, :], lookup_table[None, :], 0), axis=1)


def pack_weights_kernel(query, kv, out_rows, next_rows, packed):
    count = packed.shape[0]
    dim = out_rows.shape[1]
    extra = next_rows.shape[1]
    wide = query.shape[1] // count
    hd = wide // 2
    heads = kv.shape[1] // 2 // hd
    base = dim + extra
    for dest in range(count):
        head = dest * heads // count
        for half in range(2):
            at = half * base // 2
            packed[dest, :, at : at + dim // 2] = out_rows[
                :, half * dim // 2 : (half + 1) * dim // 2
            ]
            packed[dest, :, at + dim // 2 : at + base // 2] = next_rows[
                :, half * extra // 2 : (half + 1) * extra // 2
            ]
        packed[dest, :, base : base + wide] = query[:, dest * wide : (dest + 1) * wide]
        for half in range(2):
            source = (half * heads + head) * hd
            target = base + wide + half * hd
            packed[dest, :, target : target + hd] = kv[:, source : source + hd]


def pack_weights(query, kv, out_rows, next_rows, count):
    rows = query.shape[0]
    width = out_rows.shape[1] + next_rows.shape[1] + 2 * (query.shape[1] // count)
    in_vmem = pl.BlockSpec(memory_space=pltpu.VMEM)
    return pl.pallas_call(
        pack_weights_kernel,
        out_shape=jax.ShapeDtypeStruct((count, rows, width), jnp.bfloat16),
        in_specs=[in_vmem] * 4,
        out_specs=in_vmem,
        name="pack_weights",
    )(query, kv, out_rows, next_rows)


def pack_paths_kernel(
    token_request,
    request_leaf,
    leaf_parent,
    mid_parent,
    root_slot,
    mid_slot,
    leaf_slot,
    root,
    mid,
    leaf,
    packed,
):
    count, part, wide = packed.shape
    hd = wide // 2
    heads = count // 4
    me = lax.axis_index("mp")
    for req in range(2):
        leaf_node = request_leaf[token_request[0] + req]
        mid_node = leaf_parent[leaf_node]
        slots = (root_slot[mid_parent[mid_node]], mid_slot[mid_node], leaf_slot[leaf_node])
        levels = []
        for slot, cache in zip(slots, (root, mid, leaf)):
            here = cache.shape[0]
            rows = jnp.zeros(cache.shape[1:], cache.dtype)
            for local in range(here):
                rows = jnp.where(slot == me * here + local, cache[local], rows)
            levels.append(rows)
        top = levels[0].shape[0] - part
        middle = levels[1].shape[0]
        for head in range(heads):
            for half in range(2):
                source = slice((half * heads + head) * hd, (half * heads + head + 1) * hd)
                target = slice(half * hd, (half + 1) * hd)
                place = 4 * head + 2 * req
                packed[place, :, target] = levels[0][:part, source]
                packed[place + 1, 0:top, target] = levels[0][part:, source]
                packed[place + 1, top : top + middle, target] = levels[1][:, source]
                packed[place + 1, top + middle :, target] = levels[2][:, source]


def pack_paths(tables, root, mid, leaf, count):
    wide = root.shape[2] // 2
    part = (root.shape[1] + mid.shape[1] + leaf.shape[1]) // 2
    in_vmem = pl.BlockSpec(memory_space=pltpu.VMEM)
    in_smem = pl.BlockSpec(memory_space=pltpu.SMEM)
    return pl.pallas_call(
        pack_paths_kernel,
        out_shape=jax.ShapeDtypeStruct((count, part, wide), jnp.bfloat16),
        in_specs=[in_smem] * len(tables) + [in_vmem] * 3,
        out_specs=in_vmem,
        compiler_params=pltpu.CompilerParams(vmem_limit_bytes=24 * 1024 * 1024),
        name="pack_paths",
    )(*tables, root, mid, leaf)


def attention_kernel(
    meta,
    own,
    across,
    own_left,
    own_right,
    across_left,
    across_right,
    own_far,
    across_far,
    weight_own,
    weight_other,
    piece_0,
    piece_1,
    piece_2,
    piece_3,
    gains,
    cosine,
    sine,
    out,
    rows_all,
    weights,
    q_all,
    k_all,
    v_all,
    pk_all,
    pv_all,
    peak_all,
    total_all,
    acc_all,
):
    pieces = (piece_0, piece_1, piece_2, piece_3)
    me = meta[0]
    cut = meta[1]
    tok, dim = own.shape
    count = rows_all.shape[0] // tok
    hd = gains.shape[1]
    span = pk_all.shape[0] // 2
    part = piece_0.shape[0]
    ring = lax.rem(me, 4)
    base = me - ring
    far_base = 4 - base

    def put(first, step, block):
        at = pl.multiple_of((first + lax.rem(ring + step, 4)) * tok, tok)
        rows_all[pl.ds(at, tok), :] = block[...]

    put(base, 0, own)
    put(far_base, 0, across)
    put(base, 3, own_left)
    put(base, 1, own_right)
    put(far_base, 3, across_left)
    put(far_base, 1, across_right)
    put(base, 2, own_far)
    put(far_base, 2, across_far)
    for step, piece in enumerate(pieces):
        place = pl.multiple_of((ring ^ step) * part, part)
        pk_all[pl.ds(place, part), :] = piece[:, :hd]
        pv_all[pl.ds(place, part), :] = piece[:, hd:]
    core = meta[8]
    weights[core] = weight_own[...]
    weights[1 - core] = weight_other[...]
    weight_q = weights[0]
    weight_kv = weights[1]

    def turn(raw, gain, cos_now, sin_now):
        scaled = raw * lax.rsqrt(jnp.mean(raw * raw, axis=-1, keepdims=True) + EPS) * gain
        return (scaled * cos_now + pltpu.roll(scaled, hd // 2, 1) * sin_now).astype(jnp.bfloat16)

    large = 4 * tok

    @pl.loop(0, count // 4)
    def _(step):
        at = pl.multiple_of(step * large, large)
        rows = rows_all[pl.ds(at, large), :]
        cos_now = cosine[pl.ds(at, large), :]
        sin_now = sine[pl.ds(at, large), :]
        raw = jnp.dot(rows, weight_q, preferred_element_type=jnp.float32)
        heads = [
            turn(raw[:, half * hd : (half + 1) * hd], gains[0:1, :], cos_now, sin_now)
            for half in range(2)
        ]
        for block in range(4):
            for half in range(2):
                q_at = pl.multiple_of(2 * at + (2 * block + half) * tok, tok)
                q_all[pl.ds(q_at, tok), :] = heads[half][block * tok : (block + 1) * tok]
        raw = jnp.dot(rows, weight_kv, preferred_element_type=jnp.float32)
        k_all[pl.ds(at, large), :] = turn(raw[:, :hd], gains[1:2, :], cos_now, sin_now)
        v_all[pl.ds(at, large), :] = raw[:, hd:].astype(jnp.bfloat16)

    scale = hd ** (-0.5) * LOG2E
    col = lax.broadcasted_iota(jnp.int32, (1, span), 1)
    row = lax.broadcasted_iota(jnp.int32, (2 * tok, 1), 0)
    row = jnp.where(row >= tok, row - tok, row)

    def score(q_now, keys):
        return lax.dot_general(
            q_now, keys, (((1,), (1,)), ((), ())), preferred_element_type=jnp.float32
        )

    def join(state, scores, values):
        peak, total, acc = state
        top = jnp.maximum(peak, jnp.max(scores, axis=1, keepdims=True))
        keep = jnp.exp2(peak - top)
        weights = jnp.exp2(scores - top)
        total = total * keep + jnp.sum(weights, axis=1, keepdims=True)
        acc = acc * keep + jnp.dot(
            weights.astype(jnp.bfloat16), values, preferred_element_type=jnp.float32
        )
        return top, total, acc

    @pl.loop(0, count)
    def _(step):
        first = pl.multiple_of(step * tok, tok)
        q_now = q_all[pl.ds(pl.multiple_of(2 * step * tok, 2 * tok), 2 * tok), :]
        token = row + first
        late = token >= cut

        def prefix(req, state):
            start = pl.multiple_of(req * span, span)
            at = 2 + 3 * req
            inside = jnp.where(
                col < 512,
                (col < meta[at]).astype(jnp.int32),
                jnp.where(
                    col < 768,
                    (col - 512 < meta[at + 1]).astype(jnp.int32),
                    (col - 768 < meta[at + 2]).astype(jnp.int32),
                ),
            )
            outside = jnp.where(inside > 0, 0.0, MASKED)
            foreign = jnp.where(late.astype(jnp.int32) == req, 0.0, MASKED)
            scores = scale * score(q_now, pk_all[pl.ds(start, span), :]) + outside + foreign
            return join(state, scores, pv_all[pl.ds(start, span), :])

        peak_all[...] = jnp.full((2 * tok, 1), MASKED, jnp.float32)
        total_all[...] = jnp.zeros((2 * tok, 1), jnp.float32)
        acc_all[...] = jnp.zeros((2 * tok, hd), jnp.float32)
        low = (first >= cut).astype(jnp.int32)
        high = (first + tok > cut).astype(jnp.int32)

        @pl.loop(low, high + 1)
        def _(req):
            peak, total, acc = prefix(req, (peak_all[...], total_all[...], acc_all[...]))
            peak_all[...] = peak
            total_all[...] = total
            acc_all[...] = acc

        bottom = jnp.where(late, cut, 0)

        for quarter in range(count // 2):

            @pl.when(step // 2 == quarter)
            def _(quarter=quarter):
                keys = 2 * tok * (quarter + 1)
                other = lax.broadcasted_iota(jnp.int32, (1, keys), 1)
                allowed = jnp.logical_and(other <= token, other >= bottom)
                scores = scale * score(q_now, k_all[0:keys, :])
                peak, total, acc = join(
                    (peak_all[...], total_all[...], acc_all[...]),
                    jnp.where(allowed, scores, MASKED),
                    v_all[0:keys, :],
                )
                done = (acc / total).astype(jnp.bfloat16)
                out[pl.ds(first, tok), 0:hd] = done[:tok]
                out[pl.ds(first, tok), hd : 2 * hd] = done[tok:]


def attend(meta, rows, weights, pieces, gains, cosine, sine):
    group = cosine.shape[0]
    hd = gains.shape[1]
    path_rows = 4 * pieces[0].shape[0]
    in_vmem = pl.BlockSpec(memory_space=pltpu.VMEM)
    return pl.pallas_call(
        attention_kernel,
        out_shape=jax.ShapeDtypeStruct((group, 2 * hd), jnp.bfloat16),
        in_specs=[pl.BlockSpec(memory_space=pltpu.SMEM)] + [in_vmem] * 17,
        out_specs=in_vmem,
        scratch_shapes=[
            pltpu.VMEM((group, rows[0].shape[1]), jnp.bfloat16),
            pltpu.VMEM((2, rows[0].shape[1], 2 * hd), jnp.bfloat16),
            pltpu.VMEM((2 * group, hd), jnp.bfloat16),
            pltpu.VMEM((group, hd), jnp.bfloat16),
            pltpu.VMEM((group, hd), jnp.bfloat16),
            pltpu.VMEM((path_rows, hd), jnp.bfloat16),
            pltpu.VMEM((path_rows, hd), jnp.bfloat16),
            pltpu.VMEM((256, 1), jnp.float32),
            pltpu.VMEM((256, 1), jnp.float32),
            pltpu.VMEM((256, hd), jnp.float32),
        ],
        compiler_params=pltpu.CompilerParams(vmem_limit_bytes=60 * 1024 * 1024),
        cost_estimate=pl.CostEstimate(
            flops=16 * group * group * hd, bytes_accessed=16 * group * 512, transcendentals=3 * group * group
        ),
        name="tree_attention",
    )(meta, *rows, *weights, *pieces, gains, cosine, sine)


def column_block(step, core):
    half = jnp.where(step < 2, core, 1 - core)
    return 2 * half + lax.rem(step, 2)


def project_kernel(
    place, attended, own, other, hidden, gain, out, normed, joined_own, joined_other, layer
):
    wide = attended.shape[2]
    step = pl.program_id(0)
    x, y, core = place[0], place[1], place[2]

    @pl.when(step == 0)
    def _():
        for at, shift in enumerate((0, 3, 1, 2)):
            for turn in range(2):
                block = attended[lax.rem(x + shift, 4) * 2 + lax.rem(y + turn, 2)]
                swapped = jnp.concatenate([block[:, wide // 2 :], block[:, : wide // 2]], axis=1)
                columns = slice((2 * at + turn) * wide, (2 * at + turn + 1) * wide)
                joined_own[:, columns] = jnp.where(core == 0, block, swapped)
                joined_other[:, columns] = jnp.where(core == 0, swapped, block)

    def add(joined, weight):
        added = jnp.dot(joined[...], weight[...], preferred_element_type=jnp.float32)
        done = (hidden[...].astype(jnp.float32) + added).astype(jnp.bfloat16)
        out[...] = done
        layer[column_block(step, core)] = done

    @pl.when(step < 2)
    def _():
        add(joined_own, own)

    @pl.when(step >= 2)
    def _():
        add(joined_other, other)

    @pl.when(step == layer.shape[0] - 1)
    def _():
        columns = layer.shape[2]
        parts = [layer[at].astype(jnp.float32) for at in range(layer.shape[0])]
        square = sum(jnp.sum(part * part, axis=1, keepdims=True) for part in parts)
        inverse = lax.rsqrt(square / (columns * len(parts)) + EPS)
        for at, part in enumerate(parts):
            where = slice(at * columns, (at + 1) * columns)
            normed[:, where] = (part * inverse * gain[:, where]).astype(jnp.bfloat16)


def project(place, attended, halves, hidden, gain):
    tok, dim = hidden.shape
    columns = dim // 4
    return pl.pallas_call(
        project_kernel,
        grid_spec=pltpu.PrefetchScalarGridSpec(
            num_scalar_prefetch=1,
            grid=(4,),
            in_specs=[
                pl.BlockSpec(attended.shape, lambda j, at: (0, 0, 0)),
                pl.BlockSpec((dim, columns), lambda j, at: (0, jnp.minimum(j, 1))),
                pl.BlockSpec((dim, columns), lambda j, at: (0, jnp.maximum(j - 2, 0))),
                pl.BlockSpec((tok, columns), lambda j, at: (0, column_block(j, at[2]))),
                pl.BlockSpec((1, dim), lambda j, at: (0, 0)),
            ],
            out_specs=(
                pl.BlockSpec((tok, columns), lambda j, at: (0, column_block(j, at[2]))),
                pl.BlockSpec((tok, dim), lambda j, at: (0, 0)),
            ),
            scratch_shapes=[
                pltpu.VMEM((tok, dim), jnp.bfloat16),
                pltpu.VMEM((tok, dim), jnp.bfloat16),
                pltpu.VMEM((4, tok, columns), jnp.bfloat16),
            ],
        ),
        out_shape=(
            jax.ShapeDtypeStruct(hidden.shape, hidden.dtype),
            jax.ShapeDtypeStruct(hidden.shape, hidden.dtype),
        ),
        compiler_params=pltpu.CompilerParams(vmem_limit_bytes=60 * 1024 * 1024),
        name="project",
    )(place, attended, *halves, hidden, gain)


def exchange(values):
    return lax.all_to_all(values, BOTH, split_axis=0, concat_axis=0, tiled=True)


def expert(rows, gate_up, down_weight):
    ff_width = down_weight.shape[0]
    both = jnp.dot(rows, gate_up, preferred_element_type=jnp.float32)
    active = (jax.nn.silu(both[:, :ff_width]) * both[:, ff_width:]).astype(jnp.bfloat16)
    return jnp.dot(active, down_weight, preferred_element_type=jnp.float32).astype(jnp.bfloat16)


def rest_kernel(rows, gate_up, down_weight, main_block, out):
    del main_block
    ff_width = down_weight.shape[0]
    spans = out.shape[0]
    wide = out.shape[2]
    chunks = down_weight.shape[1] // wide
    per = rows.shape[0] // spans
    both = jnp.dot(rows[...], gate_up[...], preferred_element_type=jnp.float32)
    gate = both[:, :ff_width]
    active = (gate / (1.0 + jnp.exp(-gate)) * both[:, ff_width:]).astype(jnp.bfloat16)
    served = jnp.dot(active, down_weight[...], preferred_element_type=jnp.float32)
    served = served.astype(jnp.bfloat16)
    batch = 16
    size = batch * per * chunks
    to = lax.broadcasted_iota(jnp.int32, (size, size), 0)
    source = lax.broadcasted_iota(jnp.int32, (size, size), 1)
    device = to // (per * chunks)
    chunk = to // per % chunks
    wanted = chunk * (batch * per) + device * per + to % per
    order = (source == wanted).astype(jnp.bfloat16)
    for first in range(0, spans, batch):
        stacked = jnp.concatenate(
            [
                served[first * per : (first + batch) * per, at * wide : (at + 1) * wide]
                for at in range(chunks)
            ],
            axis=0,
        )
        sorted_rows = jnp.dot(order, stacked, preferred_element_type=jnp.float32)
        out[first : first + batch] = sorted_rows.reshape(batch, per * chunks, wide).astype(
            jnp.bfloat16
        )


def expert_rest(rows, gate_up, down_weight, main_block):
    spans, height, wide = main_block.shape
    extra = rows.shape[0] // spans * down_weight.shape[1] // wide
    in_vmem = pl.BlockSpec(memory_space=pltpu.VMEM)
    return pl.pallas_call(
        rest_kernel,
        grid=(1,),
        out_shape=jax.ShapeDtypeStruct(main_block.shape, main_block.dtype),
        in_specs=[in_vmem, in_vmem, in_vmem, pl.BlockSpec(memory_space=pl.ANY)],
        out_specs=pl.BlockSpec((spans, extra, wide), lambda i: (0, height // extra - 1, 0)),
        input_output_aliases={3: 0},
        compiler_params=pltpu.CompilerParams(vmem_limit_bytes=60 * 1024 * 1024),
        name="expert_rest",
    )(rows, gate_up, down_weight, main_block)


def reorder(place, joined):
    x, y, core = place[0], place[1], place[2]
    wide = joined.shape[1] // 8
    mine, theirs = [], []
    for shift in (0, 3, 1, 2):
        for turn in range(2):
            block_no = lax.rem(x + shift, 4) * 2 + lax.rem(y + turn, 2)
            block = joined[:, pl.ds(pl.multiple_of(block_no * wide, wide), wide)]
            swapped = jnp.concatenate([block[:, wide // 2 :], block[:, : wide // 2]], axis=1)
            mine.append(jnp.where(core == 0, block, swapped))
            theirs.append(jnp.where(core == 0, swapped, block))
    return jnp.concatenate(mine, axis=1), jnp.concatenate(theirs, axis=1)


def finish_kernel(
    place,
    main_share,
    rest_share,
    main_rows,
    rest_rows,
    stream,
    next_own,
    next_other,
    norm_gain,
    head_gain,
    cosine,
    sine,
    out,
    next_rows,
    layer,
    joined,
):
    tok = stream.shape[0]
    count = main_share.shape[1]
    wide = main_rows.shape[2]
    hd = head_gain.shape[1]
    step = pl.program_id(0)

    def flat(values):
        values = values[...].astype(jnp.float32).reshape(count, wide)
        return values.astype(jnp.bfloat16)

    total = jnp.dot(main_share[...], flat(main_rows), preferred_element_type=jnp.float32)
    total += jnp.dot(rest_share[0], flat(rest_rows), preferred_element_type=jnp.float32)
    done = (stream[...].astype(jnp.float32) + total[:tok] + total[tok:]).astype(jnp.bfloat16)
    out[...] = done
    layer[step] = done

    @pl.when(step == layer.shape[0] - 1)
    def _():
        parts = [layer[at].astype(jnp.float32) for at in range(layer.shape[0])]
        square = sum(jnp.sum(part * part, axis=1, keepdims=True) for part in parts)
        inverse = lax.rsqrt(square / (wide * len(parts)) + EPS)
        for at, part in enumerate(parts):
            columns = slice(at * wide, (at + 1) * wide)
            normed = (part * inverse * norm_gain[:, columns]).astype(jnp.bfloat16)
            joined[:, columns] = normed
        mine, theirs = reorder(place, joined)
        raw_own = jnp.dot(mine, next_own[...], preferred_element_type=jnp.float32)
        raw_other = jnp.dot(theirs, next_other[...], preferred_element_type=jnp.float32)
        keys = jnp.where(place[2] == 0, raw_own, raw_other)
        values = jnp.where(place[2] == 0, raw_other, raw_own)
        half = keys.shape[1]
        for head in range(half // hd):
            columns = slice(head * hd, (head + 1) * hd)
            key = keys[:, columns]
            key = key * lax.rsqrt(jnp.mean(key * key, axis=-1, keepdims=True) + EPS)
            key = key * head_gain[...]
            key = key * cosine[...] + pltpu.roll(key, hd // 2, 1) * sine[...]
            next_rows[:, columns] = key.astype(jnp.bfloat16)
        next_rows[:, half:] = values.astype(jnp.bfloat16)


def finish(place, main_share, rest_share, returned, stream, halves, norm_gain, head_gain, turns):
    devices, height, wide = returned.shape
    tok, dim = stream.shape
    extra = halves[0].shape[1] - dim // 2
    chunks = dim // wide
    rows = height // (chunks + 1)
    shape = main_share.shape

    def fixed(values):
        return pl.BlockSpec(values.shape, lambda j, at: (0, 0))

    next_spec = pl.BlockSpec((dim, extra), lambda j, at: (0, dim // 2 // extra))
    return pl.pallas_call(
        finish_kernel,
        grid_spec=pltpu.PrefetchScalarGridSpec(
            num_scalar_prefetch=1,
            grid=(chunks,),
            in_specs=[
                fixed(main_share),
                pl.BlockSpec((1,) + shape, lambda j, at: (j, 0, 0)),
                pl.BlockSpec((devices, rows, wide), lambda j, at: (0, j, 0)),
                pl.BlockSpec((devices, rows, wide), lambda j, at: (0, chunks, 0)),
                pl.BlockSpec((tok, wide), lambda j, at: (0, j)),
                next_spec,
                next_spec,
                fixed(norm_gain),
                fixed(head_gain),
                fixed(turns[0]),
                fixed(turns[1]),
            ],
            out_specs=(
                pl.BlockSpec((tok, wide), lambda j, at: (0, j)),
                pl.BlockSpec((tok, 2 * extra), lambda j, at: (0, 0)),
            ),
            scratch_shapes=[
                pltpu.VMEM((chunks, tok, wide), jnp.bfloat16),
                pltpu.VMEM((tok, dim), jnp.bfloat16),
            ],
        ),
        out_shape=(
            jax.ShapeDtypeStruct(stream.shape, stream.dtype),
            jax.ShapeDtypeStruct((tok, 2 * extra), stream.dtype),
        ),
        compiler_params=pltpu.CompilerParams(vmem_limit_bytes=60 * 1024 * 1024),
        name="finish",
    )(
        place,
        main_share,
        rest_share,
        returned,
        returned,
        stream,
        *halves,
        norm_gain,
        head_gain,
        *turns,
    )


def per_device(
    hidden,
    norm_gains,
    head_gains,
    query_weight,
    kv_weight,
    out_weight,
    gate_up,
    down_weight,
    next_weight,
    expert_ids,
    route_weights,
    token_request,
    request_leaf,
    leaf_parent,
    mid_parent,
    root_length,
    mid_length,
    leaf_length,
    root_slot,
    mid_slot,
    leaf_slot,
    root_cache,
    mid_cache,
    leaf_cache,
):
    tok, dim = hidden.shape
    hd = head_gains.shape[1]
    group = token_request.shape[0]
    mp_size = lax.axis_size("mp")
    dp_size = lax.axis_size("dp")
    devices = dp_size * mp_size
    me = lax.axis_index("mp")
    own_rows = query_weight.shape[0]

    pair = token_request[0] + jnp.arange(2, dtype=jnp.int32)
    cut = jnp.sum((token_request == pair[0]).astype(jnp.int32))
    leaf_node = look_up(request_leaf, pair)
    mid_node = look_up(leaf_parent, leaf_node)
    root_node = look_up(mid_parent, mid_node)
    lengths = (
        look_up(root_length, root_node),
        look_up(mid_length, mid_node),
        look_up(leaf_length, leaf_node),
    )
    prefix_length = lengths[0] + lengths[1] + lengths[2]
    token = jnp.arange(group, dtype=jnp.int32)
    positions = token + jnp.where(token >= cut, prefix_length[1] - cut, prefix_length[0])
    frequency = THETA ** (-2.0 * jnp.arange(hd // 2, dtype=jnp.float32) / hd)
    angles = positions.astype(jnp.float32)[:, None] * frequency[None, :]
    cos_half = jnp.cos(angles)
    sin_half = jnp.sin(angles)
    cosine = jnp.concatenate([cos_half, cos_half], axis=1)
    sine = jnp.concatenate([-sin_half, sin_half], axis=1)

    normed = rms_norm(hidden, norm_gains[0]).astype(jnp.bfloat16)
    def shift(values, step):
        moves = [(j, j - j % 4 + (j % 4 + step) % 4) for j in range(mp_size)]
        return lax.ppermute(values, "mp", moves)

    across = lax.ppermute(normed, "mp", [(j, (j + 4) % mp_size) for j in range(mp_size)])
    left = shift(normed, 1)
    right = shift(normed, -1)
    packed = pack_weights(query_weight, kv_weight, out_weight, next_weight, mp_size)
    packed = lax.all_to_all(packed, "mp", split_axis=0, concat_axis=0, tiled=True)
    packed, across, left, right = lax.optimization_barrier((packed, across, left, right))
    packed = packed.reshape(mp_size * own_rows, -1)
    late_width = dim + next_weight.shape[1]
    dp_at = lax.axis_index("dp")
    core = lax.rem(dp_at, 2)
    place = jnp.stack([dp_at // 4, lax.rem(dp_at // 2, 2), core]).astype(jnp.int32)

    def swap(values, bit):
        return lax.ppermute(values, "dp", [(j, j ^ bit) for j in range(dp_size)])

    def shift_x(values, step):
        moves = [(j, (j + 4 * step) % dp_size) for j in range(dp_size)]
        return lax.ppermute(values, "dp", moves)

    low, high = packed[:, : late_width // 2], packed[:, late_width // 2 : late_width]
    kept = jnp.where(core == 0, low, high)
    late = jnp.concatenate([kept, swap(jnp.where(core == 0, high, low), 1)], axis=0)
    late = jnp.concatenate([late, swap(late, 2)], axis=0)
    early = packed[:, late_width:].reshape(packed.shape[0], 2, 2 * hd).transpose(1, 0, 2)
    early = jnp.broadcast_to(early[None], (dp_size // 2,) + early.shape)
    early = early.reshape(dp_size, packed.shape[0], 2 * hd)
    early = lax.all_to_all(early, "dp", split_axis=0, concat_axis=0, tiled=True)
    early = early.reshape(dim, 2 * hd)
    sides = [left, right, shift(across, 1), shift(across, -1)]
    own_far = shift(left, 1)
    tables = (
        token_request,
        request_leaf,
        leaf_parent,
        mid_parent,
        root_slot,
        mid_slot,
        leaf_slot,
    )
    path = pack_paths(tables, root_cache, mid_cache, leaf_cache, mp_size)
    path, sides, own_far, late, early = lax.optimization_barrier(
        (path, sides, own_far, late, early)
    )
    far = [own_far, shift(sides[3], -1)]
    weights = (early, swap(early, 1))
    x_left = shift_x(late, 1)
    x_right = shift_x(late, -1)
    path = lax.all_to_all(path, "mp", split_axis=0, concat_axis=0, tiled=True)
    own_piece = jnp.sum(path.astype(jnp.float32), axis=0).astype(jnp.bfloat16)
    own_piece, far = lax.optimization_barrier((own_piece, far))
    pieces = [own_piece] + [
        lax.ppermute(own_piece, "mp", [(j, j ^ s) for j in range(mp_size)]) for s in range(1, 4)
    ]
    pieces, x_left, x_right = lax.optimization_barrier((pieces, x_left, x_right))
    middle = x_left.shape[0] // 2
    x_far = [shift_x(x_left[:middle], 1), shift_x(x_right[middle:], -1)]
    rows = [normed, across] + sides + far
    meta = jnp.concatenate(
        [
            jnp.stack([me, cut]),
            jnp.stack(lengths, axis=1).reshape(-1),
            jnp.stack([lax.rem(lax.axis_index("dp"), 2)]),
        ]
    ).astype(jnp.int32)
    attended = attend(meta, rows, weights, pieces, head_gains, cosine, sine)
    attended, late, x_left, x_right, x_far = lax.optimization_barrier(
        (attended, late, x_left, x_right, x_far)
    )
    own_half = jnp.concatenate([late, x_left, x_right] + x_far, axis=0)
    halves = (own_half, swap(own_half, 1))
    attended = lax.all_to_all(
        attended.reshape(mp_size, tok, 2 * hd), "mp", split_axis=0, concat_axis=0, tiled=True
    )
    after_attention, moe_in = project(place, attended, halves, hidden, norm_gains[1:2])

    top_k = expert_ids.shape[1]
    capacity = max(2, 5 * tok * top_k // (4 * devices))
    names = expert_ids[:, :, None] == jnp.arange(devices, dtype=jnp.int32)[None, None, :]
    named = jnp.any(names, axis=1)
    route = jnp.sum(jnp.where(names, route_weights[:, :, None], 0.0), axis=1)
    before = jnp.tril(jnp.ones((tok, tok), jnp.bfloat16), -1)
    slot_no = jnp.dot(before, named.astype(jnp.bfloat16), preferred_element_type=jnp.float32)
    slot_no = jnp.where(named, slot_no.astype(jnp.int32), -1)

    def spread(first, last):
        count = jnp.arange(first, last, dtype=jnp.int32)
        taken = slot_no.T[:, None, :] == count[None, :, None]
        return taken.astype(jnp.bfloat16).reshape(devices * (last - first), tok)

    def gather_back(first, last):
        count = jnp.arange(first, last, dtype=jnp.int32)
        taken = slot_no[:, :, None] == count[None, None, :]
        share = jnp.where(taken, route[:, :, None], 0.0).reshape(tok, devices * (last - first))
        upper = lax.reduce_precision(share, 8, 7)
        return jnp.concatenate([upper, share - upper], axis=0).astype(jnp.bfloat16)

    def outbound(first, last, source):
        picked = jnp.dot(spread(first, last), source, preferred_element_type=jnp.float32)
        return picked.astype(jnp.bfloat16).reshape(devices, last - first, dim)

    main_in = exchange(outbound(0, MAIN, moe_in))
    main_in, rest_in = lax.optimization_barrier((main_in, outbound(MAIN, capacity, moe_in)))
    rest_in = exchange(rest_in)
    chunks = MAIN // (capacity - MAIN)
    wide = dim // chunks
    main_out = expert(main_in.reshape(-1, dim), gate_up[0], down_weight[0])
    main_out = main_out.reshape(devices, MAIN, chunks, wide).transpose(0, 2, 1, 3)
    main_out = main_out.reshape(devices, MAIN * chunks, wide)
    main_out = jnp.pad(main_out, ((0, 0), (0, MAIN), (0, 0)))
    main_out, rest_in = lax.optimization_barrier((main_out, rest_in))
    returned = exchange(expert_rest(rest_in.reshape(-1, dim), gate_up[0], down_weight[0], main_out))
    main_share = gather_back(0, MAIN)
    rest_share = gather_back(MAIN, capacity).reshape(1, 2 * tok, devices, 1, capacity - MAIN)
    which = jnp.eye(chunks, dtype=jnp.bfloat16).reshape(chunks, 1, 1, chunks, 1)
    rest_share = (rest_share * which).reshape(chunks, 2 * tok, devices * MAIN)
    my_cos = lax.dynamic_slice_in_dim(cosine, me * tok, tok)
    my_sin = lax.dynamic_slice_in_dim(sine, me * tok, tok)
    layer_out, next_rows = finish(
        place,
        main_share,
        rest_share,
        returned,
        after_attention,
        halves,
        norm_gains[2:3],
        head_gains[2:3],
        (my_cos, my_sin),
    )
    return (layer_out, next_rows)


def solution(mesh):
    both = P(BOTH, None)
    placed = (
        both,
        P(),
        P(),
        both,
        both,
        both,
        P(BOTH, None, None),
        P(BOTH, None, None),
        both,
        both,
        both,
        P("dp"),
        P(),
        P(),
        P(),
        P(),
        P(),
        P(),
        P(),
        P(),
        P(),
        P("mp", None, None),
        P("mp", None, None),
        P("mp", None, None),
    )
    return jax.shard_map(
        per_device,
        mesh=mesh,
        in_specs=placed,
        out_specs=(both, both),
        check_vma=False,
    )
```

```python
import jax
import jax.numpy as jnp
from jax import lax
from jax.experimental import pallas as pl
from jax.experimental.pallas import tpu as pltpu
from jax.sharding import PartitionSpec as P

EPS = 1e-06
THETA = 1000000.0
MASKED = -1e30
LOG2E = 1.4426950408889634
BOTH = ("dp", "mp")
MAIN = 8


def rms_norm(values, weight_row):
    values = values.astype(jnp.float32)
    return values * lax.rsqrt(jnp.mean(values * values, axis=-1, keepdims=True) + EPS) * weight_row


def look_up(lookup_table, indices):
    places = jnp.arange(lookup_table.shape[0], dtype=jnp.int32)
    return jnp.sum(jnp.where(indices[:, None] == places[None, :], lookup_table[None, :], 0), axis=1)


def pack_weights_kernel(query, kv, out_rows, next_rows, packed):
    count = packed.shape[0]
    dim = out_rows.shape[1]
    extra = next_rows.shape[1]
    wide = query.shape[1] // count
    hd = wide // 2
    heads = kv.shape[1] // 2 // hd
    base = dim + extra
    for dest in range(count):
        head = dest * heads // count
        for half in range(2):
            at = half * base // 2
            packed[dest, :, at : at + dim // 2] = out_rows[
                :, half * dim // 2 : (half + 1) * dim // 2
            ]
            packed[dest, :, at + dim // 2 : at + base // 2] = next_rows[
                :, half * extra // 2 : (half + 1) * extra // 2
            ]
        packed[dest, :, base : base + wide] = query[:, dest * wide : (dest + 1) * wide]
        for half in range(2):
            source = (half * heads + head) * hd
            target = base + wide + half * hd
            packed[dest, :, target : target + hd] = kv[:, source : source + hd]


def pack_weights(query, kv, out_rows, next_rows, count):
    rows = query.shape[0]
    width = out_rows.shape[1] + next_rows.shape[1] + 2 * (query.shape[1] // count)
    in_vmem = pl.BlockSpec(memory_space=pltpu.VMEM)
    return pl.pallas_call(
        pack_weights_kernel,
        out_shape=jax.ShapeDtypeStruct((count, rows, width), jnp.bfloat16),
        in_specs=[in_vmem] * 4,
        out_specs=in_vmem,
        name="pack_weights",
    )(query, kv, out_rows, next_rows)


def pack_paths_kernel(
    token_request,
    request_leaf,
    leaf_parent,
    mid_parent,
    root_slot,
    mid_slot,
    leaf_slot,
    root,
    mid,
    leaf,
    packed,
):
    count, part, wide = packed.shape
    hd = wide // 2
    heads = count // 4
    me = lax.axis_index("mp")
    for req in range(2):
        leaf_node = request_leaf[token_request[0] + req]
        mid_node = leaf_parent[leaf_node]
        slots = (root_slot[mid_parent[mid_node]], mid_slot[mid_node], leaf_slot[leaf_node])
        levels = []
        for slot, cache in zip(slots, (root, mid, leaf)):
            here = cache.shape[0]
            rows = jnp.zeros(cache.shape[1:], cache.dtype)
            for local in range(here):
                rows = jnp.where(slot == me * here + local, cache[local], rows)
            levels.append(rows)
        top = levels[0].shape[0] - part
        middle = levels[1].shape[0]
        for head in range(heads):
            for half in range(2):
                source = slice((half * heads + head) * hd, (half * heads + head + 1) * hd)
                target = slice(half * hd, (half + 1) * hd)
                place = 4 * head + 2 * req
                packed[place, :, target] = levels[0][:part, source]
                packed[place + 1, 0:top, target] = levels[0][part:, source]
                packed[place + 1, top : top + middle, target] = levels[1][:, source]
                packed[place + 1, top + middle :, target] = levels[2][:, source]


def pack_paths(tables, root, mid, leaf, count):
    wide = root.shape[2] // 2
    part = (root.shape[1] + mid.shape[1] + leaf.shape[1]) // 2
    in_vmem = pl.BlockSpec(memory_space=pltpu.VMEM)
    in_smem = pl.BlockSpec(memory_space=pltpu.SMEM)
    return pl.pallas_call(
        pack_paths_kernel,
        out_shape=jax.ShapeDtypeStruct((count, part, wide), jnp.bfloat16),
        in_specs=[in_smem] * len(tables) + [in_vmem] * 3,
        out_specs=in_vmem,
        compiler_params=pltpu.CompilerParams(vmem_limit_bytes=24 * 1024 * 1024),
        name="pack_paths",
    )(*tables, root, mid, leaf)


def attention_kernel(
    meta,
    own,
    across,
    own_left,
    own_right,
    across_left,
    across_right,
    own_far,
    across_far,
    weight_own,
    weight_other,
    piece_0,
    piece_1,
    piece_2,
    piece_3,
    gains,
    cosine,
    sine,
    out,
    rows_all,
    weights,
    q_all,
    k_all,
    v_all,
    pk_all,
    pv_all,
    peak_all,
    total_all,
    acc_all,
):
    pieces = (piece_0, piece_1, piece_2, piece_3)
    me = meta[0]
    cut = meta[1]
    tok, dim = own.shape
    count = rows_all.shape[0] // tok
    hd = gains.shape[1]
    span = pk_all.shape[0] // 2
    part = piece_0.shape[0]
    ring = lax.rem(me, 4)
    base = me - ring
    far_base = 4 - base

    def put(first, step, block):
        at = pl.multiple_of((first + lax.rem(ring + step, 4)) * tok, tok)
        rows_all[pl.ds(at, tok), :] = block[...]

    put(base, 0, own)
    put(far_base, 0, across)
    put(base, 3, own_left)
    put(base, 1, own_right)
    put(far_base, 3, across_left)
    put(far_base, 1, across_right)
    put(base, 2, own_far)
    put(far_base, 2, across_far)
    for step, piece in enumerate(pieces):
        place = pl.multiple_of((ring ^ step) * part, part)
        pk_all[pl.ds(place, part), :] = piece[:, :hd]
        pv_all[pl.ds(place, part), :] = piece[:, hd:]
    core = meta[8]
    weights[core] = weight_own[...]
    weights[1 - core] = weight_other[...]
    weight_q = weights[0]
    weight_kv = weights[1]

    def turn(raw, gain, cos_now, sin_now):
        scaled = raw * lax.rsqrt(jnp.mean(raw * raw, axis=-1, keepdims=True) + EPS) * gain
        return (scaled * cos_now + pltpu.roll(scaled, hd // 2, 1) * sin_now).astype(jnp.bfloat16)

    large = 4 * tok

    @pl.loop(0, count // 4)
    def _(step):
        at = pl.multiple_of(step * large, large)
        rows = rows_all[pl.ds(at, large), :]
        cos_now = cosine[pl.ds(at, large), :]
        sin_now = sine[pl.ds(at, large), :]
        raw = jnp.dot(rows, weight_q, preferred_element_type=jnp.float32)
        heads = [
            turn(raw[:, half * hd : (half + 1) * hd], gains[0:1, :], cos_now, sin_now)
            for half in range(2)
        ]
        for block in range(4):
            for half in range(2):
                q_at = pl.multiple_of(2 * at + (2 * block + half) * tok, tok)
                q_all[pl.ds(q_at, tok), :] = heads[half][block * tok : (block + 1) * tok]
        raw = jnp.dot(rows, weight_kv, preferred_element_type=jnp.float32)
        k_all[pl.ds(at, large), :] = turn(raw[:, :hd], gains[1:2, :], cos_now, sin_now)
        v_all[pl.ds(at, large), :] = raw[:, hd:].astype(jnp.bfloat16)

    scale = hd ** (-0.5) * LOG2E
    col = lax.broadcasted_iota(jnp.int32, (1, span), 1)
    row = lax.broadcasted_iota(jnp.int32, (2 * tok, 1), 0)
    row = jnp.where(row >= tok, row - tok, row)

    def score(q_now, keys):
        return lax.dot_general(
            q_now, keys, (((1,), (1,)), ((), ())), preferred_element_type=jnp.float32
        )

    def join(state, scores, values):
        peak, total, acc = state
        top = jnp.maximum(peak, jnp.max(scores, axis=1, keepdims=True))
        keep = jnp.exp2(peak - top)
        weights = jnp.exp2(scores - top)
        total = total * keep + jnp.sum(weights, axis=1, keepdims=True)
        acc = acc * keep + jnp.dot(
            weights.astype(jnp.bfloat16), values, preferred_element_type=jnp.float32
        )
        return top, total, acc

    @pl.loop(0, count)
    def _(step):
        first = pl.multiple_of(step * tok, tok)
        q_now = q_all[pl.ds(pl.multiple_of(2 * step * tok, 2 * tok), 2 * tok), :]
        token = row + first
        late = token >= cut

        def prefix(req, state):
            start = pl.multiple_of(req * span, span)
            at = 2 + 3 * req
            inside = jnp.where(
                col < 512,
                (col < meta[at]).astype(jnp.int32),
                jnp.where(
                    col < 768,
                    (col - 512 < meta[at + 1]).astype(jnp.int32),
                    (col - 768 < meta[at + 2]).astype(jnp.int32),
                ),
            )
            outside = jnp.where(inside > 0, 0.0, MASKED)
            foreign = jnp.where(late.astype(jnp.int32) == req, 0.0, MASKED)
            scores = scale * score(q_now, pk_all[pl.ds(start, span), :]) + outside + foreign
            return join(state, scores, pv_all[pl.ds(start, span), :])

        peak_all[...] = jnp.full((2 * tok, 1), MASKED, jnp.float32)
        total_all[...] = jnp.zeros((2 * tok, 1), jnp.float32)
        acc_all[...] = jnp.zeros((2 * tok, hd), jnp.float32)
        low = (first >= cut).astype(jnp.int32)
        high = (first + tok > cut).astype(jnp.int32)

        @pl.loop(low, high + 1)
        def _(req):
            peak, total, acc = prefix(req, (peak_all[...], total_all[...], acc_all[...]))
            peak_all[...] = peak
            total_all[...] = total
            acc_all[...] = acc

        bottom = jnp.where(late, cut, 0)

        for quarter in range(count // 2):

            @pl.when(step // 2 == quarter)
            def _(quarter=quarter):
                keys = 2 * tok * (quarter + 1)
                other = lax.broadcasted_iota(jnp.int32, (1, keys), 1)
                allowed = jnp.logical_and(other <= token, other >= bottom)
                scores = scale * score(q_now, k_all[0:keys, :])
                peak, total, acc = join(
                    (peak_all[...], total_all[...], acc_all[...]),
                    jnp.where(allowed, scores, MASKED),
                    v_all[0:keys, :],
                )
                done = (acc / total).astype(jnp.bfloat16)
                out[pl.ds(first, tok), 0:hd] = done[:tok]
                out[pl.ds(first, tok), hd : 2 * hd] = done[tok:]


def attend(meta, rows, weights, pieces, gains, cosine, sine):
    group = cosine.shape[0]
    hd = gains.shape[1]
    path_rows = 4 * pieces[0].shape[0]
    in_vmem = pl.BlockSpec(memory_space=pltpu.VMEM)
    return pl.pallas_call(
        attention_kernel,
        out_shape=jax.ShapeDtypeStruct((group, 2 * hd), jnp.bfloat16),
        in_specs=[pl.BlockSpec(memory_space=pltpu.SMEM)] + [in_vmem] * 17,
        out_specs=in_vmem,
        scratch_shapes=[
            pltpu.VMEM((group, rows[0].shape[1]), jnp.bfloat16),
            pltpu.VMEM((2, rows[0].shape[1], 2 * hd), jnp.bfloat16),
            pltpu.VMEM((2 * group, hd), jnp.bfloat16),
            pltpu.VMEM((group, hd), jnp.bfloat16),
            pltpu.VMEM((group, hd), jnp.bfloat16),
            pltpu.VMEM((path_rows, hd), jnp.bfloat16),
            pltpu.VMEM((path_rows, hd), jnp.bfloat16),
            pltpu.VMEM((256, 1), jnp.float32),
            pltpu.VMEM((256, 1), jnp.float32),
            pltpu.VMEM((256, hd), jnp.float32),
        ],
        compiler_params=pltpu.CompilerParams(vmem_limit_bytes=60 * 1024 * 1024),
        cost_estimate=pl.CostEstimate(
            flops=16 * group * group * hd, bytes_accessed=16 * group * 512, transcendentals=3 * group * group
        ),
        name="tree_attention",
    )(meta, *rows, *weights, *pieces, gains, cosine, sine)


def column_block(step, core):
    half = jnp.where(step < 2, core, 1 - core)
    return 2 * half + lax.rem(step, 2)


def multiply(values, pieces):
    rows = pieces[0].shape[0]
    return sum(
        jnp.dot(
            values[:, at * rows : (at + 1) * rows], piece[...], preferred_element_type=jnp.float32
        )
        for at, piece in enumerate(pieces)
    )


def project_kernel(place, attended, *refs):
    own, other = refs[:4], refs[4:8]
    hidden, gain, out, normed, joined_own, joined_other, layer = refs[8:]
    wide = attended.shape[2]
    step = pl.program_id(0)
    x, y, core = place[0], place[1], place[2]

    @pl.when(step == 0)
    def _():
        for at, shift in enumerate((0, 3, 1, 2)):
            for turn in range(2):
                block = attended[lax.rem(x + shift, 4) * 2 + lax.rem(y + turn, 2)]
                swapped = jnp.concatenate([block[:, wide // 2 :], block[:, : wide // 2]], axis=1)
                columns = slice((2 * at + turn) * wide, (2 * at + turn + 1) * wide)
                joined_own[:, columns] = jnp.where(core == 0, block, swapped)
                joined_other[:, columns] = jnp.where(core == 0, swapped, block)

    def add(joined, weight):
        added = multiply(joined[...], weight)
        done = (hidden[...].astype(jnp.float32) + added).astype(jnp.bfloat16)
        out[...] = done
        layer[column_block(step, core)] = done

    @pl.when(step < 2)
    def _():
        add(joined_own, own)

    @pl.when(step >= 2)
    def _():
        add(joined_other, other)

    @pl.when(step == layer.shape[0] - 1)
    def _():
        columns = layer.shape[2]
        parts = [layer[at].astype(jnp.float32) for at in range(layer.shape[0])]
        square = sum(jnp.sum(part * part, axis=1, keepdims=True) for part in parts)
        inverse = lax.rsqrt(square / (columns * len(parts)) + EPS)
        for at, part in enumerate(parts):
            where = slice(at * columns, (at + 1) * columns)
            normed[:, where] = (part * inverse * gain[:, where]).astype(jnp.bfloat16)


def project(place, attended, halves, hidden, gain):
    tok, dim = hidden.shape
    columns = dim // 4
    return pl.pallas_call(
        project_kernel,
        grid_spec=pltpu.PrefetchScalarGridSpec(
            num_scalar_prefetch=1,
            grid=(4,),
            in_specs=[
                pl.BlockSpec(attended.shape, lambda j, at: (0, 0, 0)),
            ]
            + [pl.BlockSpec((dim // 4, columns), lambda j, at: (0, jnp.minimum(j, 1)))] * 4
            + [pl.BlockSpec((dim // 4, columns), lambda j, at: (0, jnp.maximum(j - 2, 0)))] * 4
            + [
                pl.BlockSpec((tok, columns), lambda j, at: (0, column_block(j, at[2]))),
                pl.BlockSpec((1, dim), lambda j, at: (0, 0)),
            ],
            out_specs=(
                pl.BlockSpec((tok, columns), lambda j, at: (0, column_block(j, at[2]))),
                pl.BlockSpec((tok, dim), lambda j, at: (0, 0)),
            ),
            scratch_shapes=[
                pltpu.VMEM((tok, dim), jnp.bfloat16),
                pltpu.VMEM((tok, dim), jnp.bfloat16),
                pltpu.VMEM((4, tok, columns), jnp.bfloat16),
            ],
        ),
        out_shape=(
            jax.ShapeDtypeStruct(hidden.shape, hidden.dtype),
            jax.ShapeDtypeStruct(hidden.shape, hidden.dtype),
        ),
        compiler_params=pltpu.CompilerParams(vmem_limit_bytes=60 * 1024 * 1024),
        name="project",
    )(place, attended, *halves, hidden, gain)


def exchange(values):
    return lax.all_to_all(values, BOTH, split_axis=0, concat_axis=0, tiled=True)


def expert(rows, gate_up, down_weight):
    ff_width = down_weight.shape[0]
    both = jnp.dot(rows, gate_up, preferred_element_type=jnp.float32)
    active = (jax.nn.silu(both[:, :ff_width]) * both[:, ff_width:]).astype(jnp.bfloat16)
    return jnp.dot(active, down_weight, preferred_element_type=jnp.float32).astype(jnp.bfloat16)


def rest_kernel(rows, gate_up, down_weight, main_block, out):
    del main_block
    ff_width = down_weight.shape[0]
    spans = out.shape[0]
    wide = out.shape[2]
    chunks = down_weight.shape[1] // wide
    per = rows.shape[0] // spans
    both = jnp.dot(rows[...], gate_up[...], preferred_element_type=jnp.float32)
    gate = both[:, :ff_width]
    active = (gate / (1.0 + jnp.exp(-gate)) * both[:, ff_width:]).astype(jnp.bfloat16)
    served = jnp.dot(active, down_weight[...], preferred_element_type=jnp.float32)
    served = served.astype(jnp.bfloat16)
    batch = 16
    size = batch * per * chunks
    to = lax.broadcasted_iota(jnp.int32, (size, size), 0)
    source = lax.broadcasted_iota(jnp.int32, (size, size), 1)
    device = to // (per * chunks)
    chunk = to // per % chunks
    wanted = chunk * (batch * per) + device * per + to % per
    order = (source == wanted).astype(jnp.bfloat16)
    for first in range(0, spans, batch):
        stacked = jnp.concatenate(
            [
                served[first * per : (first + batch) * per, at * wide : (at + 1) * wide]
                for at in range(chunks)
            ],
            axis=0,
        )
        sorted_rows = jnp.dot(order, stacked, preferred_element_type=jnp.float32)
        out[first : first + batch] = sorted_rows.reshape(batch, per * chunks, wide).astype(
            jnp.bfloat16
        )


def expert_rest(rows, gate_up, down_weight, main_block):
    spans, height, wide = main_block.shape
    extra = rows.shape[0] // spans * down_weight.shape[1] // wide
    in_vmem = pl.BlockSpec(memory_space=pltpu.VMEM)
    return pl.pallas_call(
        rest_kernel,
        grid=(1,),
        out_shape=jax.ShapeDtypeStruct(main_block.shape, main_block.dtype),
        in_specs=[in_vmem, in_vmem, in_vmem, pl.BlockSpec(memory_space=pl.ANY)],
        out_specs=pl.BlockSpec((spans, extra, wide), lambda i: (0, height // extra - 1, 0)),
        input_output_aliases={3: 0},
        compiler_params=pltpu.CompilerParams(vmem_limit_bytes=60 * 1024 * 1024),
        name="expert_rest",
    )(rows, gate_up, down_weight, main_block)


def reorder(place, joined):
    x, y, core = place[0], place[1], place[2]
    wide = joined.shape[1] // 8
    mine, theirs = [], []
    for shift in (0, 3, 1, 2):
        for turn in range(2):
            block_no = lax.rem(x + shift, 4) * 2 + lax.rem(y + turn, 2)
            block = joined[:, pl.ds(pl.multiple_of(block_no * wide, wide), wide)]
            swapped = jnp.concatenate([block[:, wide // 2 :], block[:, : wide // 2]], axis=1)
            mine.append(jnp.where(core == 0, block, swapped))
            theirs.append(jnp.where(core == 0, swapped, block))
    return jnp.concatenate(mine, axis=1), jnp.concatenate(theirs, axis=1)


def finish_kernel(place, main_share, rest_share, main_rows, rest_rows, stream, *refs):
    next_own, next_other = refs[:4], refs[4:8]
    norm_gain, head_gain, cosine, sine, out, next_rows, layer, joined = refs[8:]
    tok = stream.shape[0]
    count = main_share.shape[1]
    wide = main_rows.shape[2]
    hd = head_gain.shape[1]
    step = pl.program_id(0)

    def flat(values):
        values = values[...].astype(jnp.float32).reshape(count, wide)
        return values.astype(jnp.bfloat16)

    total = jnp.dot(main_share[...], flat(main_rows), preferred_element_type=jnp.float32)
    total += jnp.dot(rest_share[0], flat(rest_rows), preferred_element_type=jnp.float32)
    done = (stream[...].astype(jnp.float32) + total[:tok] + total[tok:]).astype(jnp.bfloat16)
    out[...] = done
    layer[step] = done

    @pl.when(step == layer.shape[0] - 1)
    def _():
        parts = [layer[at].astype(jnp.float32) for at in range(layer.shape[0])]
        square = sum(jnp.sum(part * part, axis=1, keepdims=True) for part in parts)
        inverse = lax.rsqrt(square / (wide * len(parts)) + EPS)
        for at, part in enumerate(parts):
            columns = slice(at * wide, (at + 1) * wide)
            normed = (part * inverse * norm_gain[:, columns]).astype(jnp.bfloat16)
            joined[:, columns] = normed
        mine, theirs = reorder(place, joined)
        raw_own = multiply(mine, next_own)
        raw_other = multiply(theirs, next_other)
        keys = jnp.where(place[2] == 0, raw_own, raw_other)
        values = jnp.where(place[2] == 0, raw_other, raw_own)
        half = keys.shape[1]
        for head in range(half // hd):
            columns = slice(head * hd, (head + 1) * hd)
            key = keys[:, columns]
            key = key * lax.rsqrt(jnp.mean(key * key, axis=-1, keepdims=True) + EPS)
            key = key * head_gain[...]
            key = key * cosine[...] + pltpu.roll(key, hd // 2, 1) * sine[...]
            next_rows[:, columns] = key.astype(jnp.bfloat16)
        next_rows[:, half:] = values.astype(jnp.bfloat16)


def finish(place, main_share, rest_share, returned, stream, halves, norm_gain, head_gain, turns):
    devices, height, wide = returned.shape
    tok, dim = stream.shape
    extra = halves[0].shape[1] - dim // 2
    chunks = dim // wide
    rows = height // (chunks + 1)
    shape = main_share.shape

    def fixed(values):
        return pl.BlockSpec(values.shape, lambda j, at: (0, 0))

    next_spec = pl.BlockSpec((dim // 4, extra), lambda j, at: (0, dim // 2 // extra))
    return pl.pallas_call(
        finish_kernel,
        grid_spec=pltpu.PrefetchScalarGridSpec(
            num_scalar_prefetch=1,
            grid=(chunks,),
            in_specs=[
                fixed(main_share),
                pl.BlockSpec((1,) + shape, lambda j, at: (j, 0, 0)),
                pl.BlockSpec((devices, rows, wide), lambda j, at: (0, j, 0)),
                pl.BlockSpec((devices, rows, wide), lambda j, at: (0, chunks, 0)),
                pl.BlockSpec((tok, wide), lambda j, at: (0, j)),
            ]
            + [next_spec] * 8
            + [
                fixed(norm_gain),
                fixed(head_gain),
                fixed(turns[0]),
                fixed(turns[1]),
            ],
            out_specs=(
                pl.BlockSpec((tok, wide), lambda j, at: (0, j)),
                pl.BlockSpec((tok, 2 * extra), lambda j, at: (0, 0)),
            ),
            scratch_shapes=[
                pltpu.VMEM((chunks, tok, wide), jnp.bfloat16),
                pltpu.VMEM((tok, dim), jnp.bfloat16),
            ],
        ),
        out_shape=(
            jax.ShapeDtypeStruct(stream.shape, stream.dtype),
            jax.ShapeDtypeStruct((tok, 2 * extra), stream.dtype),
        ),
        compiler_params=pltpu.CompilerParams(vmem_limit_bytes=60 * 1024 * 1024),
        name="finish",
    )(
        place,
        main_share,
        rest_share,
        returned,
        returned,
        stream,
        *halves,
        norm_gain,
        head_gain,
        *turns,
    )


def per_device(
    hidden,
    norm_gains,
    head_gains,
    query_weight,
    kv_weight,
    out_weight,
    gate_up,
    down_weight,
    next_weight,
    expert_ids,
    route_weights,
    token_request,
    request_leaf,
    leaf_parent,
    mid_parent,
    root_length,
    mid_length,
    leaf_length,
    root_slot,
    mid_slot,
    leaf_slot,
    root_cache,
    mid_cache,
    leaf_cache,
):
    tok, dim = hidden.shape
    hd = head_gains.shape[1]
    group = token_request.shape[0]
    mp_size = lax.axis_size("mp")
    dp_size = lax.axis_size("dp")
    devices = dp_size * mp_size
    me = lax.axis_index("mp")
    own_rows = query_weight.shape[0]

    pair = token_request[0] + jnp.arange(2, dtype=jnp.int32)
    cut = jnp.sum((token_request == pair[0]).astype(jnp.int32))
    leaf_node = look_up(request_leaf, pair)
    mid_node = look_up(leaf_parent, leaf_node)
    root_node = look_up(mid_parent, mid_node)
    lengths = (
        look_up(root_length, root_node),
        look_up(mid_length, mid_node),
        look_up(leaf_length, leaf_node),
    )
    prefix_length = lengths[0] + lengths[1] + lengths[2]
    token = jnp.arange(group, dtype=jnp.int32)
    positions = token + jnp.where(token >= cut, prefix_length[1] - cut, prefix_length[0])
    frequency = THETA ** (-2.0 * jnp.arange(hd // 2, dtype=jnp.float32) / hd)
    angles = positions.astype(jnp.float32)[:, None] * frequency[None, :]
    cos_half = jnp.cos(angles)
    sin_half = jnp.sin(angles)
    cosine = jnp.concatenate([cos_half, cos_half], axis=1)
    sine = jnp.concatenate([-sin_half, sin_half], axis=1)

    normed = rms_norm(hidden, norm_gains[0]).astype(jnp.bfloat16)
    def shift(values, step):
        moves = [(j, j - j % 4 + (j % 4 + step) % 4) for j in range(mp_size)]
        return lax.ppermute(values, "mp", moves)

    across = lax.ppermute(normed, "mp", [(j, (j + 4) % mp_size) for j in range(mp_size)])
    left = shift(normed, 1)
    right = shift(normed, -1)
    packed = pack_weights(query_weight, kv_weight, out_weight, next_weight, mp_size)
    packed = lax.all_to_all(packed, "mp", split_axis=0, concat_axis=0, tiled=True)
    packed, across, left, right = lax.optimization_barrier((packed, across, left, right))
    packed = packed.reshape(mp_size * own_rows, -1)
    late_width = dim + next_weight.shape[1]
    dp_at = lax.axis_index("dp")
    core = lax.rem(dp_at, 2)
    place = jnp.stack([dp_at // 4, lax.rem(dp_at // 2, 2), core]).astype(jnp.int32)

    def swap(values, bit):
        return lax.ppermute(values, "dp", [(j, j ^ bit) for j in range(dp_size)])

    def shift_x(values, step):
        moves = [(j, (j + 4 * step) % dp_size) for j in range(dp_size)]
        return lax.ppermute(values, "dp", moves)

    low, high = packed[:, : late_width // 2], packed[:, late_width // 2 : late_width]
    kept = jnp.where(core == 0, low, high)
    late = jnp.concatenate([kept, swap(jnp.where(core == 0, high, low), 1)], axis=0)
    late = jnp.concatenate([late, swap(late, 2)], axis=0)
    early = packed[:, late_width:].reshape(packed.shape[0], 2, 2 * hd).transpose(1, 0, 2)
    early = jnp.broadcast_to(early[None], (dp_size // 2,) + early.shape)
    early = early.reshape(dp_size, packed.shape[0], 2 * hd)
    early = lax.all_to_all(early, "dp", split_axis=0, concat_axis=0, tiled=True)
    early = early.reshape(dim, 2 * hd)
    sides = [left, right, shift(across, 1), shift(across, -1)]
    far = [shift(normed, 2), shift(across, 2)]
    tables = (
        token_request,
        request_leaf,
        leaf_parent,
        mid_parent,
        root_slot,
        mid_slot,
        leaf_slot,
    )
    path = pack_paths(tables, root_cache, mid_cache, leaf_cache, mp_size)
    meta = jnp.concatenate(
        [
            jnp.stack([me, cut]),
            jnp.stack(lengths, axis=1).reshape(-1),
            jnp.stack([lax.rem(lax.axis_index("dp"), 2)]),
        ]
    ).astype(jnp.int32)
    path, sides, far, early, cosine, sine, meta = lax.optimization_barrier(
        (path, sides, far, early, cosine, sine, meta)
    )
    weights = (early, swap(early, 1))
    x_left = shift_x(late, 1)
    x_right = shift_x(late, -1)
    path = lax.all_to_all(path, "mp", split_axis=0, concat_axis=0, tiled=True)
    own_piece = jnp.sum(path.astype(jnp.float32), axis=0).astype(jnp.bfloat16)
    own_piece, weights, handed = lax.optimization_barrier((own_piece, weights, swap(late, 1)))
    pieces = [own_piece] + [
        lax.ppermute(own_piece, "mp", [(j, j ^ s) for j in range(mp_size)]) for s in range(1, 4)
    ]
    pieces, x_left, x_right = lax.optimization_barrier((pieces, x_left, x_right))
    x_far = shift_x(x_left, 1)
    rows = [normed, across] + sides + far
    attended = attend(meta, rows, weights, pieces, head_gains, cosine, sine)
    attended, x_far = lax.optimization_barrier((attended, x_far))
    halves = (late, x_left, x_right, x_far, handed)
    halves += tuple(swap(piece, 1) for piece in (x_left, x_right, x_far))
    attended = lax.all_to_all(
        attended.reshape(mp_size, tok, 2 * hd), "mp", split_axis=0, concat_axis=0, tiled=True
    )
    after_attention, moe_in = project(place, attended, halves, hidden, norm_gains[1:2])

    top_k = expert_ids.shape[1]
    capacity = max(2, 5 * tok * top_k // (4 * devices))
    names = expert_ids[:, :, None] == jnp.arange(devices, dtype=jnp.int32)[None, None, :]
    named = jnp.any(names, axis=1)
    route = jnp.sum(jnp.where(names, route_weights[:, :, None], 0.0), axis=1)
    before = jnp.tril(jnp.ones((tok, tok), jnp.bfloat16), -1)
    slot_no = jnp.dot(before, named.astype(jnp.bfloat16), preferred_element_type=jnp.float32)
    slot_no = jnp.where(named, slot_no.astype(jnp.int32), -1)

    def spread(first, last):
        count = jnp.arange(first, last, dtype=jnp.int32)
        taken = slot_no.T[:, None, :] == count[None, :, None]
        return taken.astype(jnp.bfloat16).reshape(devices * (last - first), tok)

    def gather_back(first, last):
        count = jnp.arange(first, last, dtype=jnp.int32)
        taken = slot_no[:, :, None] == count[None, None, :]
        share = jnp.where(taken, route[:, :, None], 0.0).reshape(tok, devices * (last - first))
        upper = lax.reduce_precision(share, 8, 7)
        return jnp.concatenate([upper, share - upper], axis=0).astype(jnp.bfloat16)

    def outbound(first, last, source):
        picked = jnp.dot(spread(first, last), source, preferred_element_type=jnp.float32)
        return picked.astype(jnp.bfloat16).reshape(devices, last - first, dim)

    main_in = exchange(outbound(0, MAIN, moe_in))
    main_in, rest_in = lax.optimization_barrier((main_in, outbound(MAIN, capacity, moe_in)))
    rest_in = exchange(rest_in)
    chunks = MAIN // (capacity - MAIN)
    wide = dim // chunks
    main_out = expert(main_in.reshape(-1, dim), gate_up[0], down_weight[0])
    main_out = main_out.reshape(devices, MAIN, chunks, wide).transpose(0, 2, 1, 3)
    main_out = main_out.reshape(devices, MAIN * chunks, wide)
    main_out = jnp.pad(main_out, ((0, 0), (0, MAIN), (0, 0)))
    main_out, rest_in = lax.optimization_barrier((main_out, rest_in))
    returned = exchange(expert_rest(rest_in.reshape(-1, dim), gate_up[0], down_weight[0], main_out))
    main_share = gather_back(0, MAIN)
    rest_share = gather_back(MAIN, capacity).reshape(1, 2 * tok, devices, 1, capacity - MAIN)
    which = jnp.eye(chunks, dtype=jnp.bfloat16).reshape(chunks, 1, 1, chunks, 1)
    rest_share = (rest_share * which).reshape(chunks, 2 * tok, devices * MAIN)
    my_cos = lax.dynamic_slice_in_dim(cosine, me * tok, tok)
    my_sin = lax.dynamic_slice_in_dim(sine, me * tok, tok)
    layer_out, next_rows = finish(
        place,
        main_share,
        rest_share,
        returned,
        after_attention,
        halves,
        norm_gains[2:3],
        head_gains[2:3],
        (my_cos, my_sin),
    )
    return (layer_out, next_rows)


def solution(mesh):
    both = P(BOTH, None)
    placed = (
        both,
        P(),
        P(),
        both,
        both,
        both,
        P(BOTH, None, None),
        P(BOTH, None, None),
        both,
        both,
        both,
        P("dp"),
        P(),
        P(),
        P(),
        P(),
        P(),
        P(),
        P(),
        P(),
        P(),
        P("mp", None, None),
        P("mp", None, None),
        P("mp", None, None),
    )
    return jax.shard_map(
        per_device,
        mesh=mesh,
        in_specs=placed,
        out_specs=(both, both),
        check_vma=False,
    )
```

```python
import jax
import jax.numpy as jnp
from jax import lax
from jax.experimental import pallas as pl
from jax.experimental.pallas import tpu as pltpu
from jax.sharding import PartitionSpec as P

EPS = 1e-06
THETA = 1000000.0
MASKED = -1e30
LOG2E = 1.4426950408889634
BOTH = ("dp", "mp")
MAIN = 8


def rms_norm(values, weight_row):
    values = values.astype(jnp.float32)
    return values * lax.rsqrt(jnp.mean(values * values, axis=-1, keepdims=True) + EPS) * weight_row


def look_up(lookup_table, indices):
    places = jnp.arange(lookup_table.shape[0], dtype=jnp.int32)
    return jnp.sum(jnp.where(indices[:, None] == places[None, :], lookup_table[None, :], 0), axis=1)


def pack_weights_kernel(query, kv, out_rows, next_rows, packed):
    count = packed.shape[0]
    dim = out_rows.shape[1]
    extra = next_rows.shape[1]
    wide = query.shape[1] // count
    hd = wide // 2
    heads = kv.shape[1] // 2 // hd
    base = dim + extra
    for dest in range(count):
        head = dest * heads // count
        for half in range(2):
            at = half * base // 2
            packed[dest, :, at : at + dim // 2] = out_rows[
                :, half * dim // 2 : (half + 1) * dim // 2
            ]
            packed[dest, :, at + dim // 2 : at + base // 2] = next_rows[
                :, half * extra // 2 : (half + 1) * extra // 2
            ]
        packed[dest, :, base : base + wide] = query[:, dest * wide : (dest + 1) * wide]
        for half in range(2):
            source = (half * heads + head) * hd
            target = base + wide + half * hd
            packed[dest, :, target : target + hd] = kv[:, source : source + hd]


def pack_weights(query, kv, out_rows, next_rows, count):
    rows = query.shape[0]
    width = out_rows.shape[1] + next_rows.shape[1] + 2 * (query.shape[1] // count)
    in_vmem = pl.BlockSpec(memory_space=pltpu.VMEM)
    return pl.pallas_call(
        pack_weights_kernel,
        out_shape=jax.ShapeDtypeStruct((count, rows, width), jnp.bfloat16),
        in_specs=[in_vmem] * 4,
        out_specs=in_vmem,
        name="pack_weights",
    )(query, kv, out_rows, next_rows)


def pack_paths_kernel(
    token_request,
    request_leaf,
    leaf_parent,
    mid_parent,
    root_slot,
    mid_slot,
    leaf_slot,
    root,
    mid,
    leaf,
    packed,
):
    count, part, wide = packed.shape
    hd = wide // 2
    heads = count // 4
    me = lax.axis_index("mp")
    for req in range(2):
        leaf_node = request_leaf[token_request[0] + req]
        mid_node = leaf_parent[leaf_node]
        slots = (root_slot[mid_parent[mid_node]], mid_slot[mid_node], leaf_slot[leaf_node])
        levels = []
        for slot, cache in zip(slots, (root, mid, leaf)):
            here = cache.shape[0]
            rows = jnp.zeros(cache.shape[1:], cache.dtype)
            for local in range(here):
                rows = jnp.where(slot == me * here + local, cache[local], rows)
            levels.append(rows)
        top = levels[0].shape[0] - part
        middle = levels[1].shape[0]
        for head in range(heads):
            for half in range(2):
                source = slice((half * heads + head) * hd, (half * heads + head + 1) * hd)
                target = slice(half * hd, (half + 1) * hd)
                place = 4 * head + 2 * req
                packed[place, :, target] = levels[0][:part, source]
                packed[place + 1, 0:top, target] = levels[0][part:, source]
                packed[place + 1, top : top + middle, target] = levels[1][:, source]
                packed[place + 1, top + middle :, target] = levels[2][:, source]


def pack_paths(tables, root, mid, leaf, count):
    wide = root.shape[2] // 2
    part = (root.shape[1] + mid.shape[1] + leaf.shape[1]) // 2
    in_vmem = pl.BlockSpec(memory_space=pltpu.VMEM)
    in_smem = pl.BlockSpec(memory_space=pltpu.SMEM)
    return pl.pallas_call(
        pack_paths_kernel,
        out_shape=jax.ShapeDtypeStruct((count, part, wide), jnp.bfloat16),
        in_specs=[in_smem] * len(tables) + [in_vmem] * 3,
        out_specs=in_vmem,
        compiler_params=pltpu.CompilerParams(vmem_limit_bytes=24 * 1024 * 1024),
        name="pack_paths",
    )(*tables, root, mid, leaf)


def attention_kernel(
    meta,
    own,
    across,
    own_left,
    own_right,
    across_left,
    across_right,
    own_far,
    across_far,
    weight_own,
    weight_other,
    piece_0,
    piece_1,
    piece_2,
    piece_3,
    gains,
    cosine,
    sine,
    out,
    rows_all,
    weights,
    q_all,
    k_all,
    v_all,
    pk_all,
    pv_all,
    peak_all,
    total_all,
    acc_all,
):
    pieces = (piece_0, piece_1, piece_2, piece_3)
    me = meta[0]
    cut = meta[1]
    tok, dim = own.shape
    count = rows_all.shape[0] // tok
    hd = gains.shape[1]
    span = pk_all.shape[0] // 2
    part = piece_0.shape[0]
    ring = lax.rem(me, 4)
    base = me - ring
    far_base = 4 - base

    def put(first, step, block):
        at = pl.multiple_of((first + lax.rem(ring + step, 4)) * tok, tok)
        rows_all[pl.ds(at, tok), :] = block[...]

    put(base, 0, own)
    put(far_base, 0, across)
    put(base, 3, own_left)
    put(base, 1, own_right)
    put(far_base, 3, across_left)
    put(far_base, 1, across_right)
    put(base, 2, own_far)
    put(far_base, 2, across_far)
    for step, piece in enumerate(pieces):
        place = pl.multiple_of((ring ^ step) * part, part)
        pk_all[pl.ds(place, part), :] = piece[:, :hd]
        pv_all[pl.ds(place, part), :] = piece[:, hd:]
    core = meta[8]
    weights[core] = weight_own[...]
    weights[1 - core] = weight_other[...]
    weight_q = weights[0]
    weight_kv = weights[1]

    def turn(raw, gain, cos_now, sin_now):
        scaled = raw * lax.rsqrt(jnp.mean(raw * raw, axis=-1, keepdims=True) + EPS) * gain
        return (scaled * cos_now + pltpu.roll(scaled, hd // 2, 1) * sin_now).astype(jnp.bfloat16)

    large = 4 * tok

    @pl.loop(0, count // 4)
    def _(step):
        at = pl.multiple_of(step * large, large)
        rows = rows_all[pl.ds(at, large), :]
        cos_now = cosine[pl.ds(at, large), :]
        sin_now = sine[pl.ds(at, large), :]
        raw = jnp.dot(rows, weight_q, preferred_element_type=jnp.float32)
        heads = [
            turn(raw[:, half * hd : (half + 1) * hd], gains[0:1, :], cos_now, sin_now)
            for half in range(2)
        ]
        for block in range(4):
            for half in range(2):
                q_at = pl.multiple_of(2 * at + (2 * block + half) * tok, tok)
                q_all[pl.ds(q_at, tok), :] = heads[half][block * tok : (block + 1) * tok]
        raw = jnp.dot(rows, weight_kv, preferred_element_type=jnp.float32)
        k_all[pl.ds(at, large), :] = turn(raw[:, :hd], gains[1:2, :], cos_now, sin_now)
        v_all[pl.ds(at, large), :] = raw[:, hd:].astype(jnp.bfloat16)

    scale = hd ** (-0.5) * LOG2E
    col = lax.broadcasted_iota(jnp.int32, (1, span), 1)
    row = lax.broadcasted_iota(jnp.int32, (2 * tok, 1), 0)
    row = jnp.where(row >= tok, row - tok, row)

    def score(q_now, keys):
        return lax.dot_general(
            q_now, keys, (((1,), (1,)), ((), ())), preferred_element_type=jnp.float32
        )

    def join(state, scores, values):
        peak, total, acc = state
        top = jnp.maximum(peak, jnp.max(scores, axis=1, keepdims=True))
        keep = jnp.exp2(peak - top)
        weights = jnp.exp2(scores - top)
        total = total * keep + jnp.sum(weights, axis=1, keepdims=True)
        acc = acc * keep + jnp.dot(
            weights.astype(jnp.bfloat16), values, preferred_element_type=jnp.float32
        )
        return top, total, acc

    @pl.loop(0, count)
    def _(step):
        first = pl.multiple_of(step * tok, tok)
        q_now = q_all[pl.ds(pl.multiple_of(2 * step * tok, 2 * tok), 2 * tok), :]
        token = row + first
        late = token >= cut

        def prefix(req, state):
            start = pl.multiple_of(req * span, span)
            at = 2 + 3 * req
            inside = jnp.where(
                col < 512,
                (col < meta[at]).astype(jnp.int32),
                jnp.where(
                    col < 768,
                    (col - 512 < meta[at + 1]).astype(jnp.int32),
                    (col - 768 < meta[at + 2]).astype(jnp.int32),
                ),
            )
            outside = jnp.where(inside > 0, 0.0, MASKED)
            foreign = jnp.where(late.astype(jnp.int32) == req, 0.0, MASKED)
            scores = scale * score(q_now, pk_all[pl.ds(start, span), :]) + outside + foreign
            return join(state, scores, pv_all[pl.ds(start, span), :])

        peak_all[...] = jnp.full((2 * tok, 1), MASKED, jnp.float32)
        total_all[...] = jnp.zeros((2 * tok, 1), jnp.float32)
        acc_all[...] = jnp.zeros((2 * tok, hd), jnp.float32)
        low = (first >= cut).astype(jnp.int32)
        high = (first + tok > cut).astype(jnp.int32)

        @pl.loop(low, high + 1)
        def _(req):
            peak, total, acc = prefix(req, (peak_all[...], total_all[...], acc_all[...]))
            peak_all[...] = peak
            total_all[...] = total
            acc_all[...] = acc

        bottom = jnp.where(late, cut, 0)

        for quarter in range(count // 2):

            @pl.when(step // 2 == quarter)
            def _(quarter=quarter):
                keys = 2 * tok * (quarter + 1)
                other = lax.broadcasted_iota(jnp.int32, (1, keys), 1)
                allowed = jnp.logical_and(other <= token, other >= bottom)
                scores = scale * score(q_now, k_all[0:keys, :])
                peak, total, acc = join(
                    (peak_all[...], total_all[...], acc_all[...]),
                    jnp.where(allowed, scores, MASKED),
                    v_all[0:keys, :],
                )
                done = (acc / total).astype(jnp.bfloat16)
                out[pl.ds(first, tok), 0:hd] = done[:tok]
                out[pl.ds(first, tok), hd : 2 * hd] = done[tok:]


def attend(meta, rows, weights, pieces, gains, cosine, sine):
    group = cosine.shape[0]
    hd = gains.shape[1]
    path_rows = 4 * pieces[0].shape[0]
    in_vmem = pl.BlockSpec(memory_space=pltpu.VMEM)
    return pl.pallas_call(
        attention_kernel,
        out_shape=jax.ShapeDtypeStruct((group, 2 * hd), jnp.bfloat16),
        in_specs=[pl.BlockSpec(memory_space=pltpu.SMEM)] + [in_vmem] * 17,
        out_specs=in_vmem,
        scratch_shapes=[
            pltpu.VMEM((group, rows[0].shape[1]), jnp.bfloat16),
            pltpu.VMEM((2, rows[0].shape[1], 2 * hd), jnp.bfloat16),
            pltpu.VMEM((2 * group, hd), jnp.bfloat16),
            pltpu.VMEM((group, hd), jnp.bfloat16),
            pltpu.VMEM((group, hd), jnp.bfloat16),
            pltpu.VMEM((path_rows, hd), jnp.bfloat16),
            pltpu.VMEM((path_rows, hd), jnp.bfloat16),
            pltpu.VMEM((256, 1), jnp.float32),
            pltpu.VMEM((256, 1), jnp.float32),
            pltpu.VMEM((256, hd), jnp.float32),
        ],
        compiler_params=pltpu.CompilerParams(vmem_limit_bytes=60 * 1024 * 1024),
        cost_estimate=pl.CostEstimate(
            flops=16 * group * group * hd, bytes_accessed=16 * group * 512, transcendentals=3 * group * group
        ),
        name="tree_attention",
    )(meta, *rows, *weights, *pieces, gains, cosine, sine)


def column_block(step, core):
    half = jnp.where(step < 2, core, 1 - core)
    return 2 * half + lax.rem(step, 2)


def multiply(values, pieces):
    rows = pieces[0].shape[0]
    return sum(
        jnp.dot(
            values[:, at * rows : (at + 1) * rows], piece[...], preferred_element_type=jnp.float32
        )
        for at, piece in enumerate(pieces)
    )


def project_kernel(place, attended, *refs):
    own, other = refs[:4], refs[4:8]
    hidden, gain, out, normed, joined_own, joined_other, layer = refs[8:]
    wide = attended.shape[2]
    step = pl.program_id(0)
    x, y, core = place[0], place[1], place[2]

    @pl.when(step == 0)
    def _():
        for at, shift in enumerate((0, 3, 1, 2)):
            for turn in range(2):
                block = attended[lax.rem(x + shift, 4) * 2 + lax.rem(y + turn, 2)]
                swapped = jnp.concatenate([block[:, wide // 2 :], block[:, : wide // 2]], axis=1)
                columns = slice((2 * at + turn) * wide, (2 * at + turn + 1) * wide)
                joined_own[:, columns] = jnp.where(core == 0, block, swapped)
                joined_other[:, columns] = jnp.where(core == 0, swapped, block)

    def add(joined, weight):
        added = multiply(joined[...], weight)
        done = (hidden[...].astype(jnp.float32) + added).astype(jnp.bfloat16)
        out[...] = done
        layer[column_block(step, core)] = done

    @pl.when(step < 2)
    def _():
        add(joined_own, own)

    @pl.when(step >= 2)
    def _():
        add(joined_other, other)

    @pl.when(step == layer.shape[0] - 1)
    def _():
        columns = layer.shape[2]
        parts = [layer[at].astype(jnp.float32) for at in range(layer.shape[0])]
        square = sum(jnp.sum(part * part, axis=1, keepdims=True) for part in parts)
        inverse = lax.rsqrt(square / (columns * len(parts)) + EPS)
        for at, part in enumerate(parts):
            where = slice(at * columns, (at + 1) * columns)
            normed[:, where] = (part * inverse * gain[:, where]).astype(jnp.bfloat16)


def project(place, attended, halves, hidden, gain):
    tok, dim = hidden.shape
    columns = dim // 4
    return pl.pallas_call(
        project_kernel,
        grid_spec=pltpu.PrefetchScalarGridSpec(
            num_scalar_prefetch=1,
            grid=(4,),
            in_specs=[
                pl.BlockSpec(attended.shape, lambda j, at: (0, 0, 0)),
            ]
            + [pl.BlockSpec((dim // 4, columns), lambda j, at: (0, jnp.minimum(j, 1)))] * 4
            + [pl.BlockSpec((dim // 4, columns), lambda j, at: (0, jnp.maximum(j - 2, 0)))] * 4
            + [
                pl.BlockSpec((tok, columns), lambda j, at: (0, column_block(j, at[2]))),
                pl.BlockSpec((1, dim), lambda j, at: (0, 0)),
            ],
            out_specs=(
                pl.BlockSpec((tok, columns), lambda j, at: (0, column_block(j, at[2]))),
                pl.BlockSpec((tok, dim), lambda j, at: (0, 0)),
            ),
            scratch_shapes=[
                pltpu.VMEM((tok, dim), jnp.bfloat16),
                pltpu.VMEM((tok, dim), jnp.bfloat16),
                pltpu.VMEM((4, tok, columns), jnp.bfloat16),
            ],
        ),
        out_shape=(
            jax.ShapeDtypeStruct(hidden.shape, hidden.dtype),
            jax.ShapeDtypeStruct(hidden.shape, hidden.dtype),
        ),
        compiler_params=pltpu.CompilerParams(vmem_limit_bytes=60 * 1024 * 1024),
        name="project",
    )(place, attended, *halves, hidden, gain)


def exchange(values):
    return lax.all_to_all(values, BOTH, split_axis=0, concat_axis=0, tiled=True)


def expert(rows, gate_up, down_weight):
    ff_width = down_weight.shape[0]
    both = jnp.dot(rows, gate_up, preferred_element_type=jnp.float32)
    active = (jax.nn.silu(both[:, :ff_width]) * both[:, ff_width:]).astype(jnp.bfloat16)
    return jnp.dot(active, down_weight, preferred_element_type=jnp.float32).astype(jnp.bfloat16)


def rest_kernel(rows, gate_up, down_weight, main_block, out):
    del main_block
    ff_width = down_weight.shape[0]
    spans = out.shape[0]
    wide = out.shape[2]
    chunks = down_weight.shape[1] // wide
    per = rows.shape[0] // spans
    both = jnp.dot(rows[...], gate_up[...], preferred_element_type=jnp.float32)
    gate = both[:, :ff_width]
    active = (gate / (1.0 + jnp.exp(-gate)) * both[:, ff_width:]).astype(jnp.bfloat16)
    served = jnp.dot(active, down_weight[...], preferred_element_type=jnp.float32)
    served = served.astype(jnp.bfloat16)
    batch = 16
    size = batch * per * chunks
    to = lax.broadcasted_iota(jnp.int32, (size, size), 0)
    source = lax.broadcasted_iota(jnp.int32, (size, size), 1)
    device = to // (per * chunks)
    chunk = to // per % chunks
    wanted = chunk * (batch * per) + device * per + to % per
    order = (source == wanted).astype(jnp.bfloat16)
    for first in range(0, spans, batch):
        stacked = jnp.concatenate(
            [
                served[first * per : (first + batch) * per, at * wide : (at + 1) * wide]
                for at in range(chunks)
            ],
            axis=0,
        )
        sorted_rows = jnp.dot(order, stacked, preferred_element_type=jnp.float32)
        out[first : first + batch] = sorted_rows.reshape(batch, per * chunks, wide).astype(
            jnp.bfloat16
        )


def expert_rest(rows, gate_up, down_weight, main_block):
    spans, height, wide = main_block.shape
    extra = rows.shape[0] // spans * down_weight.shape[1] // wide
    in_vmem = pl.BlockSpec(memory_space=pltpu.VMEM)
    return pl.pallas_call(
        rest_kernel,
        grid=(1,),
        out_shape=jax.ShapeDtypeStruct(main_block.shape, main_block.dtype),
        in_specs=[in_vmem, in_vmem, in_vmem, pl.BlockSpec(memory_space=pl.ANY)],
        out_specs=pl.BlockSpec((spans, extra, wide), lambda i: (0, height // extra - 1, 0)),
        input_output_aliases={3: 0},
        compiler_params=pltpu.CompilerParams(vmem_limit_bytes=60 * 1024 * 1024),
        name="expert_rest",
    )(rows, gate_up, down_weight, main_block)


def reorder(place, joined):
    x, y, core = place[0], place[1], place[2]
    wide = joined.shape[1] // 8
    mine, theirs = [], []
    for shift in (0, 3, 1, 2):
        for turn in range(2):
            block_no = lax.rem(x + shift, 4) * 2 + lax.rem(y + turn, 2)
            block = joined[:, pl.ds(pl.multiple_of(block_no * wide, wide), wide)]
            swapped = jnp.concatenate([block[:, wide // 2 :], block[:, : wide // 2]], axis=1)
            mine.append(jnp.where(core == 0, block, swapped))
            theirs.append(jnp.where(core == 0, swapped, block))
    return jnp.concatenate(mine, axis=1), jnp.concatenate(theirs, axis=1)


def finish_kernel(place, main_share, rest_share, main_rows, rest_rows, stream, *refs):
    next_own, next_other = refs[:4], refs[4:8]
    norm_gain, head_gain, cosine, sine, out, next_rows, layer, joined = refs[8:]
    tok = stream.shape[0]
    count = main_share.shape[1]
    wide = main_rows.shape[2]
    hd = head_gain.shape[1]
    step = pl.program_id(0)

    def flat(values):
        values = values[...].astype(jnp.float32).reshape(count, wide)
        return values.astype(jnp.bfloat16)

    total = jnp.dot(main_share[...], flat(main_rows), preferred_element_type=jnp.float32)
    total += jnp.dot(rest_share[0], flat(rest_rows), preferred_element_type=jnp.float32)
    done = (stream[...].astype(jnp.float32) + total[:tok] + total[tok:]).astype(jnp.bfloat16)
    out[...] = done
    layer[step] = done

    @pl.when(step == layer.shape[0] - 1)
    def _():
        parts = [layer[at].astype(jnp.float32) for at in range(layer.shape[0])]
        square = sum(jnp.sum(part * part, axis=1, keepdims=True) for part in parts)
        inverse = lax.rsqrt(square / (wide * len(parts)) + EPS)
        for at, part in enumerate(parts):
            columns = slice(at * wide, (at + 1) * wide)
            normed = (part * inverse * norm_gain[:, columns]).astype(jnp.bfloat16)
            joined[:, columns] = normed
        mine, theirs = reorder(place, joined)
        raw_own = multiply(mine, next_own)
        raw_other = multiply(theirs, next_other)
        keys = jnp.where(place[2] == 0, raw_own, raw_other)
        values = jnp.where(place[2] == 0, raw_other, raw_own)
        half = keys.shape[1]
        for head in range(half // hd):
            columns = slice(head * hd, (head + 1) * hd)
            key = keys[:, columns]
            key = key * lax.rsqrt(jnp.mean(key * key, axis=-1, keepdims=True) + EPS)
            key = key * head_gain[...]
            key = key * cosine[...] + pltpu.roll(key, hd // 2, 1) * sine[...]
            next_rows[:, columns] = key.astype(jnp.bfloat16)
        next_rows[:, half:] = values.astype(jnp.bfloat16)


def finish(place, main_share, rest_share, returned, stream, halves, norm_gain, head_gain, turns):
    devices, height, wide = returned.shape
    tok, dim = stream.shape
    extra = halves[0].shape[1] - dim // 2
    chunks = dim // wide
    rows = height // (chunks + 1)
    shape = main_share.shape

    def fixed(values):
        return pl.BlockSpec(values.shape, lambda j, at: (0, 0))

    next_spec = pl.BlockSpec((dim // 4, extra), lambda j, at: (0, dim // 2 // extra))
    return pl.pallas_call(
        finish_kernel,
        grid_spec=pltpu.PrefetchScalarGridSpec(
            num_scalar_prefetch=1,
            grid=(chunks,),
            in_specs=[
                fixed(main_share),
                pl.BlockSpec((1,) + shape, lambda j, at: (j, 0, 0)),
                pl.BlockSpec((devices, rows, wide), lambda j, at: (0, j, 0)),
                pl.BlockSpec((devices, rows, wide), lambda j, at: (0, chunks, 0)),
                pl.BlockSpec((tok, wide), lambda j, at: (0, j)),
            ]
            + [next_spec] * 8
            + [
                fixed(norm_gain),
                fixed(head_gain),
                fixed(turns[0]),
                fixed(turns[1]),
            ],
            out_specs=(
                pl.BlockSpec((tok, wide), lambda j, at: (0, j)),
                pl.BlockSpec((tok, 2 * extra), lambda j, at: (0, 0)),
            ),
            scratch_shapes=[
                pltpu.VMEM((chunks, tok, wide), jnp.bfloat16),
                pltpu.VMEM((tok, dim), jnp.bfloat16),
            ],
        ),
        out_shape=(
            jax.ShapeDtypeStruct(stream.shape, stream.dtype),
            jax.ShapeDtypeStruct((tok, 2 * extra), stream.dtype),
        ),
        compiler_params=pltpu.CompilerParams(vmem_limit_bytes=60 * 1024 * 1024),
        name="finish",
    )(
        place,
        main_share,
        rest_share,
        returned,
        returned,
        stream,
        *halves,
        norm_gain,
        head_gain,
        *turns,
    )


def per_device(
    hidden,
    norm_gains,
    head_gains,
    query_weight,
    kv_weight,
    out_weight,
    gate_up,
    down_weight,
    next_weight,
    expert_ids,
    route_weights,
    token_request,
    request_leaf,
    leaf_parent,
    mid_parent,
    root_length,
    mid_length,
    leaf_length,
    root_slot,
    mid_slot,
    leaf_slot,
    root_cache,
    mid_cache,
    leaf_cache,
):
    tok, dim = hidden.shape
    hd = head_gains.shape[1]
    group = token_request.shape[0]
    mp_size = lax.axis_size("mp")
    dp_size = lax.axis_size("dp")
    devices = dp_size * mp_size
    me = lax.axis_index("mp")
    own_rows = query_weight.shape[0]

    pair = token_request[0] + jnp.arange(2, dtype=jnp.int32)
    cut = jnp.sum((token_request == pair[0]).astype(jnp.int32))
    leaf_node = look_up(request_leaf, pair)
    mid_node = look_up(leaf_parent, leaf_node)
    root_node = look_up(mid_parent, mid_node)
    lengths = (
        look_up(root_length, root_node),
        look_up(mid_length, mid_node),
        look_up(leaf_length, leaf_node),
    )
    prefix_length = lengths[0] + lengths[1] + lengths[2]
    token = jnp.arange(group, dtype=jnp.int32)
    positions = token + jnp.where(token >= cut, prefix_length[1] - cut, prefix_length[0])
    frequency = THETA ** (-2.0 * jnp.arange(hd // 2, dtype=jnp.float32) / hd)
    angles = positions.astype(jnp.float32)[:, None] * frequency[None, :]
    cos_half = jnp.cos(angles)
    sin_half = jnp.sin(angles)
    cosine = jnp.concatenate([cos_half, cos_half], axis=1)
    sine = jnp.concatenate([-sin_half, sin_half], axis=1)

    packed = pack_weights(query_weight, kv_weight, out_weight, next_weight, mp_size)
    packed = lax.all_to_all(packed, "mp", split_axis=0, concat_axis=0, tiled=True)
    packed, stream = lax.optimization_barrier((packed, hidden))
    normed = rms_norm(stream, norm_gains[0]).astype(jnp.bfloat16)
    def shift(values, step):
        moves = [(j, j - j % 4 + (j % 4 + step) % 4) for j in range(mp_size)]
        return lax.ppermute(values, "mp", moves)

    across = lax.ppermute(normed, "mp", [(j, (j + 4) % mp_size) for j in range(mp_size)])
    left = shift(normed, 1)
    right = shift(normed, -1)
    packed = packed.reshape(mp_size * own_rows, -1)
    late_width = dim + next_weight.shape[1]
    dp_at = lax.axis_index("dp")
    core = lax.rem(dp_at, 2)
    place = jnp.stack([dp_at // 4, lax.rem(dp_at // 2, 2), core]).astype(jnp.int32)

    def swap(values, bit):
        return lax.ppermute(values, "dp", [(j, j ^ bit) for j in range(dp_size)])

    def shift_x(values, step):
        moves = [(j, (j + 4 * step) % dp_size) for j in range(dp_size)]
        return lax.ppermute(values, "dp", moves)

    low, high = packed[:, : late_width // 2], packed[:, late_width // 2 : late_width]
    kept = jnp.where(core == 0, low, high)
    late = jnp.concatenate([kept, swap(jnp.where(core == 0, high, low), 1)], axis=0)
    late = jnp.concatenate([late, swap(late, 2)], axis=0)
    early = packed[:, late_width:].reshape(packed.shape[0], 2, 2 * hd).transpose(1, 0, 2)
    early = jnp.broadcast_to(early[None], (dp_size // 2,) + early.shape)
    early = early.reshape(dp_size, packed.shape[0], 2 * hd)
    early = lax.all_to_all(early, "dp", split_axis=0, concat_axis=0, tiled=True)
    early = early.reshape(dim, 2 * hd)
    sides = [left, right, shift(across, 1), shift(across, -1)]
    tables = (
        token_request,
        request_leaf,
        leaf_parent,
        mid_parent,
        root_slot,
        mid_slot,
        leaf_slot,
    )
    path = pack_paths(tables, root_cache, mid_cache, leaf_cache, mp_size)
    meta = jnp.concatenate(
        [
            jnp.stack([me, cut]),
            jnp.stack(lengths, axis=1).reshape(-1),
            jnp.stack([lax.rem(lax.axis_index("dp"), 2)]),
        ]
    ).astype(jnp.int32)
    path, sides, early, cosine, sine, meta = lax.optimization_barrier(
        (path, sides, early, cosine, sine, meta)
    )
    far = [shift(sides[0], 1), shift(sides[3], -1)]
    weights = (early, swap(early, 1))
    x_left = shift_x(late, 1)
    x_right = shift_x(late, -1)
    path = lax.all_to_all(path, "mp", split_axis=0, concat_axis=0, tiled=True)
    own_piece = jnp.sum(path.astype(jnp.float32), axis=0).astype(jnp.bfloat16)
    own_piece, weights, handed = lax.optimization_barrier((own_piece, weights, swap(late, 1)))
    pieces = [own_piece] + [
        lax.ppermute(own_piece, "mp", [(j, j ^ s) for j in range(mp_size)]) for s in range(1, 4)
    ]
    pieces, far, x_left, x_right = lax.optimization_barrier((pieces, far, x_left, x_right))
    x_far = shift_x(x_left, 1)
    rows = [normed, across] + sides + far
    attended = attend(meta, rows, weights, pieces, head_gains, cosine, sine)
    attended, x_far = lax.optimization_barrier((attended, x_far))
    halves = (late, x_left, x_right, x_far, handed)
    halves += tuple(swap(piece, 1) for piece in (x_left, x_right, x_far))
    attended = lax.all_to_all(
        attended.reshape(mp_size, tok, 2 * hd), "mp", split_axis=0, concat_axis=0, tiled=True
    )
    after_attention, moe_in = project(place, attended, halves, hidden, norm_gains[1:2])

    top_k = expert_ids.shape[1]
    capacity = max(2, 5 * tok * top_k // (4 * devices))
    names = expert_ids[:, :, None] == jnp.arange(devices, dtype=jnp.int32)[None, None, :]
    named = jnp.any(names, axis=1)
    route = jnp.sum(jnp.where(names, route_weights[:, :, None], 0.0), axis=1)
    before = jnp.tril(jnp.ones((tok, tok), jnp.bfloat16), -1)
    slot_no = jnp.dot(before, named.astype(jnp.bfloat16), preferred_element_type=jnp.float32)
    slot_no = jnp.where(named, slot_no.astype(jnp.int32), -1)

    def spread(first, last):
        count = jnp.arange(first, last, dtype=jnp.int32)
        taken = slot_no.T[:, None, :] == count[None, :, None]
        return taken.astype(jnp.bfloat16).reshape(devices * (last - first), tok)

    def gather_back(first, last):
        count = jnp.arange(first, last, dtype=jnp.int32)
        taken = slot_no[:, :, None] == count[None, None, :]
        share = jnp.where(taken, route[:, :, None], 0.0).reshape(tok, devices * (last - first))
        upper = lax.reduce_precision(share, 8, 7)
        return jnp.concatenate([upper, share - upper], axis=0).astype(jnp.bfloat16)

    def outbound(first, last, source):
        picked = jnp.dot(spread(first, last), source, preferred_element_type=jnp.float32)
        return picked.astype(jnp.bfloat16).reshape(devices, last - first, dim)

    main_in = exchange(outbound(0, MAIN, moe_in))
    main_in, rest_in = lax.optimization_barrier((main_in, outbound(MAIN, capacity, moe_in)))
    rest_in = exchange(rest_in)
    chunks = MAIN // (capacity - MAIN)
    wide = dim // chunks
    main_out = expert(main_in.reshape(-1, dim), gate_up[0], down_weight[0])
    main_out = main_out.reshape(devices, MAIN, chunks, wide).transpose(0, 2, 1, 3)
    main_out = main_out.reshape(devices, MAIN * chunks, wide)
    main_out = jnp.pad(main_out, ((0, 0), (0, MAIN), (0, 0)))
    main_out, rest_in = lax.optimization_barrier((main_out, rest_in))
    returned = exchange(expert_rest(rest_in.reshape(-1, dim), gate_up[0], down_weight[0], main_out))
    main_share = gather_back(0, MAIN)
    rest_share = gather_back(MAIN, capacity).reshape(1, 2 * tok, devices, 1, capacity - MAIN)
    which = jnp.eye(chunks, dtype=jnp.bfloat16).reshape(chunks, 1, 1, chunks, 1)
    rest_share = (rest_share * which).reshape(chunks, 2 * tok, devices * MAIN)
    my_cos = lax.dynamic_slice_in_dim(cosine, me * tok, tok)
    my_sin = lax.dynamic_slice_in_dim(sine, me * tok, tok)
    layer_out, next_rows = finish(
        place,
        main_share,
        rest_share,
        returned,
        after_attention,
        halves,
        norm_gains[2:3],
        head_gains[2:3],
        (my_cos, my_sin),
    )
    return (layer_out, next_rows)


def solution(mesh):
    both = P(BOTH, None)
    placed = (
        both,
        P(),
        P(),
        both,
        both,
        both,
        P(BOTH, None, None),
        P(BOTH, None, None),
        both,
        both,
        both,
        P("dp"),
        P(),
        P(),
        P(),
        P(),
        P(),
        P(),
        P(),
        P(),
        P(),
        P("mp", None, None),
        P("mp", None, None),
        P("mp", None, None),
    )
    return jax.shard_map(
        per_device,
        mesh=mesh,
        in_specs=placed,
        out_specs=(both, both),
        check_vma=False,
    )
```

```python
import jax
import jax.numpy as jnp
from jax import lax
from jax.experimental import pallas as pl
from jax.experimental.pallas import tpu as pltpu
from jax.sharding import PartitionSpec as P

EPS = 1e-06
THETA = 1000000.0
MASKED = -1e30
LOG2E = 1.4426950408889634
BOTH = ("dp", "mp")
MAIN = 8


def rms_norm(values, weight_row):
    values = values.astype(jnp.float32)
    return values * lax.rsqrt(jnp.mean(values * values, axis=-1, keepdims=True) + EPS) * weight_row


def look_up(lookup_table, indices):
    places = jnp.arange(lookup_table.shape[0], dtype=jnp.int32)
    return jnp.sum(jnp.where(indices[:, None] == places[None, :], lookup_table[None, :], 0), axis=1)


def pack_weights_kernel(query, kv, out_rows, next_rows, packed):
    count = packed.shape[0]
    dim = out_rows.shape[1]
    extra = next_rows.shape[1]
    wide = query.shape[1] // count
    hd = wide // 2
    heads = kv.shape[1] // 2 // hd
    base = dim + extra
    for dest in range(count):
        head = dest * heads // count
        for half in range(2):
            at = half * base // 2
            packed[dest, :, at : at + dim // 2] = out_rows[
                :, half * dim // 2 : (half + 1) * dim // 2
            ]
            packed[dest, :, at + dim // 2 : at + base // 2] = next_rows[
                :, half * extra // 2 : (half + 1) * extra // 2
            ]
        packed[dest, :, base : base + wide] = query[:, dest * wide : (dest + 1) * wide]
        for half in range(2):
            source = (half * heads + head) * hd
            target = base + wide + half * hd
            packed[dest, :, target : target + hd] = kv[:, source : source + hd]


def pack_weights(query, kv, out_rows, next_rows, count):
    rows = query.shape[0]
    width = out_rows.shape[1] + next_rows.shape[1] + 2 * (query.shape[1] // count)
    in_vmem = pl.BlockSpec(memory_space=pltpu.VMEM)
    return pl.pallas_call(
        pack_weights_kernel,
        out_shape=jax.ShapeDtypeStruct((count, rows, width), jnp.bfloat16),
        in_specs=[in_vmem] * 4,
        out_specs=in_vmem,
        name="pack_weights",
    )(query, kv, out_rows, next_rows)


def pack_paths_kernel(
    token_request,
    request_leaf,
    leaf_parent,
    mid_parent,
    root_slot,
    mid_slot,
    leaf_slot,
    root,
    mid,
    leaf,
    packed,
):
    count, part, wide = packed.shape
    hd = wide // 2
    heads = count // 4
    me = lax.axis_index("mp")
    for req in range(2):
        leaf_node = request_leaf[token_request[0] + req]
        mid_node = leaf_parent[leaf_node]
        slots = (root_slot[mid_parent[mid_node]], mid_slot[mid_node], leaf_slot[leaf_node])
        levels = []
        for slot, cache in zip(slots, (root, mid, leaf)):
            here = cache.shape[0]
            rows = jnp.zeros(cache.shape[1:], cache.dtype)
            for local in range(here):
                rows = jnp.where(slot == me * here + local, cache[local], rows)
            levels.append(rows)
        top = levels[0].shape[0] - part
        middle = levels[1].shape[0]
        for head in range(heads):
            for half in range(2):
                source = slice((half * heads + head) * hd, (half * heads + head + 1) * hd)
                target = slice(half * hd, (half + 1) * hd)
                place = 4 * head + 2 * req
                packed[place, :, target] = levels[0][:part, source]
                packed[place + 1, 0:top, target] = levels[0][part:, source]
                packed[place + 1, top : top + middle, target] = levels[1][:, source]
                packed[place + 1, top + middle :, target] = levels[2][:, source]


def pack_paths(tables, root, mid, leaf, count):
    wide = root.shape[2] // 2
    part = (root.shape[1] + mid.shape[1] + leaf.shape[1]) // 2
    in_vmem = pl.BlockSpec(memory_space=pltpu.VMEM)
    in_smem = pl.BlockSpec(memory_space=pltpu.SMEM)
    return pl.pallas_call(
        pack_paths_kernel,
        out_shape=jax.ShapeDtypeStruct((count, part, wide), jnp.bfloat16),
        in_specs=[in_smem] * len(tables) + [in_vmem] * 3,
        out_specs=in_vmem,
        compiler_params=pltpu.CompilerParams(vmem_limit_bytes=24 * 1024 * 1024),
        name="pack_paths",
    )(*tables, root, mid, leaf)


def attention_kernel(
    meta,
    own,
    across,
    own_left,
    own_right,
    across_left,
    across_right,
    own_far,
    across_far,
    weight_own,
    weight_other,
    piece_0,
    piece_1,
    piece_2,
    piece_3,
    gains,
    cosine,
    sine,
    out,
    rows_all,
    weights,
    q_all,
    k_all,
    v_all,
    pk_all,
    pv_all,
):
    pieces = (piece_0, piece_1, piece_2, piece_3)
    me = meta[0]
    cut = meta[1]
    tok, dim = own.shape
    count = rows_all.shape[0] // tok
    hd = gains.shape[1]
    span = pk_all.shape[0] // 2
    part = piece_0.shape[0]
    ring = lax.rem(me, 4)
    base = me - ring
    far_base = 4 - base

    def put(first, step, block):
        at = pl.multiple_of((first + lax.rem(ring + step, 4)) * tok, tok)
        rows_all[pl.ds(at, tok), :] = block[...]

    put(base, 0, own)
    put(far_base, 0, across)
    put(base, 3, own_left)
    put(base, 1, own_right)
    put(far_base, 3, across_left)
    put(far_base, 1, across_right)
    put(base, 2, own_far)
    put(far_base, 2, across_far)
    for step, piece in enumerate(pieces):
        place = pl.multiple_of((ring ^ step) * part, part)
        pk_all[pl.ds(place, part), :] = piece[:, :hd]
        pv_all[pl.ds(place, part), :] = piece[:, hd:]
    core = meta[8]
    weights[core] = weight_own[...]
    weights[1 - core] = weight_other[...]
    weight_q = weights[0]
    weight_kv = weights[1]

    def turn(raw, gain, cos_now, sin_now):
        scaled = raw * lax.rsqrt(jnp.mean(raw * raw, axis=-1, keepdims=True) + EPS) * gain
        return (scaled * cos_now + pltpu.roll(scaled, hd // 2, 1) * sin_now).astype(jnp.bfloat16)

    large = 4 * tok

    @pl.loop(0, count // 4)
    def _(step):
        at = pl.multiple_of(step * large, large)
        rows = rows_all[pl.ds(at, large), :]
        cos_now = cosine[pl.ds(at, large), :]
        sin_now = sine[pl.ds(at, large), :]
        raw = jnp.dot(rows, weight_q, preferred_element_type=jnp.float32)
        heads = [
            turn(raw[:, half * hd : (half + 1) * hd], gains[0:1, :], cos_now, sin_now)
            for half in range(2)
        ]
        for block in range(4):
            for half in range(2):
                q_at = pl.multiple_of(2 * at + (2 * block + half) * tok, tok)
                q_all[pl.ds(q_at, tok), :] = heads[half][block * tok : (block + 1) * tok]
        raw = jnp.dot(rows, weight_kv, preferred_element_type=jnp.float32)
        k_all[pl.ds(at, large), :] = turn(raw[:, :hd], gains[1:2, :], cos_now, sin_now)
        v_all[pl.ds(at, large), :] = raw[:, hd:].astype(jnp.bfloat16)

    scale = hd ** (-0.5) * LOG2E
    col = lax.broadcasted_iota(jnp.int32, (1, span), 1)
    row = lax.broadcasted_iota(jnp.int32, (2 * tok, 1), 0)
    row = jnp.where(row >= tok, row - tok, row)

    def score(q_now, keys):
        return lax.dot_general(
            q_now, keys, (((1,), (1,)), ((), ())), preferred_element_type=jnp.float32
        )

    def join(state, scores, values):
        peak, total, acc = state
        top = jnp.maximum(peak, jnp.max(scores, axis=1, keepdims=True))
        keep = jnp.exp2(peak - top)
        weights = jnp.exp2(scores - top)
        total = total * keep + jnp.sum(weights, axis=1, keepdims=True)
        acc = acc * keep + jnp.dot(
            weights.astype(jnp.bfloat16), values, preferred_element_type=jnp.float32
        )
        return top, total, acc

    @pl.loop(0, count)
    def _(step):
        first = pl.multiple_of(step * tok, tok)
        q_now = q_all[pl.ds(pl.multiple_of(2 * step * tok, 2 * tok), 2 * tok), :]
        token = row + first
        late = token >= cut

        def prefix(req, state):
            start = pl.multiple_of(req * span, span)
            at = 2 + 3 * req
            inside = jnp.where(
                col < 512,
                (col < meta[at]).astype(jnp.int32),
                jnp.where(
                    col < 768,
                    (col - 512 < meta[at + 1]).astype(jnp.int32),
                    (col - 768 < meta[at + 2]).astype(jnp.int32),
                ),
            )
            outside = jnp.where(inside > 0, 0.0, MASKED)
            foreign = jnp.where(late.astype(jnp.int32) == req, 0.0, MASKED)
            scores = scale * score(q_now, pk_all[pl.ds(start, span), :]) + outside + foreign
            return join(state, scores, pv_all[pl.ds(start, span), :])

        low = (first >= cut).astype(jnp.int32)
        high = (first + tok > cut).astype(jnp.int32)
        before = lax.fori_loop(
            low,
            high + 1,
            prefix,
            (
                jnp.full((2 * tok, 1), MASKED, jnp.float32),
                jnp.zeros((2 * tok, 1), jnp.float32),
                jnp.zeros((2 * tok, hd), jnp.float32),
            ),
        )
        bottom = jnp.where(late, cut, 0)

        for quarter in range(count // 2):

            @pl.when(step // 2 == quarter)
            def _(quarter=quarter):
                keys = 2 * tok * (quarter + 1)
                other = lax.broadcasted_iota(jnp.int32, (1, keys), 1)
                allowed = jnp.logical_and(other <= token, other >= bottom)
                scores = scale * score(q_now, k_all[0:keys, :])
                peak, total, acc = join(
                    before,
                    jnp.where(allowed, scores, MASKED),
                    v_all[0:keys, :],
                )
                done = (acc / total).astype(jnp.bfloat16)
                out[pl.ds(first, tok), 0:hd] = done[:tok]
                out[pl.ds(first, tok), hd : 2 * hd] = done[tok:]


def attend(meta, rows, weights, pieces, gains, cosine, sine):
    group = cosine.shape[0]
    hd = gains.shape[1]
    path_rows = 4 * pieces[0].shape[0]
    in_vmem = pl.BlockSpec(memory_space=pltpu.VMEM)
    return pl.pallas_call(
        attention_kernel,
        out_shape=jax.ShapeDtypeStruct((group, 2 * hd), jnp.bfloat16),
        in_specs=[pl.BlockSpec(memory_space=pltpu.SMEM)] + [in_vmem] * 17,
        out_specs=in_vmem,
        scratch_shapes=[
            pltpu.VMEM((group, rows[0].shape[1]), jnp.bfloat16),
            pltpu.VMEM((2, rows[0].shape[1], 2 * hd), jnp.bfloat16),
            pltpu.VMEM((2 * group, hd), jnp.bfloat16),
            pltpu.VMEM((group, hd), jnp.bfloat16),
            pltpu.VMEM((group, hd), jnp.bfloat16),
            pltpu.VMEM((path_rows, hd), jnp.bfloat16),
            pltpu.VMEM((path_rows, hd), jnp.bfloat16),
        ],
        compiler_params=pltpu.CompilerParams(vmem_limit_bytes=60 * 1024 * 1024),
        cost_estimate=pl.CostEstimate(
            flops=16 * group * group * hd, bytes_accessed=16 * group * 512, transcendentals=3 * group * group
        ),
        name="tree_attention",
    )(meta, *rows, *weights, *pieces, gains, cosine, sine)


def column_block(step, core):
    half = jnp.where(step < 2, core, 1 - core)
    return 2 * half + lax.rem(step, 2)


def multiply(values, pieces):
    rows = pieces[0].shape[0]
    return sum(
        jnp.dot(
            values[:, at * rows : (at + 1) * rows], piece[...], preferred_element_type=jnp.float32
        )
        for at, piece in enumerate(pieces)
    )


def project_kernel(place, attended, *refs):
    own, other = refs[:4], refs[4:8]
    hidden, gain, out, normed, joined_own, joined_other, layer = refs[8:]
    wide = attended.shape[2]
    step = pl.program_id(0)
    x, y, core = place[0], place[1], place[2]

    @pl.when(step == 0)
    def _():
        for at, shift in enumerate((0, 3, 1, 2)):
            for turn in range(2):
                block = attended[lax.rem(x + shift, 4) * 2 + lax.rem(y + turn, 2)]
                swapped = jnp.concatenate([block[:, wide // 2 :], block[:, : wide // 2]], axis=1)
                columns = slice((2 * at + turn) * wide, (2 * at + turn + 1) * wide)
                joined_own[:, columns] = jnp.where(core == 0, block, swapped)
                joined_other[:, columns] = jnp.where(core == 0, swapped, block)

    def add(joined, weight):
        added = multiply(joined[...], weight)
        done = (hidden[...].astype(jnp.float32) + added).astype(jnp.bfloat16)
        out[...] = done
        layer[column_block(step, core)] = done

    @pl.when(step < 2)
    def _():
        add(joined_own, own)

    @pl.when(step >= 2)
    def _():
        add(joined_other, other)

    @pl.when(step == layer.shape[0] - 1)
    def _():
        columns = layer.shape[2]
        parts = [layer[at].astype(jnp.float32) for at in range(layer.shape[0])]
        square = sum(jnp.sum(part * part, axis=1, keepdims=True) for part in parts)
        inverse = lax.rsqrt(square / (columns * len(parts)) + EPS)
        for at, part in enumerate(parts):
            where = slice(at * columns, (at + 1) * columns)
            normed[:, where] = (part * inverse * gain[:, where]).astype(jnp.bfloat16)


def project(place, attended, halves, hidden, gain):
    tok, dim = hidden.shape
    columns = dim // 4
    return pl.pallas_call(
        project_kernel,
        grid_spec=pltpu.PrefetchScalarGridSpec(
            num_scalar_prefetch=1,
            grid=(4,),
            in_specs=[
                pl.BlockSpec(attended.shape, lambda j, at: (0, 0, 0)),
            ]
            + [pl.BlockSpec((dim // 4, columns), lambda j, at: (0, jnp.minimum(j, 1)))] * 4
            + [pl.BlockSpec((dim // 4, columns), lambda j, at: (0, jnp.maximum(j - 2, 0)))] * 4
            + [
                pl.BlockSpec((tok, columns), lambda j, at: (0, column_block(j, at[2]))),
                pl.BlockSpec((1, dim), lambda j, at: (0, 0)),
            ],
            out_specs=(
                pl.BlockSpec((tok, columns), lambda j, at: (0, column_block(j, at[2]))),
                pl.BlockSpec((tok, dim), lambda j, at: (0, 0)),
            ),
            scratch_shapes=[
                pltpu.VMEM((tok, dim), jnp.bfloat16),
                pltpu.VMEM((tok, dim), jnp.bfloat16),
                pltpu.VMEM((4, tok, columns), jnp.bfloat16),
            ],
        ),
        out_shape=(
            jax.ShapeDtypeStruct(hidden.shape, hidden.dtype),
            jax.ShapeDtypeStruct(hidden.shape, hidden.dtype),
        ),
        compiler_params=pltpu.CompilerParams(vmem_limit_bytes=18 * 1024 * 1024),
        name="project",
    )(place, attended, *halves, hidden, gain)


def exchange(values):
    return lax.all_to_all(values, BOTH, split_axis=0, concat_axis=0, tiled=True)


def expert(rows, gate_up, down_weight):
    ff_width = down_weight.shape[0]
    both = jnp.dot(rows, gate_up, preferred_element_type=jnp.float32)
    active = (jax.nn.silu(both[:, :ff_width]) * both[:, ff_width:]).astype(jnp.bfloat16)
    return jnp.dot(active, down_weight, preferred_element_type=jnp.float32).astype(jnp.bfloat16)


def rest_kernel(rows, gate_up, down_weight, main_block, out):
    del main_block
    ff_width = down_weight.shape[0]
    spans = out.shape[0]
    wide = out.shape[2]
    chunks = down_weight.shape[1] // wide
    per = rows.shape[0] // spans
    both = jnp.dot(rows[...], gate_up[...], preferred_element_type=jnp.float32)
    gate = both[:, :ff_width]
    active = (gate / (1.0 + jnp.exp(-gate)) * both[:, ff_width:]).astype(jnp.bfloat16)
    served = jnp.dot(active, down_weight[...], preferred_element_type=jnp.float32)
    served = served.astype(jnp.bfloat16)
    batch = 16
    size = batch * per * chunks
    to = lax.broadcasted_iota(jnp.int32, (size, size), 0)
    source = lax.broadcasted_iota(jnp.int32, (size, size), 1)
    device = to // (per * chunks)
    chunk = to // per % chunks
    wanted = chunk * (batch * per) + device * per + to % per
    order = (source == wanted).astype(jnp.bfloat16)
    for first in range(0, spans, batch):
        stacked = jnp.concatenate(
            [
                served[first * per : (first + batch) * per, at * wide : (at + 1) * wide]
                for at in range(chunks)
            ],
            axis=0,
        )
        sorted_rows = jnp.dot(order, stacked, preferred_element_type=jnp.float32)
        out[first : first + batch] = sorted_rows.reshape(batch, per * chunks, wide).astype(
            jnp.bfloat16
        )


def expert_rest(rows, gate_up, down_weight, main_block):
    spans, height, wide = main_block.shape
    extra = rows.shape[0] // spans * down_weight.shape[1] // wide
    in_vmem = pl.BlockSpec(memory_space=pltpu.VMEM)
    return pl.pallas_call(
        rest_kernel,
        grid=(1,),
        out_shape=jax.ShapeDtypeStruct(main_block.shape, main_block.dtype),
        in_specs=[in_vmem, in_vmem, in_vmem, pl.BlockSpec(memory_space=pl.ANY)],
        out_specs=pl.BlockSpec((spans, extra, wide), lambda i: (0, height // extra - 1, 0)),
        input_output_aliases={3: 0},
        compiler_params=pltpu.CompilerParams(vmem_limit_bytes=60 * 1024 * 1024),
        name="expert_rest",
    )(rows, gate_up, down_weight, main_block)


def reorder(place, joined):
    x, y, core = place[0], place[1], place[2]
    wide = joined.shape[1] // 8
    mine, theirs = [], []
    for shift in (0, 3, 1, 2):
        for turn in range(2):
            block_no = lax.rem(x + shift, 4) * 2 + lax.rem(y + turn, 2)
            block = joined[:, pl.ds(pl.multiple_of(block_no * wide, wide), wide)]
            swapped = jnp.concatenate([block[:, wide // 2 :], block[:, : wide // 2]], axis=1)
            mine.append(jnp.where(core == 0, block, swapped))
            theirs.append(jnp.where(core == 0, swapped, block))
    return jnp.concatenate(mine, axis=1), jnp.concatenate(theirs, axis=1)


def finish_kernel(place, main_share, rest_share, main_rows, rest_rows, stream, *refs):
    next_own, next_other = refs[:4], refs[4:8]
    norm_gain, head_gain, cosine, sine, out, next_rows, layer, joined = refs[8:]
    tok = stream.shape[0]
    count = main_share.shape[1]
    wide = main_rows.shape[2]
    hd = head_gain.shape[1]
    step = pl.program_id(0)

    def flat(values):
        values = values[...].astype(jnp.float32).reshape(count, wide)
        return values.astype(jnp.bfloat16)

    total = jnp.dot(main_share[...], flat(main_rows), preferred_element_type=jnp.float32)
    total += jnp.dot(rest_share[0], flat(rest_rows), preferred_element_type=jnp.float32)
    done = (stream[...].astype(jnp.float32) + total[:tok] + total[tok:]).astype(jnp.bfloat16)
    out[...] = done
    layer[step] = done

    @pl.when(step == layer.shape[0] - 1)
    def _():
        parts = [layer[at].astype(jnp.float32) for at in range(layer.shape[0])]
        square = sum(jnp.sum(part * part, axis=1, keepdims=True) for part in parts)
        inverse = lax.rsqrt(square / (wide * len(parts)) + EPS)
        for at, part in enumerate(parts):
            columns = slice(at * wide, (at + 1) * wide)
            normed = (part * inverse * norm_gain[:, columns]).astype(jnp.bfloat16)
            joined[:, columns] = normed
        mine, theirs = reorder(place, joined)
        raw_own = multiply(mine, next_own)
        raw_other = multiply(theirs, next_other)
        keys = jnp.where(place[2] == 0, raw_own, raw_other)
        values = jnp.where(place[2] == 0, raw_other, raw_own)
        half = keys.shape[1]
        for head in range(half // hd):
            columns = slice(head * hd, (head + 1) * hd)
            key = keys[:, columns]
            key = key * lax.rsqrt(jnp.mean(key * key, axis=-1, keepdims=True) + EPS)
            key = key * head_gain[...]
            key = key * cosine[...] + pltpu.roll(key, hd // 2, 1) * sine[...]
            next_rows[:, columns] = key.astype(jnp.bfloat16)
        next_rows[:, half:] = values.astype(jnp.bfloat16)


def finish(place, main_share, rest_share, returned, stream, halves, norm_gain, head_gain, turns):
    devices, height, wide = returned.shape
    tok, dim = stream.shape
    extra = halves[0].shape[1] - dim // 2
    chunks = dim // wide
    rows = height // (chunks + 1)
    shape = main_share.shape

    def fixed(values):
        return pl.BlockSpec(values.shape, lambda j, at: (0, 0))

    next_spec = pl.BlockSpec((dim // 4, extra), lambda j, at: (0, dim // 2 // extra))
    return pl.pallas_call(
        finish_kernel,
        grid_spec=pltpu.PrefetchScalarGridSpec(
            num_scalar_prefetch=1,
            grid=(chunks,),
            in_specs=[
                fixed(main_share),
                pl.BlockSpec((1,) + shape, lambda j, at: (j, 0, 0)),
                pl.BlockSpec((devices, rows, wide), lambda j, at: (0, j, 0)),
                pl.BlockSpec((devices, rows, wide), lambda j, at: (0, chunks, 0)),
                pl.BlockSpec((tok, wide), lambda j, at: (0, j)),
            ]
            + [next_spec] * 8
            + [
                fixed(norm_gain),
                fixed(head_gain),
                fixed(turns[0]),
                fixed(turns[1]),
            ],
            out_specs=(
                pl.BlockSpec((tok, wide), lambda j, at: (0, j)),
                pl.BlockSpec((tok, 2 * extra), lambda j, at: (0, 0)),
            ),
            scratch_shapes=[
                pltpu.VMEM((chunks, tok, wide), jnp.bfloat16),
                pltpu.VMEM((tok, dim), jnp.bfloat16),
            ],
        ),
        out_shape=(
            jax.ShapeDtypeStruct(stream.shape, stream.dtype),
            jax.ShapeDtypeStruct((tok, 2 * extra), stream.dtype),
        ),
        compiler_params=pltpu.CompilerParams(vmem_limit_bytes=60 * 1024 * 1024),
        name="finish",
    )(
        place,
        main_share,
        rest_share,
        returned,
        returned,
        stream,
        *halves,
        norm_gain,
        head_gain,
        *turns,
    )


def per_device(
    hidden,
    norm_gains,
    head_gains,
    query_weight,
    kv_weight,
    out_weight,
    gate_up,
    down_weight,
    next_weight,
    expert_ids,
    route_weights,
    token_request,
    request_leaf,
    leaf_parent,
    mid_parent,
    root_length,
    mid_length,
    leaf_length,
    root_slot,
    mid_slot,
    leaf_slot,
    root_cache,
    mid_cache,
    leaf_cache,
):
    tok, dim = hidden.shape
    hd = head_gains.shape[1]
    group = token_request.shape[0]
    mp_size = lax.axis_size("mp")
    dp_size = lax.axis_size("dp")
    devices = dp_size * mp_size
    me = lax.axis_index("mp")
    own_rows = query_weight.shape[0]

    pair = token_request[0] + jnp.arange(2, dtype=jnp.int32)
    cut = jnp.sum((token_request == pair[0]).astype(jnp.int32))
    leaf_node = look_up(request_leaf, pair)
    mid_node = look_up(leaf_parent, leaf_node)
    root_node = look_up(mid_parent, mid_node)
    lengths = (
        look_up(root_length, root_node),
        look_up(mid_length, mid_node),
        look_up(leaf_length, leaf_node),
    )
    prefix_length = lengths[0] + lengths[1] + lengths[2]
    token = jnp.arange(group, dtype=jnp.int32)
    positions = token + jnp.where(token >= cut, prefix_length[1] - cut, prefix_length[0])
    frequency = THETA ** (-2.0 * jnp.arange(hd // 2, dtype=jnp.float32) / hd)
    angles = positions.astype(jnp.float32)[:, None] * frequency[None, :]
    cos_half = jnp.cos(angles)
    sin_half = jnp.sin(angles)
    cosine = jnp.concatenate([cos_half, cos_half], axis=1)
    sine = jnp.concatenate([-sin_half, sin_half], axis=1)

    packed = pack_weights(query_weight, kv_weight, out_weight, next_weight, mp_size)
    packed = lax.all_to_all(packed, "mp", split_axis=0, concat_axis=0, tiled=True)
    packed, stream = lax.optimization_barrier((packed, hidden))
    normed = rms_norm(stream, norm_gains[0]).astype(jnp.bfloat16)
    def shift(values, step):
        moves = [(j, j - j % 4 + (j % 4 + step) % 4) for j in range(mp_size)]
        return lax.ppermute(values, "mp", moves)

    across = lax.ppermute(normed, "mp", [(j, (j + 4) % mp_size) for j in range(mp_size)])
    left = shift(normed, 1)
    right = shift(normed, -1)
    packed = packed.reshape(mp_size * own_rows, -1)
    late_width = dim + next_weight.shape[1]
    dp_at = lax.axis_index("dp")
    core = lax.rem(dp_at, 2)
    place = jnp.stack([dp_at // 4, lax.rem(dp_at // 2, 2), core]).astype(jnp.int32)

    def swap(values, bit):
        return lax.ppermute(values, "dp", [(j, j ^ bit) for j in range(dp_size)])

    def shift_x(values, step):
        moves = [(j, (j + 4 * step) % dp_size) for j in range(dp_size)]
        return lax.ppermute(values, "dp", moves)

    low, high = packed[:, : late_width // 2], packed[:, late_width // 2 : late_width]
    kept = jnp.where(core == 0, low, high)
    late = jnp.concatenate([kept, swap(jnp.where(core == 0, high, low), 1)], axis=0)
    late = jnp.concatenate([late, swap(late, 2)], axis=0)
    early = packed[:, late_width:].reshape(packed.shape[0], 2, 2 * hd).transpose(1, 0, 2)
    early = jnp.broadcast_to(early[None], (dp_size // 2,) + early.shape)
    early = early.reshape(dp_size, packed.shape[0], 2 * hd)
    early = lax.all_to_all(early, "dp", split_axis=0, concat_axis=0, tiled=True)
    early = early.reshape(dim, 2 * hd)
    sides = [left, right, shift(across, 1), shift(across, -1)]
    tables = (
        token_request,
        request_leaf,
        leaf_parent,
        mid_parent,
        root_slot,
        mid_slot,
        leaf_slot,
    )
    path = pack_paths(tables, root_cache, mid_cache, leaf_cache, mp_size)
    meta = jnp.concatenate(
        [
            jnp.stack([me, cut]),
            jnp.stack(lengths, axis=1).reshape(-1),
            jnp.stack([lax.rem(lax.axis_index("dp"), 2)]),
        ]
    ).astype(jnp.int32)
    path, sides, early, cosine, sine, meta = lax.optimization_barrier(
        (path, sides, early, cosine, sine, meta)
    )
    far = [shift(sides[0], 1), shift(sides[3], -1)]
    weights = (early, swap(early, 1))
    x_left = shift_x(late, 1)
    x_right = shift_x(late, -1)
    path = lax.all_to_all(path, "mp", split_axis=0, concat_axis=0, tiled=True)
    own_piece = jnp.sum(path.astype(jnp.float32), axis=0).astype(jnp.bfloat16)
    own_piece, weights, handed = lax.optimization_barrier((own_piece, weights, swap(late, 1)))
    pieces = [own_piece] + [
        lax.ppermute(own_piece, "mp", [(j, j ^ s) for j in range(mp_size)]) for s in range(1, 4)
    ]
    pieces, far, x_left, x_right = lax.optimization_barrier((pieces, far, x_left, x_right))
    x_far = shift_x(x_left, 1)
    rows = [normed, across] + sides + far
    attended = attend(meta, rows, weights, pieces, head_gains, cosine, sine)
    attended, x_far = lax.optimization_barrier((attended, x_far))
    halves = (late, x_left, x_right, x_far, handed)
    halves += tuple(swap(piece, 1) for piece in (x_left, x_right, x_far))
    attended = lax.all_to_all(
        attended.reshape(mp_size, tok, 2 * hd), "mp", split_axis=0, concat_axis=0, tiled=True
    )
    after_attention, moe_in = project(place, attended, halves, hidden, norm_gains[1:2])

    top_k = expert_ids.shape[1]
    capacity = max(2, 5 * tok * top_k // (4 * devices))
    names = expert_ids[:, :, None] == jnp.arange(devices, dtype=jnp.int32)[None, None, :]
    named = jnp.any(names, axis=1)
    route = jnp.sum(jnp.where(names, route_weights[:, :, None], 0.0), axis=1)
    before = jnp.tril(jnp.ones((tok, tok), jnp.bfloat16), -1)
    slot_no = jnp.dot(before, named.astype(jnp.bfloat16), preferred_element_type=jnp.float32)
    slot_no = jnp.where(named, slot_no.astype(jnp.int32), -1)

    def spread(first, last):
        count = jnp.arange(first, last, dtype=jnp.int32)
        taken = slot_no.T[:, None, :] == count[None, :, None]
        return taken.astype(jnp.bfloat16).reshape(devices * (last - first), tok)

    def gather_back(first, last):
        count = jnp.arange(first, last, dtype=jnp.int32)
        taken = slot_no[:, :, None] == count[None, None, :]
        share = jnp.where(taken, route[:, :, None], 0.0).reshape(tok, devices * (last - first))
        upper = lax.reduce_precision(share, 8, 7)
        return jnp.concatenate([upper, share - upper], axis=0).astype(jnp.bfloat16)

    def outbound(first, last, source):
        picked = jnp.dot(spread(first, last), source, preferred_element_type=jnp.float32)
        return picked.astype(jnp.bfloat16).reshape(devices, last - first, dim)

    main_in = exchange(outbound(0, MAIN, moe_in))
    main_in, rest_in = lax.optimization_barrier((main_in, outbound(MAIN, capacity, moe_in)))
    rest_in = exchange(rest_in)
    chunks = MAIN // (capacity - MAIN)
    wide = dim // chunks
    main_out = expert(main_in.reshape(-1, dim), gate_up[0], down_weight[0])
    main_out = main_out.reshape(devices, MAIN, chunks, wide).transpose(0, 2, 1, 3)
    main_out = main_out.reshape(devices, MAIN * chunks, wide)
    main_out = jnp.pad(main_out, ((0, 0), (0, MAIN), (0, 0)))
    main_out, rest_in = lax.optimization_barrier((main_out, rest_in))
    returned = exchange(expert_rest(rest_in.reshape(-1, dim), gate_up[0], down_weight[0], main_out))
    main_share = gather_back(0, MAIN)
    rest_share = gather_back(MAIN, capacity).reshape(1, 2 * tok, devices, 1, capacity - MAIN)
    which = jnp.eye(chunks, dtype=jnp.bfloat16).reshape(chunks, 1, 1, chunks, 1)
    rest_share = (rest_share * which).reshape(chunks, 2 * tok, devices * MAIN)
    my_cos = lax.dynamic_slice_in_dim(cosine, me * tok, tok)
    my_sin = lax.dynamic_slice_in_dim(sine, me * tok, tok)
    layer_out, next_rows = finish(
        place,
        main_share,
        rest_share,
        returned,
        after_attention,
        halves,
        norm_gains[2:3],
        head_gains[2:3],
        (my_cos, my_sin),
    )
    return (layer_out, next_rows)


def solution(mesh):
    both = P(BOTH, None)
    placed = (
        both,
        P(),
        P(),
        both,
        both,
        both,
        P(BOTH, None, None),
        P(BOTH, None, None),
        both,
        both,
        both,
        P("dp"),
        P(),
        P(),
        P(),
        P(),
        P(),
        P(),
        P(),
        P(),
        P(),
        P("mp", None, None),
        P("mp", None, None),
        P("mp", None, None),
    )
    return jax.shard_map(
        per_device,
        mesh=mesh,
        in_specs=placed,
        out_specs=(both, both),
        check_vma=False,
    )
```
